32 devices in a mesh: dp: 8 (over y, x, core), tp: 4 (over z).
Axes of the slice: x: 2, y: 2, z: 4, core: 2. Of those that a mesh axis runs over, the one named last changes fastest.
Arguments:
- tokens: bfloat16 [32768, 512], P(('dp', 'tp')), may hold values from -6 to 6
- cotangent: bfloat16 [32768, 512], P(('dp', 'tp')), may hold values from -12 to 12
- head_choice: int32 [32768, 8], P(('dp', 'tp')), may hold values from 0 to 23, all different within a row
- segment_ids: int32 [32, 1024], P(('dp', 'tp')), may hold values from 0 to 3, never falling along the last dimension, each value on 1 to 512 neighbouring positions
- query_weight: float32 [2, 512, 1536], P(None, 'dp', 'tp'), may hold values from -0.25 to 0.25
- output_weight: float32 [2, 512, 1536], P(None, 'dp', 'tp'), may hold values from -6 to 6
- up_weight: float32 [2, 512, 2048], P(None, 'dp', 'tp'), may hold values from -0.25 to 0.25
- down_weight: float32 [2, 512, 2048], P(None, 'dp', 'tp'), may hold values from -0.25 to 0.25
- keyval_weight: float32 [2, 512, 128], P(None, ('dp', 'tp')), may hold values from -0.25 to 0.25
- router_weight: float32 [2, 512, 24], P(None, ('dp', 'tp')), may hold values from -0.3125 to 0.3125
- norm_gains: float32 [2, 2, 512], P(None, None, ('dp', 'tp')), may hold values from 0.32 to 3
- first_query: float32 [2, 512, 1536], P(None, 'dp', 'tp'), may hold values from -1.5258789e-05 to 1.5258789e-05
- first_output: float32 [2, 512, 1536], P(None, 'dp', 'tp'), may hold values from -7.1525574e-07 to 7.1525574e-07
- first_up: float32 [2, 512, 2048], P(None, 'dp', 'tp'), may hold values from -5.340576e-05 to 5.340576e-05
- first_down: float32 [2, 512, 2048], P(None, 'dp', 'tp'), may hold values from -1.9073486e-05 to 1.9073486e-05
- first_keyval: float32 [2, 512, 128], P(None, ('dp', 'tp')), may hold values from -3.0517578e-05 to 3.0517578e-05
- first_router: float32 [2, 512, 24], P(None, ('dp', 'tp')), may hold values from -3.0517578e-05 to 3.0517578e-05
- first_gains: float32 [2, 2, 512], P(None, None, ('dp', 'tp')), may hold values from -3.0517578e-05 to 3.0517578e-05
- second_query: float32 [2, 512, 1536], P(None, 'dp', 'tp'), may hold values from 4.387996e-12 to 1.7538646e-11
- second_output: float32 [2, 512, 1536], P(None, 'dp', 'tp'), may hold values from 1.0936646e-14 to 4.387996e-14
- second_up: float32 [2, 512, 2048], P(None, 'dp', 'tp'), may hold values from 5.068202e-11 to 2.0272808e-10
- second_down: float32 [2, 512, 2048], P(None, 'dp', 'tp'), may hold values from 8.602606e-12 to 3.4410422e-11
- second_keyval: float32 [2, 512, 128], P(None, ('dp', 'tp')), may hold values from 1.7551984e-11 to 7.0154584e-11
- second_router: float32 [2, 512, 24], P(None, ('dp', 'tp')), may hold values from 1.7551984e-11 to 7.0154584e-11
- second_gains: float32 [2, 2, 512], P(None, None, ('dp', 'tp')), may hold values from 1.7551984e-11 to 7.0154584e-11
- average_query: float32 [2, 512, 1536], P(None, 'dp', 'tp'), may hold values from -0.25 to 0.25
- average_output: float32 [2, 512, 1536], P(None, 'dp', 'tp'), may hold values from -6 to 6
- average_up: float32 [2, 512, 2048], P(None, 'dp', 'tp'), may hold values from -0.25 to 0.25
- average_down: float32 [2, 512, 2048], P(None, 'dp', 'tp'), may hold values from -0.25 to 0.25
- average_keyval: float32 [2, 512, 128], P(None, ('dp', 'tp')), may hold values from -0.25 to 0.25
- average_router: float32 [2, 512, 24], P(None, ('dp', 'tp')), may hold values from -0.3125 to 0.3125
- average_gains: float32 [2, 2, 512], P(None, None, ('dp', 'tp')), may hold values from 0.1 to 3
Outputs:
- layer_out: bfloat16 [32768, 512], P(('dp', 'tp'))
- input_grad: float32 [32768, 512], P(('dp', 'tp'))
- grad_norm: float32 [], replicated
- new_query: float32 [2, 512, 1536], P(None, 'dp', 'tp')
- new_first_query: float32 [2, 512, 1536], P(None, 'dp', 'tp')
- new_second_query: float32 [2, 512, 1536], P(None, 'dp', 'tp')
- new_average_query: float32 [2, 512, 1536], P(None, 'dp', 'tp')
- new_output: float32 [2, 512, 1536], P(None, 'dp', 'tp')
- new_first_output: float32 [2, 512, 1536], P(None, 'dp', 'tp')
- new_second_output: float32 [2, 512, 1536], P(None, 'dp', 'tp')
- new_average_output: float32 [2, 512, 1536], P(None, 'dp', 'tp')
- new_up: float32 [2, 512, 2048], P(None, 'dp', 'tp')
- new_first_up: float32 [2, 512, 2048], P(None, 'dp', 'tp')
- new_second_up: float32 [2, 512, 2048], P(None, 'dp', 'tp')
- new_average_up: float32 [2, 512, 2048], P(None, 'dp', 'tp')
- new_down: float32 [2, 512, 2048], P(None, 'dp', 'tp')
- new_first_down: float32 [2, 512, 2048], P(None, 'dp', 'tp')
- new_second_down: float32 [2, 512, 2048], P(None, 'dp', 'tp')
- new_average_down: float32 [2, 512, 2048], P(None, 'dp', 'tp')
- new_keyval: float32 [2, 512, 128], P(None, ('dp', 'tp'))
- new_first_keyval: float32 [2, 512, 128], P(None, ('dp', 'tp'))
- new_second_keyval: float32 [2, 512, 128], P(None, ('dp', 'tp'))
- new_average_keyval: float32 [2, 512, 128], P(None, ('dp', 'tp'))
- new_router: float32 [2, 512, 24], P(None, ('dp', 'tp'))
- new_first_router: float32 [2, 512, 24], P(None, ('dp', 'tp'))
- new_second_router: float32 [2, 512, 24], P(None, ('dp', 'tp'))
- new_average_router: float32 [2, 512, 24], P(None, ('dp', 'tp'))
- new_gains: float32 [2, 2, 512], P(None, None, ('dp', 'tp'))
- new_first_gains: float32 [2, 2, 512], P(None, None, ('dp', 'tp'))
- new_second_gains: float32 [2, 2, 512], P(None, None, ('dp', 'tp'))
- new_average_gains: float32 [2, 2, 512], P(None, None, ('dp', 'tp'))
The draws below stay inside these ranges and needn't reach their ends.
Inputs may be any that keep to these rules, and one draw needn't show every extreme that they name: `head_choice`: each token names 8 different head experts, and every expert is named by some token. `segment_ids`: within a packed row of 1024 tokens the ids never fall; a document covers at most half of a row, and some document covers exactly half.
All inputs are finite; a program needn't handle non-finite values.
Results may differ from the reference program's by a relative error of at most 0.03.
The reference program's roundings to bfloat16 on the way count: a program that leaves them out, or rounds other values in their place, can miss the bound.
Values may be sent and summed in bfloat16 or wider, within the bound.
No kernel may reach another device: no remote copies, remote signals or barrier semaphores. Data moves between devices by JAX's collectives and lax.ppermute only.
A program may use at most 320 MiB of HBM per device.

```python
import math
import jax
import jax.numpy as jnp
import numpy as np
from jax import lax

D = 512
E = 24
H = 64
TOPK = 8
FF = 2048
LEN = 1024
LAYERS = 2
STEP = 10
NSEQ = 32
TOKENS = 32768
NPARAM = 7497728


def draw_cotangent(key, part):
    column = jnp.arange(D).astype(jnp.float32) / (D - 1)
    column_scale = jnp.exp(jnp.log(4.0) * (column - 0.5))
    base = jnp.clip(jax.random.normal(key, (TOKENS, D), jnp.float32), -6.0, 6.0)
    return (base * column_scale[None, :]).astype(jnp.bfloat16)


def draw_norm_gains(key, part):
    column = jnp.arange(D).astype(jnp.float32) / (D - 1)
    rough = jax.random.uniform(key, (LAYERS, 2, D), jnp.float32, 0.8, 1.2)
    column_scale = 0.5 * jnp.exp(jnp.log(4.0) * column)
    return rough * column_scale[None, None, :]


def draw_average_gains(key, part):
    log_values = jax.random.uniform(key, (LAYERS, 2, D), jnp.float32, math.log(0.1), math.log(3.0))
    return jnp.clip(jnp.exp(log_values), 0.1, 3.0)


def level_of(stream_key, dims, split, low, largest):
    loudness = 1.0
    for dim, parts in split:
        draws = jax.random.uniform(jax.random.fold_in(jax.random.fold_in(stream_key, 6), dim), (parts,), jnp.float32, low / len(split), largest / len(split))
        loudness = loudness * jnp.repeat(jnp.exp(draws), dims[dim] // parts).reshape((-1,) + (1,) * (len(dims) - 1 - dim))
    return loudness


def distinct(own_key, rows, count, top, lift):
    ranking = jax.random.permutation(jax.random.fold_in(own_key, 1), count)
    pull = ranking
    for power in range(3):
        pull = pull * pull // count
    pull = pull * lift // count
    chance = jax.random.randint(jax.random.fold_in(own_key, 2), (rows, count), 0, 4096) + pull
    holders = jax.random.permutation(jax.random.fold_in(own_key, 3), rows)[jnp.arange(count) % rows]
    chance = jnp.where(jnp.arange(rows)[:, None] == holders[None, :], 1 << 14, chance)
    merit = chance * count + jnp.arange(count)
    return lax.top_k(merit.astype(jnp.int32), top)[1].astype(jnp.int32)


def length_profile(amount, total, bound, slope):
    weights = [(1 << 20) // math.isqrt(grade ** slope) + 1 for grade in range(2, amount + 1)]
    rest, holding = total - bound - (amount - 1), [1] * (amount - 1)
    while rest > 0:
        candidates = [i for i in range(amount - 1) if holding[i] < bound]
        pool, remaining = sum([weights[i] for i in candidates]), rest
        for i in candidates:
            more = min(bound - holding[i], max(1, remaining * weights[i] // pool), rest)
            holding[i] = holding[i] + more
            rest = rest - more
    return np.array([bound] + holding)


def ragged(key, number_of, total, most, lean):
    if number_of == 2:
        one = jax.random.randint(key, (), max(1, total - most), min(most, total - 1) + 1)
        return jnp.stack([one, total - one])
    lengths = jnp.asarray(length_profile(number_of, total, most, lean), jnp.int32)
    couples = (number_of - 1) // 2
    source_of, receiver = lengths[1:1 + 2 * couples:2], lengths[2:2 + 2 * couples:2]
    slack = jnp.minimum(source_of - 1, most - receiver)
    passed = jax.random.randint(jax.random.fold_in(key, 1), (couples,), 0, 1 << 20) % (slack + 1)
    lengths = lengths.at[1:1 + 2 * couples:2].set(source_of - passed).at[2:2 + 2 * couples:2].set(receiver + passed)
    return lengths[jax.random.permutation(jax.random.fold_in(key, 2), number_of)]


def normal_values(stream_key, shape, width, reach, shards=(), kind=jnp.bfloat16):
    array = jax.random.normal(stream_key, shape, jnp.float32) * width
    if len(shards) > 0:
        array = level_of(stream_key, shape, shards, -0.22, 0.18) * array
    return jnp.clip(array, min=-reach, max=reach).astype(kind)


def setup_inputs(seed: int = 0) -> dict:
    key_list = jax.random.split(jax.random.key(seed), 33)
    return {
        "tokens": normal_values(key_list[0], (TOKENS, D), 1.0, 6.0, ((0, 32),)),
        "cotangent": draw_cotangent(jax.random.fold_in(key_list[32], 71), 0),
        "head_choice": distinct(key_list[2], TOKENS, E, TOPK, 2730),
        "segment_ids": jax.vmap(lambda own: jnp.searchsorted(jnp.cumsum(ragged(own, 4, LEN, LEN // 2, 0)), jnp.arange(LEN), side="right"))(jax.random.split(key_list[3], NSEQ)).reshape((NSEQ, LEN)).astype(jnp.int32),
        "query_weight": normal_values(key_list[4], (LAYERS, D, E * H), D ** -0.5, 0.25, ((1, 8), (2, 4)), jnp.float32),
        "output_weight": normal_values(key_list[5], (LAYERS, D, E * H), (12.0 / (H ** 0.5)), 6.0, ((1, 8), (2, 4)), jnp.float32),
        "up_weight": normal_values(key_list[6], (LAYERS, D, FF), D ** -0.5, 0.25, ((1, 8), (2, 4)), jnp.float32),
        "down_weight": normal_values(key_list[7], (LAYERS, D, FF), (FF // 4) ** -0.5, 0.25, ((1, 8), (2, 4)), jnp.float32),
        "keyval_weight": normal_values(key_list[8], (LAYERS, D, 2 * H), D ** -0.5, 0.25, ((1, 32),), jnp.float32),
        "router_weight": normal_values(key_list[9], (LAYERS, D, E), (0.5 / (D ** 0.5)), 0.3125, ((1, 32),), jnp.float32),
        "norm_gains": draw_norm_gains(jax.random.fold_in(key_list[32], 71), 0),
        "first_query": normal_values(key_list[11], (LAYERS, D, E * H), (0.00275 / (NPARAM ** 0.5)), 1.52587890625e-05, ((1, 8), (2, 4)), jnp.float32),
        "first_output": normal_values(key_list[12], (LAYERS, D, E * H), (0.0001375 / (NPARAM ** 0.5)), 7.152557373046875e-07, ((1, 8), (2, 4)), jnp.float32),
        "first_up": normal_values(key_list[13], (LAYERS, D, FF), (0.00935 / (NPARAM ** 0.5)), 5.340576171875e-05, ((1, 8), (2, 4)), jnp.float32),
        "first_down": normal_values(key_list[14], (LAYERS, D, FF), (0.00385 / (NPARAM ** 0.5)), 1.9073486328125e-05, ((1, 8), (2, 4)), jnp.float32),
        "first_keyval": normal_values(key_list[15], (LAYERS, D, 2 * H), (0.0055 / (NPARAM ** 0.5)), 3.0517578125e-05, ((1, 32),), jnp.float32),
        "first_router": normal_values(key_list[16], (LAYERS, D, E), (0.0055 / (NPARAM ** 0.5)), 3.0517578125e-05, ((1, 32),), jnp.float32),
        "first_gains": normal_values(key_list[17], (LAYERS, 2, D), (0.0055 / (NPARAM ** 0.5)), 3.0517578125e-05, ((2, 32),), jnp.float32),
        "second_query": jnp.clip(jnp.exp(math.log(1.7538645882830828e-11) - 1.38553414 * jax.random.uniform(key_list[18], (LAYERS, D, E * H), jnp.float32) ** level_of(key_list[18], (LAYERS, D, E * H), ((1, 8), (2, 4)), -0.2, 0.2)), 4.387996042909403e-12, 1.7538645882830828e-11),
        "second_output": jnp.clip(jnp.exp(math.log(4.387995907384132e-14) - 1.3893385 * jax.random.uniform(key_list[19], (LAYERS, D, E * H), jnp.float32) ** level_of(key_list[19], (LAYERS, D, E * H), ((1, 8), (2, 4)), -0.2, 0.2)), 1.0936646316491664e-14, 4.387995907384132e-14),
        "second_up": jnp.clip(jnp.exp(math.log(2.0272808431975875e-10) - 1.3862944 * jax.random.uniform(key_list[20], (LAYERS, D, FF), jnp.float32) ** level_of(key_list[20], (LAYERS, D, FF), ((1, 8), (2, 4)), -0.2, 0.2)), 5.068202107993969e-11, 2.0272808431975875e-10),
        "second_down": jnp.clip(jnp.exp(math.log(3.441042242813275e-11) - 1.3862944 * jax.random.uniform(key_list[21], (LAYERS, D, FF), jnp.float32) ** level_of(key_list[21], (LAYERS, D, FF), ((1, 8), (2, 4)), -0.2, 0.2)), 8.602605607033187e-12, 3.441042242813275e-11),
        "second_keyval": jnp.clip(jnp.exp(math.log(7.015458353132331e-11) - 1.38553414 * jax.random.uniform(key_list[22], (LAYERS, D, 2 * H), jnp.float32) ** level_of(key_list[22], (LAYERS, D, 2 * H), ((1, 32),), -0.2, 0.2)), 1.7551984171637613e-11, 7.015458353132331e-11),
        "second_router": jnp.clip(jnp.exp(math.log(7.015458353132331e-11) - 1.38553414 * jax.random.uniform(key_list[23], (LAYERS, D, E), jnp.float32) ** level_of(key_list[23], (LAYERS, D, E), ((1, 32),), -0.2, 0.2)), 1.7551984171637613e-11, 7.015458353132331e-11),
        "second_gains": jnp.clip(jnp.exp(math.log(7.015458353132331e-11) - 1.38553414 * jax.random.uniform(key_list[24], (LAYERS, 2, D), jnp.float32) ** level_of(key_list[24], (LAYERS, 2, D), ((2, 32),), -0.2, 0.2)), 1.7551984171637613e-11, 7.015458353132331e-11),
        "average_query": normal_values(key_list[25], (LAYERS, D, E * H), D ** -0.5, 0.25, ((1, 8), (2, 4)), jnp.float32),
        "average_output": normal_values(key_list[26], (LAYERS, D, E * H), (12.0 / (H ** 0.5)), 6.0, ((1, 8), (2, 4)), jnp.float32),
        "average_up": normal_values(key_list[27], (LAYERS, D, FF), D ** -0.5, 0.25, ((1, 8), (2, 4)), jnp.float32),
        "average_down": normal_values(key_list[28], (LAYERS, D, FF), (FF // 4) ** -0.5, 0.25, ((1, 8), (2, 4)), jnp.float32),
        "average_keyval": normal_values(key_list[29], (LAYERS, D, 2 * H), D ** -0.5, 0.25, ((1, 32),), jnp.float32),
        "average_router": normal_values(key_list[30], (LAYERS, D, E), (0.5 / (D ** 0.5)), 0.3125, ((1, 32),), jnp.float32),
        "average_gains": draw_average_gains(jax.random.fold_in(key_list[32], 71), 0),
    }


@jax.custom_vjp
def low(v):
    return lax.optimization_barrier(v.astype(jnp.bfloat16)).astype(jnp.float32)

@jax.custom_vjp
def low_back(v):
    return v

def low_keep(v):
    return (low(v), None)

def low_pass(kept, grad):
    return (grad,)

def back_keep(v):
    return (v, None)

def back_low(kept, grad):
    return (low(grad),)
low.defvjp(low_keep, low_pass)
low_back.defvjp(back_keep, back_low)
epsilon = 1e-06
clip_bound = 0.05
learn_rates = (0.1, 1.0, 0.1, 0.1, 0.1, 0.1, 0.6)
beta_one = 0.9
beta_two = 0.95
adam_floor = 1e-08
weight_decay = 0.1
ema_decay = 0.7
masked_value = -1e+30

def product(left_op, right_op):
    return jnp.dot(left_op, right_op, precision=lax.Precision.HIGHEST, preferred_element_type=jnp.float32)

def normalize(row_data, gain):
    return row_data * lax.rsqrt(lax.optimization_barrier(jnp.mean(row_data * row_data, -1, keepdims=True)) + epsilon) * gain

def attend(members):
    query_seq, key_seq, value_seq, segment_row = members
    score_scale = H ** (-0.5)
    scores = low_back(jnp.einsum('qch,kh->cqk', query_seq, key_seq, precision=lax.Precision.HIGHEST) * score_scale)
    positions = jnp.arange(LEN)
    visible = (positions[None, :] <= positions[:, None]) & (segment_row[:, None] == segment_row[None, :])
    scores = jnp.where(visible[None], scores, masked_value)
    row_max = lax.optimization_barrier(jnp.max(scores, -1, keepdims=True))
    powers = jnp.exp(scores - row_max)
    attention = powers / lax.optimization_barrier(jnp.sum(powers, -1, keepdims=True))
    return jnp.einsum('cqk,kh->qch', low(attention), value_seq, precision=lax.Precision.HIGHEST)

def one_layer(residual, params, depth, picks, onehot, select, segments):
    query_w, output_w, up_w, down_w, keyval_w, router_w, gains = params
    act_rows = low(normalize(residual, gains[depth, 0]))
    logits = low_back(product(act_rows, low(router_w[depth])))
    powers = select * jnp.exp(logits - lax.optimization_barrier(jnp.max(logits, -1, keepdims=True)))
    gate_probs = low(powers / lax.optimization_barrier(jnp.sum(powers, -1, keepdims=True)))
    keyval = low_back(low(product(act_rows, low(keyval_w[depth]))))
    key_rows = keyval[:, :H].reshape(NSEQ, LEN, H)
    value_rows = keyval[:, H:].reshape(NSEQ, LEN, H)
    queries = product(act_rows, low(query_w[depth])).reshape(TOKENS, E, H)
    picked = low_back(low(jnp.take_along_axis(queries, picks[:, :, None], axis=1)))
    heads_out = lax.map(jax.checkpoint(attend), (picked.reshape(NSEQ, LEN, TOPK, H), key_rows, value_rows, segments))
    heads_out = low_back(heads_out.reshape(TOKENS, TOPK, H))
    gate_pick = jnp.take_along_axis(gate_probs, picks, axis=1)
    mixed_heads = low(gate_pick[:, :, None] * heads_out)
    spread = jnp.einsum('tke,tkh->teh', onehot, mixed_heads, precision=lax.Precision.HIGHEST).reshape(TOKENS, E * H)
    branch = low_back(product(spread, low(output_w[depth]).T))
    after_attn = residual + branch
    act_ffn = low(normalize(after_attn, gains[depth, 1]))
    pre_act = low_back(product(act_ffn, low(up_w[depth])))
    hidden = low(jax.nn.gelu(pre_act, approximate=True))
    ffn_out = low_back(product(hidden, low(down_w[depth]).T))
    return after_attn + ffn_out

def adamw(weight, moment_one, moment_two, average, grad_full, factor, learn_rate):
    clipped = grad_full * factor
    first_new = beta_one * moment_one + (1.0 - beta_one) * clipped
    second_new = beta_two * moment_two + (1.0 - beta_two) * clipped * clipped
    step_ratio = first_new / (1.0 - beta_one ** STEP) / (jnp.sqrt(second_new / (1.0 - beta_two ** STEP)) + adam_floor)
    weight_new = weight - learn_rate * (step_ratio + weight_decay * weight)
    return (weight_new, first_new, second_new, ema_decay * average + (1.0 - ema_decay) * weight_new)

def reference(tokens, cotangent, head_choice, segment_ids, query_weight, output_weight, up_weight, down_weight, keyval_weight, router_weight, norm_gains, first_query, first_output, first_up, first_down, first_keyval, first_router, first_gains, second_query, second_output, second_up, second_down, second_keyval, second_router, second_gains, average_query, average_output, average_up, average_down, average_keyval, average_router, average_gains):
    onehot = (head_choice[:, :, None] == jnp.arange(E)[None, None, :]).astype(jnp.float32)
    select = lax.optimization_barrier(jnp.sum(onehot, 1))
    weights = (query_weight, output_weight, up_weight, down_weight, keyval_weight, router_weight, norm_gains)

    def forward(residual, params):
        for depth in range(LAYERS):
            residual = one_layer(residual, params, depth, head_choice, onehot, select, segment_ids)
        return residual
    result, pullback = jax.vjp(forward, tokens.astype(jnp.float32), weights)
    input_grad, raw_grads = pullback(cotangent.astype(jnp.float32))
    grads = [entry_grad / TOKENS for entry_grad in raw_grads]
    squares = jnp.sum(jnp.stack([jnp.sum(entry_grad * entry_grad) for entry_grad in grads]))
    grad_norm = jnp.sqrt(squares)
    factor = jnp.minimum(1.0, clip_bound / grad_norm)
    firsts = (first_query, first_output, first_up, first_down, first_keyval, first_router, first_gains)
    seconds = (second_query, second_output, second_up, second_down, second_keyval, second_router, second_gains)
    averages = (average_query, average_output, average_up, average_down, average_keyval, average_router, average_gains)
    updates = []
    for position in range(7):
        updates.append(adamw(weights[position], firsts[position], seconds[position], averages[position], grads[position], factor, learn_rates[position]))
    return (result.astype(jnp.bfloat16), input_grad, grad_norm, updates[0][0], updates[0][1], updates[0][2], updates[0][3], updates[1][0], updates[1][1], updates[1][2], updates[1][3], updates[2][0], updates[2][1], updates[2][2], updates[2][3], updates[3][0], updates[3][1], updates[3][2], updates[3][3], updates[4][0], updates[4][1], updates[4][2], updates[4][3], updates[5][0], updates[5][1], updates[5][2], updates[5][3], updates[6][0], updates[6][1], updates[6][2], updates[6][3])
```

```python
import functools

import jax
import jax.numpy as jnp
from jax import lax
from jax.experimental import pallas as pl
from jax.experimental.pallas import tpu as pltpu
from jax.sharding import PartitionSpec as P

E = 24
H = 64
TOPK = 8
LEN = 1024
LAYERS = 2
STEP = 10
D = 512
FF = 2048
EH = E * H
KH = TOPK * H
PAIRS = TOPK // 2
COLS = EH // 128
ROWS = 256
STEPS = LEN // ROWS
SUB = 128
VDP = 8
VTP = 4
RW = D // VDP
CA = EH // VTP
CF = FF // VTP
RM = D // (VDP * VTP)
RA = 2 * RW + RM
RQ = RW + RM
VMEM = 60 * 1024 * 1024

epsilon = 1e-06
clip_bound = 0.05
learn_rates = (0.1, 1.0, 0.1, 0.1, 0.1, 0.1, 0.6)
beta_one = 0.9
beta_two = 0.95
adam_floor = 1e-08
weight_decay = 0.1
ema_decay = 0.7
masked_value = -1e30
f32 = jnp.float32
bf16 = jnp.bfloat16


def dot(a, b):
    return lax.dot_general(a, b, (((1,), (0,)), ((), ())), preferred_element_type=f32)


def dot_nt(a, b):
    return lax.dot_general(a, b, (((1,), (1,)), ((), ())), preferred_element_type=f32)


def lanes(rows, dtype=jnp.int32):
    return lax.broadcasted_iota(jnp.int32, (rows, 128), 1).astype(dtype)


def normalize(x):
    factor = lax.rsqrt(jnp.mean(x * x, -1, keepdims=True) + epsilon)
    return x * factor, factor


def both_halves(x, low_half):
    turned = pltpu.roll(x, 64, 1)
    return jnp.where(low_half, x, turned), jnp.where(low_half, turned, x)


def slot_columns(hc):
    rows = hc.shape[0]
    return [jnp.broadcast_to(hc[:, k : k + 1], (rows, 128)).astype(bf16) for k in range(TOPK)]


def pick_heads(full, slots):
    rows = full.shape[0]
    low_half = lanes(rows) < 64
    low_half16 = lanes(rows).astype(bf16) < jnp.asarray(64, bf16)
    pairs = [jnp.where(low_half16, slots[2 * p], slots[2 * p + 1]) for p in range(PAIRS)]
    out = [jnp.zeros((rows, 128), bf16) for _ in range(PAIRS)]
    for c in range(COLS):
        even, odd = both_halves(full[:, c * 128 : (c + 1) * 128], low_half)
        even = even.astype(bf16)
        odd = odd.astype(bf16)
        for p in range(PAIRS):
            out[p] = jnp.where(pairs[p] == jnp.asarray(2 * c, bf16), even, out[p])
            out[p] = jnp.where(pairs[p] == jnp.asarray(2 * c + 1, bf16), odd, out[p])
    return out


def spread_heads(pair_values, slots, store):
    rows = pair_values[0].shape[0]
    low_half = lanes(rows) < 64
    copies = []
    for p in range(PAIRS):
        even, odd = both_halves(pair_values[p], low_half)
        copies += [even.astype(bf16), odd.astype(bf16)]
    half = jnp.where(lanes(rows).astype(bf16) < jnp.asarray(64, bf16), jnp.asarray(0, bf16), jnp.asarray(1, bf16))
    for c in range(COLS):
        expert = half + jnp.asarray(2 * c, bf16)
        total = jnp.zeros((rows, 128), bf16)
        for k in range(TOPK):
            total = jnp.where(slots[k] == expert, copies[k], total)
        store(c, total)


def place(refs, scratch, idx, first, count, width):
    stride = refs[0].shape[0] // VTP
    for j in range(VDP):
        row = pl.multiple_of(idx[j] * count, count)
        for q in range(VTP):
            col = pl.multiple_of(idx[VDP + q] * width, 128)
            scratch[pl.ds(row, count), pl.ds(col, width)] = refs[j][
                q * stride + first : q * stride + first + count, :
            ]


def place_misc(refs, scratch, idx, first):
    stride = refs[0].shape[0] // VTP
    for j in range(VDP):
        for q in range(VTP):
            row = pl.multiple_of((idx[j] * VTP + idx[VDP + q]) * RM, RM)
            scratch[pl.ds(row, RM), :] = refs[j][q * stride + first : q * stride + first + RM, :]


def hand_out(keep, send, grad, idx, first, count):
    for j in range(VDP):
        row = pl.multiple_of(idx[j] * count, count)
        target = keep if j % 2 == 0 else send
        target[j // 2, 0, first : first + count, :] = grad[pl.ds(row, count), :].astype(bf16)


def bias_of(segc, segr_ref, row0, start, width):
    rows = row0 + lax.broadcasted_iota(jnp.int32, (SUB, width), 0)
    cols = start + lax.broadcasted_iota(jnp.int32, (SUB, width), 1)
    same = segc[:, 0:1] == segr_ref[0:1, pl.ds(start, width)]
    return jnp.where((cols <= rows) & same, 0.0, masked_value).astype(f32)


def attn_forward_kernel(idx, x_ref, hc_ref, segc_ref, segr_ref, *rest):
    w_refs = rest[:VDP]
    (mid_ref, qs_ref, kv_ref, ho_ref, lse_ref, spread_ref, gate_ref, gsl_ref, gains_ref) = rest[VDP : VDP + 9]
    (wq, wo, misc, gain_s, kt_lo, kt_hi, v_lo, v_hi, qst, mixed_s) = rest[VDP + 9 :]
    step = pl.program_id(0)

    @pl.when(step == 0)
    def _():
        place(w_refs, wq, idx, 0, RW, CA)
        place(w_refs, wo, idx, RW, RW, CA)
        place_misc(w_refs, misc, idx, 2 * RW)
        turned = misc[:, 128:256].astype(f32).T
        gain_s[...] = jnp.zeros_like(gain_s)
        gain_s[0:1, :] = turned[24:25] + turned[25:26] + turned[26:27]
        gain_s[1:2, :] = turned[27:28] + turned[28:29] + turned[29:30]
        gains_ref[...] = gain_s[...]

    x = x_ref[...].astype(f32)
    normed, _ = normalize(x)
    act = (normed * gain_s[0:1, :]).astype(bf16)
    hc = hc_ref[...]
    slots = slot_columns(hc)
    low_half = lanes(ROWS) < 64
    lane = lanes(ROWS)
    small = dot(act, misc[:, 0:256])
    kv = small[:, 0:128].astype(bf16)
    logits = jnp.where(lane < E, small[:, 128:256], masked_value)
    top = jnp.max(logits, -1, keepdims=True)
    lane_f = lane.astype(f32)
    hit = [hc[:, k : k + 1] == lane_f for k in range(TOPK)]
    chosen = hit[0]
    for k in range(1, TOPK):
        chosen = chosen | hit[k]
    powers = jnp.where(chosen, jnp.exp(logits - top), 0.0)
    gate = powers / jnp.sum(powers, -1, keepdims=True)
    gate_ref[...] = gate
    gate_low = gate.astype(bf16).astype(f32)
    gates = [jnp.sum(jnp.where(hit[k], gate_low, 0.0), -1, keepdims=True) for k in range(TOPK)]
    compact = jnp.zeros((ROWS, 128), f32)
    for p in range(PAIRS):
        compact = jnp.where(lane == p, gates[2 * p], compact)
        compact = jnp.where(lane == 64 + p, gates[2 * p + 1], compact)
    gsl_ref[...] = compact
    kv_ref[...] = kv
    row = pl.multiple_of(step * ROWS, ROWS)
    kv_f = kv.astype(f32)
    k_lo = jnp.where(low_half, kv_f, 0.0)
    k_hi = pltpu.roll(k_lo, 64, 1)
    val_hi = jnp.where(low_half, 0.0, kv_f)
    val_lo = pltpu.roll(val_hi, 64, 1)
    kt_lo[:, pl.ds(row, ROWS)] = k_lo.T.astype(bf16)
    kt_hi[:, pl.ds(row, ROWS)] = k_hi.T.astype(bf16)
    ones = jnp.where(low_half, 1.0, 0.0)
    v_lo[pl.ds(row, ROWS), 0:128] = val_lo.astype(bf16)
    v_lo[pl.ds(row, ROWS), 128:256] = ones.astype(bf16)
    v_hi[pl.ds(row, ROWS), 0:128] = val_hi.astype(bf16)
    v_hi[pl.ds(row, ROWS), 128:256] = (1.0 - ones).astype(bf16)
    queries = dot(act, wq[...])
    picked = pick_heads(queries, slots)
    for p in range(PAIRS):
        scaled = picked[p] * jnp.asarray(H ** (-0.5), bf16)
        qs_ref[:, p * 128 : (p + 1) * 128] = scaled
        for s in range(ROWS // SUB):
            qst[s, p * SUB : (p + 1) * SUB, :] = scaled[s * SUB : (s + 1) * SUB]

    for s in range(ROWS // SUB):
        block = step * (ROWS // SUB) + s
        count = idx[VDP + VTP + block]
        rows = slice(s * SUB, (s + 1) * SUB)

        def attend(n, s=s, block=block, rows=rows):
            width = n * SUB
            start = pl.multiple_of((block + 1 - n) * SUB, SUB)
            bias = bias_of(segc_ref[rows, :], segr_ref, block * SUB, start, width)
            q4 = qst[s]
            parts = []
            tops = []
            for kt in (kt_lo, kt_hi):
                scores = dot(q4, kt[:, pl.ds(start, width)]).reshape(PAIRS, SUB, width) + bias[None]
                peak = jnp.max(scores, -1, keepdims=True)
                parts.append(jnp.exp(scores - peak).astype(bf16).reshape(PAIRS * SUB, width))
                tops.append(peak.reshape(PAIRS * SUB, 1))
            result = dot(parts[0], v_lo[pl.ds(start, width), :]) + dot(parts[1], v_hi[pl.ds(start, width), :])
            total = result[:, 128:256]
            heads = result[:, 0:128] / total
            log_sum = jnp.where(lanes(PAIRS * SUB) < 64, tops[0], tops[1]) + jnp.log(total)
            keep = jnp.zeros((SUB, 128), f32)
            for p in range(PAIRS):
                one = slice(p * SUB, (p + 1) * SUB)
                ho_ref[rows, p * 128 : (p + 1) * 128] = heads[one]
                keep = jnp.where((lanes(SUB) & 63) == p, log_sum[one], keep)
            lse_ref[rows, :] = keep

        for n in range(1, 6):
            pl.when(count == n)(functools.partial(attend, n))

    mixed = []
    for p in range(PAIRS):
        gate_pair = jnp.where(low_half, gates[2 * p], gates[2 * p + 1])
        mixed.append(gate_pair * ho_ref[:, p * 128 : (p + 1) * 128])

    def store(c, value):
        spread_ref[:, c * 128 : (c + 1) * 128] = value

    spread_heads(mixed, slots, store)
    mid_ref[...] = x + dot_nt(spread_ref[...], wo[...])


def ffn_forward_kernel(last, idx, x_ref, gains_ref, *rest):
    w_refs = rest[:VDP]
    out_ref = rest[VDP]
    wu, wd = rest[VDP + 1 :]

    @pl.when(pl.program_id(0) == 0)
    def _():
        place(w_refs, wu, idx, 0, RW, CF)
        place(w_refs, wd, idx, RW, RW, CF)

    x = x_ref[...]
    normed, _ = normalize(x)
    act = (normed * gains_ref[1:2, :]).astype(bf16)
    pre = dot(act, wu[...])
    hidden = jax.nn.gelu(pre, approximate=True).astype(bf16)
    out_ref[...] = (x + dot_nt(hidden, wd[...])).astype(out_ref.dtype)


def ffn_backward_kernel(idx, up_ref, x_ref, gains_ref, *rest):
    w_refs = rest[:VDP]
    mid_ref, gain_ref, keep_ref, send_ref = rest[VDP : VDP + 4]
    wu, wd, hid_s, gp_s, grad_t, act_t, part = rest[VDP + 4 :]
    step = pl.program_id(0)

    @pl.when(step == 0)
    def _():
        place(w_refs, wu, idx, 0, RW, CF)
        place(w_refs, wd, idx, RW, RW, CF)
        gain_ref[...] = jnp.zeros_like(gain_ref)

    @pl.when(step < STEPS)
    def _():
        row = pl.multiple_of(step * ROWS, ROWS)
        up = up_ref[...].astype(f32)
        gain = gains_ref[1:2, :]
        normed, factor = normalize(x_ref[...])
        act_f = normed * gain
        act = act_f.astype(bf16)
        act_t[:, pl.ds(row, ROWS)] = act_f.T.astype(bf16)
        grad_t[:, pl.ds(row, ROWS)] = up.T.astype(bf16)
        pre = dot(act, wu[...])
        grad_hidden = dot(up.astype(bf16), wd[...])
        square = pre * pre
        arg = 0.7978845608028654 * pre * (1.0 + 0.044715 * square)
        bend = jnp.tanh(arg)
        half = 0.5 * (1.0 + bend)
        hid_s[pl.ds(row, ROWS), :] = (pre * half).astype(bf16)
        slope = half + (0.5 * 0.7978845608028654) * pre * (1.0 - bend * bend) * (
            1.0 + 3.0 * 0.044715 * square
        )
        grad_pre = (grad_hidden * slope).astype(bf16)
        gp_s[pl.ds(row, ROWS), :] = grad_pre
        grad_act = dot_nt(grad_pre, wu[...])
        scaled = grad_act * gain
        inner = jnp.mean(scaled * normed, -1, keepdims=True)
        mid_ref[...] = up + factor * (scaled - normed * inner)
        gain_ref[0:1, :] += jnp.sum(grad_act * normed, 0, keepdims=True)

    @pl.when(step >= STEPS)
    def _():
        q = step - STEPS
        col = pl.multiple_of(idx[VDP + q] * CF, CF)
        part[...] = dot(act_t[...], gp_s[:, pl.ds(col, CF)])
        hand_out(keep_ref, send_ref, part, idx, 0, RW)
        part[...] = dot(grad_t[...], hid_s[:, pl.ds(col, CF)])
        hand_out(keep_ref, send_ref, part, idx, RW, RW)


def output_backward_kernel(idx, mid_ref, hc_ref, ho_ref, gate_ref, gsl_ref, spread_ref, *rest):
    w_refs = rest[:VDP]
    gh_ref, dd_ref, gl_ref, keep_ref, send_ref = rest[VDP : VDP + 5]
    wo, grad_t, part = rest[VDP + 5 :]
    step = pl.program_id(0)

    @pl.when(step == 0)
    def _():
        place(w_refs, wo, idx, RW, RW, CA)

    @pl.when(step < STEPS)
    def _():
        row = pl.multiple_of(step * ROWS, ROWS)
        mid = mid_ref[...]
        grad_t[:, pl.ds(row, ROWS)] = mid.T.astype(bf16)
        full = dot(mid.astype(bf16), wo[...])
        hc = hc_ref[...]
        slots = slot_columns(hc)
        mixed = pick_heads(full, slots)
        lane = lanes(ROWS)
        low_half = lane < 64
        lane_f = lane.astype(f32)
        gsl = gsl_ref[...]
        inner = jnp.zeros((ROWS, 128), f32)
        grad_gates = jnp.zeros((ROWS, 128), f32)
        for p in range(PAIRS):
            value = mixed[p].astype(f32)
            ga = gsl[:, p : p + 1]
            gb = gsl[:, 64 + p : 65 + p]
            gh_ref[:, p * 128 : (p + 1) * 128] = (jnp.where(low_half, ga, gb) * value).astype(bf16)
            product = value * ho_ref[:, p * 128 : (p + 1) * 128]
            sum_a = jnp.sum(jnp.where(low_half, product, 0.0), -1, keepdims=True)
            sum_b = jnp.sum(jnp.where(low_half, 0.0, product), -1, keepdims=True)
            inner = jnp.where(lane == p, ga * sum_a, inner)
            inner = jnp.where(lane == 64 + p, gb * sum_b, inner)
            grad_gates = jnp.where(hc[:, 2 * p : 2 * p + 1] == lane_f, sum_a, grad_gates)
            grad_gates = jnp.where(hc[:, 2 * p + 1 : 2 * p + 2] == lane_f, sum_b, grad_gates)
        dd_ref[...] = inner
        gate = gate_ref[...]
        total = jnp.sum(gate * grad_gates, -1, keepdims=True)
        gl_ref[...] = (gate * (grad_gates - total)).astype(bf16)

    @pl.when(step >= STEPS)
    def _():
        q = step - STEPS
        col = pl.multiple_of(idx[VDP + q] * CA, 128)
        part[...] = dot(grad_t[...], spread_ref[:, pl.ds(col, CA)])
        hand_out(keep_ref, send_ref, part, idx, 0, RW)


def attn_backward_kernel(
    idx, mid_ref, x_ref, hc_ref, segc_ref, segr_ref, qs_ref, gh_ref, kv_ref, lse_ref, dd_ref, gl_ref, gains_ref, gfg_ref, *rest
):
    w_refs = rest[:VDP]
    out_ref, keep_ref, send_ref = rest[VDP : VDP + 3]
    (wq, misc, kt_lo, kt_hi, vt_lo, vt_hi, k_lo, k_hi, dkv_t, qst, gst, dq_s, gq_s, act_t, dkv_s, gain_s, part, pmisc) = rest[
        VDP + 3 :
    ]
    step = pl.program_id(0)

    @pl.when(step == 0)
    def _():
        place(w_refs, wq, idx, 0, RW, CA)
        place_misc(w_refs, misc, idx, 2 * RW)
        low = lanes(LEN) < 64
        kv = kv_ref[...].astype(f32)
        one = jnp.where(low, kv, 0.0)
        two = pltpu.roll(one, 64, 1)
        k_lo[...] = one.astype(bf16)
        k_hi[...] = two.astype(bf16)
        kt_lo[...] = one.T.astype(bf16)
        kt_hi[...] = two.T.astype(bf16)
        one = jnp.where(low, 0.0, kv)
        vt_hi[...] = one.T.astype(bf16)
        vt_lo[...] = pltpu.roll(one, 64, 1).T.astype(bf16)
        dkv_t[...] = jnp.zeros_like(dkv_t)
        gain_s[...] = jnp.zeros_like(gain_s)

    @pl.when(step < STEPS)
    def _():
        row = pl.multiple_of(step * ROWS, ROWS)
        for p in range(PAIRS):
            for s in range(ROWS // SUB):
                qst[s, p * SUB : (p + 1) * SUB, :] = qs_ref[s * SUB : (s + 1) * SUB, p * 128 : (p + 1) * 128]
                gst[s, p * SUB : (p + 1) * SUB, :] = gh_ref[s * SUB : (s + 1) * SUB, p * 128 : (p + 1) * 128]
        for s in range(ROWS // SUB):
            block = step * (ROWS // SUB) + s
            count = idx[VDP + VTP + block]
            rows = slice(s * SUB, (s + 1) * SUB)

            def attend(n, s=s, block=block, rows=rows):
                width = n * SUB
                start = pl.multiple_of((block + 1 - n) * SUB, SUB)
                win = pl.ds(start, width)
                bias = bias_of(segc_ref[rows, :], segr_ref, block * SUB, start, width)
                q4 = qst[s]
                g4 = gst[s]
                q4t = q4.astype(f32).T.astype(bf16)
                g4t = g4.astype(f32).T.astype(bf16)
                lse = lse_ref[rows, :]
                dd = dd_ref[rows, :]
                dq = None
                dk = None
                dv = None
                for half, (kt, vt, kk) in enumerate(((kt_lo, vt_lo, k_lo), (kt_hi, vt_hi, k_hi))):
                    off = 64 * half
                    log_sum = jnp.stack([lse[:, off + p : off + p + 1] for p in range(PAIRS)])
                    inner = jnp.stack([dd[:, off + p : off + p + 1] for p in range(PAIRS)])
                    scores = dot(q4, kt[:, win]).reshape(PAIRS, SUB, width)
                    prob = jnp.exp(scores + bias[None] - log_sum)
                    dprob = dot(g4, vt[:, win]).reshape(PAIRS, SUB, width)
                    dscore = (prob * (dprob - inner)).astype(bf16).reshape(PAIRS * SUB, width)
                    low_prob = prob.astype(bf16).reshape(PAIRS * SUB, width)
                    a = dot(dscore, kk[win, :])
                    b = dot(q4t[off : off + 64], dscore)
                    c = dot(g4t[off : off + 64], low_prob)
                    dq = a if dq is None else dq + a
                    dk = b if dk is None else dk + b
                    dv = c if dv is None else dv + c
                dkv_t[0:64, win] += dk
                dkv_t[64:128, win] += dv
                dq = dq * (H ** (-0.5))
                for p in range(PAIRS):
                    dq_s[rows, p * 128 : (p + 1) * 128] = dq[p * SUB : (p + 1) * SUB]

            for n in range(1, 6):
                pl.when(count == n)(functools.partial(attend, n))

        slots = slot_columns(hc_ref[...])

        def store(c, value):
            gq_s[pl.ds(row, ROWS), c * 128 : (c + 1) * 128] = value

        spread_heads([dq_s[:, p * 128 : (p + 1) * 128] for p in range(PAIRS)], slots, store)

    @pl.when(step == STEPS)
    def _():
        dkv_s[...] = dkv_t[...].T.astype(bf16)

    @pl.when((step >= STEPS) & (step < 2 * STEPS))
    def _():
        row = pl.multiple_of((step - STEPS) * ROWS, ROWS)
        here = pl.ds(row, ROWS)
        gain = gains_ref[0:1, :]
        normed, factor = normalize(x_ref[...].astype(f32))
        act_t[:, here] = (normed * gain).T.astype(bf16)
        grad_act = dot_nt(gq_s[here, :], wq[...])
        grad_act += dot_nt(dkv_s[here, :], misc[:, 0:128])
        router = jnp.where(lanes(D) < E, misc[:, 128:256].astype(f32), 0.0).astype(bf16)
        grad_act += dot_nt(gl_ref[here, :], router)
        scaled = grad_act * gain
        inner = jnp.mean(scaled * normed, -1, keepdims=True)
        out_ref[...] = mid_ref[...] + factor * (scaled - normed * inner)
        gain_s[0:1, :] += jnp.sum(grad_act * normed, 0, keepdims=True)

    @pl.when(step == 2 * STEPS)
    def _():
        pmisc[:, 0:128] = dot(act_t[...], dkv_s[...])
        router = dot(act_t[...], gl_ref[...])
        gain_s[1:2, :] = gfg_ref[0:1, :]
        turned = gain_s[...].T
        lane = lanes(D)
        router = jnp.where(lane < E, router, 0.0)
        router = jnp.where(lane == E, turned[:, 0:1], router)
        router = jnp.where(lane == E + 1, turned[:, 1:2], router)
        pmisc[:, 128:256] = router
        pmisc[:, 256:384] = jnp.zeros((D, 128), f32)

    @pl.when(step >= 2 * STEPS)
    def _():
        q = step - 2 * STEPS
        col = pl.multiple_of(idx[VDP + q] * CA, 128)
        part[...] = dot(act_t[...], gq_s[:, pl.ds(col, CA)])
        hand_out(keep_ref, send_ref, part, idx, 0, RW)
        for j in range(VDP):
            row = pl.multiple_of((idx[j] * VTP + idx[VDP + q]) * RM, RM)
            target = keep_ref if j % 2 == 0 else send_ref
            target[j // 2, 0, RW : RW + RM, :] = pmisc[pl.ds(row, RM), :].astype(bf16)


def rows_spec(width, phase=0, single=False):
    def index(i, idx):
        return (jnp.clip(i - phase * STEPS, 0, STEPS - 1), 0)

    return pl.BlockSpec((ROWS, width), index)


def full_spec(shape):
    zeros = (0,) * len(shape)
    return pl.BlockSpec(shape, lambda i, idx: zeros, pipeline_mode=pl.Buffered(1))


def kept_spec(shape):
    zeros = (0,) * len(shape)
    return pl.BlockSpec(shape, lambda i, idx: zeros)


def parts_spec(rows, width, phase):
    def index(i, idx):
        return (0, jnp.maximum(i - phase * STEPS, 0), 0, 0)

    return pl.BlockSpec((4, 1, rows, width), index)


def call(kernel, steps, in_specs, out_specs, out_shapes, scratch, name, flops, moved):
    return pl.pallas_call(
        kernel,
        grid_spec=pltpu.PrefetchScalarGridSpec(
            num_scalar_prefetch=1,
            grid=(steps,),
            in_specs=in_specs,
            out_specs=out_specs,
            scratch_shapes=scratch,
        ),
        out_shape=[jax.ShapeDtypeStruct(s, d) for s, d in out_shapes],
        compiler_params=pltpu.CompilerParams(
            dimension_semantics=("arbitrary",), vmem_limit_bytes=VMEM
        ),
        cost_estimate=pl.CostEstimate(flops=flops, bytes_accessed=moved, transcendentals=0),
        name=name,
    )


def vm(*shape, dtype=bf16):
    return pltpu.VMEM(shape, dtype)


def attn_forward(idx, x, hc, segc, segr, weights):
    return call(
        attn_forward_kernel,
        STEPS,
        [rows_spec(D), rows_spec(TOPK), rows_spec(128), full_spec((8, LEN))]
        + [full_spec((VTP * RA, CA))] * VDP,
        [
            rows_spec(D), rows_spec(KH), rows_spec(128), rows_spec(KH), rows_spec(128),
            rows_spec(EH), rows_spec(128), rows_spec(128), kept_spec((8, D)),
        ],
        [
            ((LEN, D), f32), ((LEN, KH), bf16), ((LEN, 128), bf16), ((LEN, KH), f32), ((LEN, 128), f32),
            ((LEN, EH), bf16), ((LEN, 128), f32), ((LEN, 128), f32), ((8, D), f32),
        ],
        [
            vm(D, EH), vm(D, EH), vm(D, 384), vm(8, D, dtype=f32), vm(128, LEN), vm(128, LEN),
            vm(LEN, 256), vm(LEN, 256), vm(ROWS // SUB, PAIRS * SUB, 128), vm(ROWS, 128),
        ],
        "attn_forward", 8 * 10**9, 14 * 10**6,
    )(idx, x, hc, segc, segr, *weights)


def ffn_forward(idx, x, gains, weights, last):
    return call(
        functools.partial(ffn_forward_kernel, last),
        STEPS,
        [rows_spec(D), full_spec((8, D))] + [full_spec((VTP * 2 * RW, CF))] * VDP,
        [rows_spec(D)],
        [((LEN, D), bf16 if last else f32)],
        [vm(D, FF), vm(D, FF)],
        "ffn_forward", 5 * 10**9, 8 * 10**6,
    )(idx, x, gains, *weights)[0]


def ffn_backward(idx, upstream, x, gains, weights):
    return call(
        ffn_backward_kernel,
        2 * STEPS,
        [rows_spec(D), rows_spec(D), full_spec((8, D))] + [full_spec((VTP * 2 * RW, CF))] * VDP,
        [rows_spec(D), kept_spec((8, D)), parts_spec(2 * RW, CF, 1), parts_spec(2 * RW, CF, 1)],
        [
            ((LEN, D), f32), ((8, D), f32),
            ((4, VTP, 2 * RW, CF), bf16), ((4, VTP, 2 * RW, CF), bf16),
        ],
        [
            vm(D, FF), vm(D, FF), vm(LEN, FF), vm(LEN, FF), vm(D, LEN), vm(D, LEN), vm(D, CF, dtype=f32),
        ],
        "ffn_backward", 13 * 10**9, 14 * 10**6,
    )(idx, upstream, x, gains, *weights)


def output_backward(idx, mid, hc, heads, gate, gsl, spread, weights):
    return call(
        output_backward_kernel,
        2 * STEPS,
        [rows_spec(D), rows_spec(TOPK), rows_spec(KH), rows_spec(128), rows_spec(128), full_spec((LEN, EH))]
        + [full_spec((VTP * RA, CA))] * VDP,
        [rows_spec(KH), rows_spec(128), rows_spec(128), parts_spec(RW, CA, 1), parts_spec(RW, CA, 1)],
        [
            ((LEN, KH), bf16), ((LEN, 128), f32), ((LEN, 128), bf16),
            ((4, VTP, RW, CA), bf16), ((4, VTP, RW, CA), bf16),
        ],
        [vm(D, EH), vm(D, LEN), vm(D, CA, dtype=f32)],
        "output_backward", 5 * 10**9, 16 * 10**6,
    )(idx, mid, hc, heads, gate, gsl, spread, *weights)


def attn_backward(idx, mid, x, hc, segc, segr, qs, gh, kv, lse, dd, gl, gains, gfg, weights):
    return call(
        attn_backward_kernel,
        3 * STEPS,
        [
            rows_spec(D, 1), rows_spec(D, 1), rows_spec(TOPK), rows_spec(128), full_spec((8, LEN)),
            rows_spec(KH), rows_spec(KH), full_spec((LEN, 128)), rows_spec(128), rows_spec(128),
            full_spec((LEN, 128)), full_spec((8, D)), full_spec((8, D)),
        ]
        + [full_spec((VTP * RA, CA))] * VDP,
        [rows_spec(D, 1), parts_spec(RQ, CA, 2), parts_spec(RQ, CA, 2)],
        [((LEN, D), f32), ((4, VTP, RQ, CA), bf16), ((4, VTP, RQ, CA), bf16)],
        [
            vm(D, EH), vm(D, 384), vm(128, LEN), vm(128, LEN), vm(128, LEN), vm(128, LEN),
            vm(LEN, 128), vm(LEN, 128), vm(128, LEN, dtype=f32), vm(ROWS // SUB, PAIRS * SUB, 128),
            vm(ROWS // SUB, PAIRS * SUB, 128), vm(ROWS, KH, dtype=f32), vm(LEN, EH), vm(D, LEN),
            vm(LEN, 128), vm(8, D, dtype=f32), vm(D, CA, dtype=f32), vm(D, 384, dtype=f32),
        ],
        "attn_backward", 10 * 10**9, 16 * 10**6,
    )(idx, mid, x, hc, segc, segr, qs, gh, kv, lse, dd, gl, gains, gfg, *weights)


def shift(size, k):
    return [(i, (i - k) % size) for i in range(size)]


def unshift(size, k):
    return [(i, (i + k) % size) for i in range(size)]


def swap(k):
    return [(i, i ^ k) for i in range(VDP)]


def gather_piece(mine):
    stack = jnp.concatenate(
        [mine] + [lax.ppermute(mine, "tp", unshift(VTP, k)) for k in range(1, VTP)], 0
    )
    plane = [stack] + [lax.ppermute(stack, "dp", swap(2 * k)) for k in range(1, 4)]
    other = [lax.ppermute(part, "dp", swap(1)) for part in plane]
    return [plane[j // 2] if j % 2 == 0 else other[j // 2] for j in range(VDP)]


def reduce_piece(keep, send):
    got = lax.ppermute(send, "dp", swap(1))
    pair = [(keep[k].astype(f32) + got[k].astype(f32)).astype(bf16) for k in range(4)]
    total = pair[0].astype(f32)
    for k in range(1, 4):
        total = total + lax.ppermute(pair[k], "dp", swap(2 * k)).astype(f32)
    line = total.astype(bf16)
    total = line[0].astype(f32)
    for k in range(1, VTP):
        total = total + lax.ppermute(line[k], "tp", shift(VTP, k)).astype(f32)
    return total


def block_piece(whole_parts, misc):
    out = []
    for j in range(VDP):
        stack = []
        for q in range(VTP):
            for part in whole_parts:
                width = part.shape[1] // VTP
                stack.append(part[j * RW : (j + 1) * RW, q * width : (q + 1) * width])
            if misc is not None:
                row = (j * VTP + q) * RM
                stack.append(misc[row : row + RM])
        out.append(jnp.concatenate(stack, 0))
    return out


def unblock_piece(keep, send, counts):
    both = jnp.stack([keep, send], 1).reshape((VDP,) + keep.shape[1:])
    out = []
    first = 0
    for count in counts:
        part = both[:, :, first : first + count]
        first += count
        if count == RW:
            out.append(part.transpose(0, 2, 1, 3).reshape(D, VTP * part.shape[3]))
        else:
            out.append(part.reshape(D, part.shape[3]))
    return out


def split_gain(gain):
    high = lax.reduce_precision(gain, 8, 7)
    rest = gain - high
    middle = lax.reduce_precision(rest, 8, 7)
    return [high, middle, rest - middle]


def global_sum(value, native):
    if not native:
        return lax.psum(value, ("dp", "tp"))
    total = value
    for k in range(1, VDP):
        total = total + lax.ppermute(value, "dp", swap(k))
    out = total
    for k in range(1, VTP):
        out = out + lax.ppermute(total, "tp", shift(VTP, k))
    return out


def adamw(weight, moment_one, moment_two, average, grad_full, factor, learn_rate):
    clipped = grad_full * factor
    first_new = beta_one * moment_one + (1.0 - beta_one) * clipped
    second_new = beta_two * moment_two + (1.0 - beta_two) * clipped * clipped
    step_ratio = (
        first_new
        / (1.0 - beta_one**STEP)
        / (jnp.sqrt(second_new / (1.0 - beta_two**STEP)) + adam_floor)
    )
    weight_new = weight - learn_rate * (step_ratio + weight_decay * weight)
    return (weight_new, first_new, second_new, ema_decay * average + (1.0 - ema_decay) * weight_new)


def local(tokens, cotangent, head_choice, segment_ids, *state):
    weights, firsts, seconds, averages = state[0:7], state[7:14], state[14:21], state[21:28]
    query_w, output_w, up_w, down_w, keyval_w, router_w, gains_w = weights
    size_dp = lax.axis_size("dp")
    size_tp = lax.axis_size("tp")
    token_total = tokens.shape[0] * size_dp * size_tp
    native = (size_dp, size_tp) == (VDP, VTP)
    gain_parts = split_gain(gains_w)
    low_parts = [w.astype(bf16) for w in weights[:6]]

    def small_rows(l, kv, router, gains):
        columns = [g[l, which].astype(bf16)[:, None] for which in range(2) for g in gains]
        block = jnp.concatenate([kv[l], router[l]] + columns, 1)
        return jnp.pad(block, ((0, 0), (0, CA - block.shape[1])))

    pieces_a, pieces_f = [], []
    if native:
        own = jnp.arange(VDP, dtype=jnp.int32) ^ lax.axis_index("dp").astype(jnp.int32)
        line = (lax.axis_index("tp").astype(jnp.int32) - jnp.arange(VTP, dtype=jnp.int32)) % VTP
        for l in range(LAYERS):
            misc = small_rows(l, low_parts[4], low_parts[5], gain_parts)
            pieces_a.append(gather_piece(jnp.concatenate([low_parts[0][l], low_parts[1][l], misc], 0)))
            pieces_f.append(gather_piece(jnp.concatenate([low_parts[2][l], low_parts[3][l]], 0)))
    else:
        own = jnp.arange(VDP, dtype=jnp.int32)
        line = jnp.arange(VTP, dtype=jnp.int32)
        big = [
            lax.all_gather(lax.all_gather(w, "dp", axis=1, tiled=True), "tp", axis=2, tiled=True)
            for w in low_parts[:4]
        ]
        small = [lax.all_gather(w, ("dp", "tp"), axis=1, tiled=True) for w in low_parts[4:6]]
        wide = [lax.all_gather(g, ("dp", "tp"), axis=2, tiled=True) for g in gain_parts]
        for l in range(LAYERS):
            misc = small_rows(l, small[0], small[1], wide)
            pieces_a.append(block_piece([big[0][l], big[1][l]], misc))
            pieces_f.append(block_piece([big[2][l], big[3][l]], None))

    segment = segment_ids.reshape(LEN)
    heads_at = segment[:: SUB]
    first_at = jnp.sum((segment[None, :] < heads_at[:, None]).astype(jnp.int32), 1)
    blocks = jnp.arange(LEN // SUB, dtype=jnp.int32) - first_at // SUB + 1
    idx = jnp.concatenate([own, line, blocks])
    segc = jnp.broadcast_to(segment.astype(f32)[:, None], (LEN, 128))
    segr = jnp.broadcast_to(segment.astype(f32)[None, :], (8, LEN))
    hc = head_choice.astype(f32)

    saved = []
    residual = tokens
    for l in range(LAYERS):
        mid, qs, kv, heads, lse, spread, gate, gsl, gains = attn_forward(
            idx, residual, hc, segc, segr, pieces_a[l]
        )
        saved.append((residual, mid, qs, kv, heads, lse, spread, gate, gsl, gains))
        residual = ffn_forward(idx, mid, gains, pieces_f[l], l == LAYERS - 1)
    layer_out = residual

    upstream = cotangent
    parts = [None] * LAYERS
    for l in reversed(range(LAYERS)):
        residual, mid, qs, kv, heads, lse, spread, gate, gsl, gains = saved[l]
        mid_grad, gain_ffn_grad, keep_f, send_f = ffn_backward(idx, upstream, mid, gains, pieces_f[l])
        gh, dd, gl, keep_o, send_o = output_backward(
            idx, mid_grad, hc, heads, gate, gsl, spread, pieces_a[l]
        )
        upstream, keep_q, send_q = attn_backward(
            idx, mid_grad, residual, hc, segc, segr, qs, gh, kv, lse, dd, gl, gains, gain_ffn_grad, pieces_a[l]
        )
        parts[l] = ((keep_q, send_q), (keep_o, send_o), (keep_f, send_f))

    scale = 1.0 / token_total
    if native:
        done = [[reduce_piece(*piece) for piece in parts[l]] for l in range(LAYERS)]
        sums = [
            jnp.stack([d[0][:RW] for d in done]),
            jnp.stack([d[1] for d in done]),
            jnp.stack([d[2][:RW] for d in done]),
            jnp.stack([d[2][RW:] for d in done]),
            jnp.stack([d[0][RW:, :128] for d in done]),
            jnp.stack([d[0][RW:, 128 : 128 + E] for d in done]),
            jnp.stack([d[0][RW:, 128 + E : 130 + E].T for d in done]),
        ]
    else:
        whole = []
        for l in range(LAYERS):
            grad_q, misc = unblock_piece(*parts[l][0], (RW, RM))
            (grad_o,) = unblock_piece(*parts[l][1], (RW,))
            grad_u, grad_d = unblock_piece(*parts[l][2], (RW, RW))
            whole.append((grad_q, grad_o, grad_u, grad_d, misc))
        sums = []
        for i in range(4):
            grad = jnp.stack([w[i] for w in whole]).astype(f32)
            grad = lax.psum_scatter(grad, "tp", scatter_dimension=2, tiled=True)
            sums.append(lax.psum_scatter(grad, "dp", scatter_dimension=1, tiled=True))
        misc = jnp.stack([w[4] for w in whole]).astype(f32)
        misc = lax.psum_scatter(misc, ("dp", "tp"), scatter_dimension=1, tiled=True)
        sums += [misc[:, :, :128], misc[:, :, 128 : 128 + E], misc[:, :, 128 + E : 130 + E].transpose(0, 2, 1)]
    sums = [s * scale for s in sums]
    squares = jnp.sum(jnp.stack([jnp.sum(s * s) for s in sums]))
    grad_norm = jnp.sqrt(global_sum(squares.reshape(1, 1), native))[0, 0]
    factor = jnp.minimum(1.0, clip_bound / grad_norm)
    outs = [layer_out, upstream, grad_norm]
    for i in range(7):
        outs += adamw(weights[i], firsts[i], seconds[i], averages[i], sums[i], factor, learn_rates[i])
    return tuple(outs)


def solution(mesh):
    token = P(("dp", "tp"), None)
    big = P(None, "dp", "tp")
    small = P(None, ("dp", "tp"), None)
    gain = P(None, None, ("dp", "tp"))
    group = (big, big, big, big, small, small, gain)
    in_specs = (token,) * 4 + group * 4
    out_specs = (token, token, P()) + tuple(spec for spec in group for _ in range(4))
    return jax.shard_map(local, mesh=mesh, in_specs=in_specs, out_specs=out_specs, check_vma=False)
```

```python
import functools

import jax
import jax.numpy as jnp
from jax import lax
from jax.experimental import pallas as pl
from jax.experimental.pallas import tpu as pltpu
from jax.sharding import PartitionSpec as P

E = 24
H = 64
TOPK = 8
LEN = 1024
LAYERS = 2
STEP = 10
D = 512
FF = 2048
EH = E * H
KH = TOPK * H
PAIRS = TOPK // 2
COLS = EH // 128
ROWS = 256
STEPS = LEN // ROWS
SUB = 128
VDP = 8
VTP = 4
RW = D // VDP
CA = EH // VTP
CF = FF // VTP
RM = D // (VDP * VTP)
TA = CA // 128
TF = CF // 128
RQ = TA * RW + 2 * RM
RA = RQ + TA * RW
RF = 2 * TF * RW
REST = 1024
REDUCE = VDP + VTP
BLOCKS = 2 * (VDP + VTP)
VMEM = 60 * 1024 * 1024

epsilon = 1e-06
clip_bound = 0.05
learn_rates = (0.1, 1.0, 0.1, 0.1, 0.1, 0.1, 0.6)
beta_one = 0.9
beta_two = 0.95
adam_floor = 1e-08
weight_decay = 0.1
ema_decay = 0.7
masked_value = -1e30
f32 = jnp.float32
bf16 = jnp.bfloat16


def dot(a, b):
    return lax.dot_general(a, b, (((1,), (0,)), ((), ())), preferred_element_type=f32)


def dot_nt(a, b):
    return lax.dot_general(a, b, (((1,), (1,)), ((), ())), preferred_element_type=f32)


def lanes(rows, dtype=jnp.int32):
    return lax.broadcasted_iota(jnp.int32, (rows, 128), 1).astype(dtype)


def normalize(x):
    factor = lax.rsqrt(jnp.mean(x * x, -1, keepdims=True) + epsilon)
    return x * factor, factor


def both_halves(x, low_half):
    turned = pltpu.roll(x, 64, 1)
    return jnp.where(low_half, x, turned), jnp.where(low_half, turned, x)


def slot_columns(hc):
    rows = hc.shape[0]
    return [jnp.broadcast_to(hc[:, k : k + 1], (rows, 128)).astype(bf16) for k in range(TOPK)]


def pick_heads(full, slots):
    rows = full.shape[0]
    low_half = lanes(rows) < 64
    low_half16 = lanes(rows).astype(bf16) < jnp.asarray(64, bf16)
    pairs = [jnp.where(low_half16, slots[2 * p], slots[2 * p + 1]) for p in range(PAIRS)]
    out = [jnp.zeros((rows, 128), bf16) for _ in range(PAIRS)]
    for c in range(COLS):
        even, odd = both_halves(full[:, c * 128 : (c + 1) * 128], low_half)
        even = even.astype(bf16)
        odd = odd.astype(bf16)
        for p in range(PAIRS):
            out[p] = jnp.where(pairs[p] == jnp.asarray(2 * c, bf16), even, out[p])
            out[p] = jnp.where(pairs[p] == jnp.asarray(2 * c + 1, bf16), odd, out[p])
    return out


def spread_heads(pair_values, slots, store):
    rows = pair_values[0].shape[0]
    low_half = lanes(rows) < 64
    copies = []
    for p in range(PAIRS):
        even, odd = both_halves(pair_values[p], low_half)
        copies += [even.astype(bf16), odd.astype(bf16)]
    half = jnp.where(lanes(rows).astype(bf16) < jnp.asarray(64, bf16), jnp.asarray(0, bf16), jnp.asarray(1, bf16))
    for c in range(COLS):
        expert = half + jnp.asarray(2 * c, bf16)
        total = jnp.zeros((rows, 128), bf16)
        for k in range(TOPK):
            total = jnp.where(slots[k] == expert, copies[k], total)
        store(c, total)


def block_of(refs, spot):
    rows = refs[0].shape[0] // 16
    return refs[spot[0]], spot[1] * rows


def spots(plane_first):
    out = []
    for j in range(VDP):
        for q in range(VTP):
            position = q * 4 + j // 2 if plane_first else (j // 2) * 4 + q
            out.append((j, q, (j % 2, position)))
    return out


def place(refs, scratch, idx, first, tiles, plane_first=False):
    for j, q, spot in spots(plane_first):
        source, base = block_of(refs, spot)
        row = pl.multiple_of(idx[j] * RW, RW)
        for t in range(tiles):
            col = pl.multiple_of(idx[VDP + q] * (tiles * 128) + t * 128, 128)
            start = base + first + t * RW
            scratch[pl.ds(row, RW), pl.ds(col, 128)] = source[start : start + RW, :]


def place_misc(refs, scratch, idx, first):
    for j, q, spot in spots(False):
        source, base = block_of(refs, spot)
        row = pl.multiple_of((idx[j] * VTP + idx[VDP + q]) * RM, RM)
        for t in range(2):
            start = base + first + t * RM
            scratch[pl.ds(row, RM), t * 128 : (t + 1) * 128] = source[start : start + RM, :]


def target_of(targets, j):
    return (targets[0], j) if len(targets) == 1 else (targets[j % 2], j // 2)


def hand_out(targets, grad, idx, first, tiles):
    for j in range(VDP):
        row = pl.multiple_of(idx[REDUCE + j] * RW, RW)
        target, place_at = target_of(targets, j)
        for t in range(tiles):
            start = first + t * RW
            target[place_at, 0, start : start + RW, :] = grad[pl.ds(row, RW), t * 128 : (t + 1) * 128].astype(bf16)


def bias_of(segc, segr_ref, row0, start, width):
    rows = row0 + lax.broadcasted_iota(jnp.int32, (SUB, width), 0)
    cols = start + lax.broadcasted_iota(jnp.int32, (SUB, width), 1)
    same = segc[:, 0:1] == segr_ref[0:1, pl.ds(start, width)]
    return jnp.where((cols <= rows) & same, 0.0, masked_value).astype(f32)


def attn_forward_kernel(idx, x_ref, hc_ref, segc_ref, segr_ref, *rest):
    w_refs, rest = rest[:2], rest[2:]
    (mid_ref, qs_ref, kv_ref, ho_ref, lse_ref, spread_ref, gate_ref, gsl_ref, gains_ref) = rest[:9]
    (wq, wo, misc, gain_s, kt_lo, kt_hi, v_lo, v_hi, qst) = rest[9:]
    step = pl.program_id(0)

    @pl.when(step == 0)
    def _():
        place(w_refs, wq, idx, 0, TA)
        place(w_refs, wo, idx, RQ, TA)
        place_misc(w_refs, misc, idx, TA * RW)
        turned = misc[:, 128:256].astype(f32).T
        gain_s[...] = jnp.zeros_like(gain_s)
        gain_s[0:1, :] = turned[24:25] + turned[25:26] + turned[26:27]
        gain_s[1:2, :] = turned[27:28] + turned[28:29] + turned[29:30]
        gains_ref[...] = gain_s[...]

    x = x_ref[...].astype(f32)
    normed, _ = normalize(x)
    act = (normed * gain_s[0:1, :]).astype(bf16)
    hc = hc_ref[...]
    slots = slot_columns(hc)
    low_half = lanes(ROWS) < 64
    lane = lanes(ROWS)
    small = dot(act, misc[:, 0:256])
    kv = small[:, 0:128].astype(bf16)
    logits = jnp.where(lane < E, small[:, 128:256], masked_value)
    top = jnp.max(logits, -1, keepdims=True)
    lane_f = lane.astype(f32)
    hit = [hc[:, k : k + 1] == lane_f for k in range(TOPK)]
    chosen = hit[0]
    for k in range(1, TOPK):
        chosen = chosen | hit[k]
    powers = jnp.where(chosen, jnp.exp(logits - top), 0.0)
    gate = powers / jnp.sum(powers, -1, keepdims=True)
    gate_ref[...] = gate
    gate_low = gate.astype(bf16).astype(f32)
    gates = [jnp.sum(jnp.where(hit[k], gate_low, 0.0), -1, keepdims=True) for k in range(TOPK)]
    compact = jnp.zeros((ROWS, 128), f32)
    for p in range(PAIRS):
        compact = jnp.where(lane == p, gates[2 * p], compact)
        compact = jnp.where(lane == 64 + p, gates[2 * p + 1], compact)
    gsl_ref[...] = compact
    kv_ref[...] = kv
    row = pl.multiple_of(step * ROWS, ROWS)
    kv_f = kv.astype(f32)
    k_lo = jnp.where(low_half, kv_f, 0.0)
    k_hi = pltpu.roll(k_lo, 64, 1)
    val_hi = jnp.where(low_half, 0.0, kv_f)
    val_lo = pltpu.roll(val_hi, 64, 1)
    kt_lo[:, pl.ds(row, ROWS)] = k_lo.T.astype(bf16)
    kt_hi[:, pl.ds(row, ROWS)] = k_hi.T.astype(bf16)
    ones = jnp.where(low_half, 1.0, 0.0)
    v_lo[pl.ds(row, ROWS), 0:128] = val_lo.astype(bf16)
    v_lo[pl.ds(row, ROWS), 128:256] = ones.astype(bf16)
    v_hi[pl.ds(row, ROWS), 0:128] = val_hi.astype(bf16)
    v_hi[pl.ds(row, ROWS), 128:256] = (1.0 - ones).astype(bf16)
    queries = dot(act, wq[...])
    picked = pick_heads(queries, slots)
    for p in range(PAIRS):
        scaled = picked[p] * jnp.asarray(H ** (-0.5), bf16)
        qs_ref[:, p * 128 : (p + 1) * 128] = scaled
        for s in range(ROWS // SUB):
            qst[s, p * SUB : (p + 1) * SUB, :] = scaled[s * SUB : (s + 1) * SUB]

    for s in range(ROWS // SUB):
        block = step * (ROWS // SUB) + s
        count = idx[BLOCKS + block]
        rows = slice(s * SUB, (s + 1) * SUB)

        def attend(n, s=s, block=block, rows=rows):
            width = n * SUB
            start = pl.multiple_of((block + 1 - n) * SUB, SUB)
            bias = bias_of(segc_ref[rows, :], segr_ref, block * SUB, start, width)
            q4 = qst[s]
            parts = []
            tops = []
            for kt in (kt_lo, kt_hi):
                scores = dot(q4, kt[:, pl.ds(start, width)]).reshape(PAIRS, SUB, width) + bias[None]
                peak = jnp.max(scores, -1, keepdims=True)
                parts.append(jnp.exp(scores - peak).astype(bf16).reshape(PAIRS * SUB, width))
                tops.append(peak.reshape(PAIRS * SUB, 1))
            result = dot(parts[0], v_lo[pl.ds(start, width), :]) + dot(parts[1], v_hi[pl.ds(start, width), :])
            total = result[:, 128:256]
            heads = result[:, 0:128] / total
            log_sum = jnp.where(lanes(PAIRS * SUB) < 64, tops[0], tops[1]) + jnp.log(total)
            keep = jnp.zeros((SUB, 128), f32)
            for p in range(PAIRS):
                one = slice(p * SUB, (p + 1) * SUB)
                ho_ref[rows, p * 128 : (p + 1) * 128] = heads[one]
                keep = jnp.where((lanes(SUB) & 63) == p, log_sum[one], keep)
            lse_ref[rows, :] = keep

        for n in range(1, 6):
            pl.when(count == n)(functools.partial(attend, n))

    mixed = []
    for p in range(PAIRS):
        gate_pair = jnp.where(low_half, gates[2 * p], gates[2 * p + 1])
        mixed.append(gate_pair * ho_ref[:, p * 128 : (p + 1) * 128])

    def store(c, value):
        spread_ref[:, c * 128 : (c + 1) * 128] = value

    spread_heads(mixed, slots, store)
    mid_ref[...] = x + dot_nt(spread_ref[...], wo[...])


def ffn_forward_kernel(plane_first, idx, x_ref, gains_ref, *rest):
    w_refs, rest = rest[:2], rest[2:]
    out_ref = rest[0]
    wu, wd = rest[1:]

    @pl.when(pl.program_id(0) == 0)
    def _():
        place(w_refs, wu, idx, 0, TF, plane_first)
        place(w_refs, wd, idx, TF * RW, TF, plane_first)

    x = x_ref[...]
    normed, _ = normalize(x)
    act = (normed * gains_ref[1:2, :]).astype(bf16)
    pre = dot(act, wu[...])
    hidden = jax.nn.gelu(pre, approximate=True).astype(bf16)
    out_ref[...] = (x + dot_nt(hidden, wd[...])).astype(out_ref.dtype)


def ffn_backward_kernel(plane_first, idx, up_ref, x_ref, gains_ref, *rest):
    w_refs, rest = rest[:2], rest[2:]
    mid_ref, gain_ref = rest[:2]
    targets = rest[2:-7]
    wu, wd, hid_s, gp_s, grad_t, act_t, part = rest[-7:]
    step = pl.program_id(0)

    @pl.when(step == 0)
    def _():
        place(w_refs, wu, idx, 0, TF, plane_first)
        place(w_refs, wd, idx, TF * RW, TF, plane_first)
        gain_ref[...] = jnp.zeros_like(gain_ref)

    @pl.when(step < STEPS)
    def _():
        row = pl.multiple_of(step * ROWS, ROWS)
        up = up_ref[...].astype(f32)
        gain = gains_ref[1:2, :]
        normed, factor = normalize(x_ref[...])
        act_f = normed * gain
        act = act_f.astype(bf16)
        act_t[:, pl.ds(row, ROWS)] = act_f.T.astype(bf16)
        grad_t[:, pl.ds(row, ROWS)] = up.T.astype(bf16)
        pre = dot(act, wu[...])
        grad_hidden = dot(up.astype(bf16), wd[...])
        square = pre * pre
        arg = 0.7978845608028654 * pre * (1.0 + 0.044715 * square)
        bend = jnp.tanh(arg)
        half = 0.5 * (1.0 + bend)
        hid_s[pl.ds(row, ROWS), :] = (pre * half).astype(bf16)
        slope = half + (0.5 * 0.7978845608028654) * pre * (1.0 - bend * bend) * (
            1.0 + 3.0 * 0.044715 * square
        )
        grad_pre = (grad_hidden * slope).astype(bf16)
        gp_s[pl.ds(row, ROWS), :] = grad_pre
        grad_act = dot_nt(grad_pre, wu[...])
        scaled = grad_act * gain
        inner = jnp.mean(scaled * normed, -1, keepdims=True)
        mid_ref[...] = up + factor * (scaled - normed * inner)
        gain_ref[0:1, :] += jnp.sum(grad_act * normed, 0, keepdims=True)

    @pl.when(step >= STEPS)
    def _():
        q = step - STEPS
        col = pl.multiple_of(idx[REDUCE + VDP + q] * CF, CF)
        part[...] = dot(act_t[...], gp_s[:, pl.ds(col, CF)])
        hand_out(targets, part, idx, 0, TF)
        part[...] = dot(grad_t[...], hid_s[:, pl.ds(col, CF)])
        hand_out(targets, part, idx, TF * RW, TF)


def output_backward_kernel(idx, mid_ref, hc_ref, ho_ref, gate_ref, gsl_ref, spread_ref, *rest):
    w_refs, rest = rest[:2], rest[2:]
    gh_ref, dd_ref, gl_ref = rest[:3]
    targets = rest[3:-3]
    wo, grad_t, part = rest[-3:]
    step = pl.program_id(0)

    @pl.when(step == 0)
    def _():
        place(w_refs, wo, idx, RQ, TA)

    @pl.when(step < STEPS)
    def _():
        row = pl.multiple_of(step * ROWS, ROWS)
        mid = mid_ref[...]
        grad_t[:, pl.ds(row, ROWS)] = mid.T.astype(bf16)
        full = dot(mid.astype(bf16), wo[...])
        hc = hc_ref[...]
        slots = slot_columns(hc)
        mixed = pick_heads(full, slots)
        lane = lanes(ROWS)
        low_half = lane < 64
        lane_f = lane.astype(f32)
        gsl = gsl_ref[...]
        inner = jnp.zeros((ROWS, 128), f32)
        grad_gates = jnp.zeros((ROWS, 128), f32)
        for p in range(PAIRS):
            value = mixed[p].astype(f32)
            ga = gsl[:, p : p + 1]
            gb = gsl[:, 64 + p : 65 + p]
            gh_ref[:, p * 128 : (p + 1) * 128] = (jnp.where(low_half, ga, gb) * value).astype(bf16)
            product = value * ho_ref[:, p * 128 : (p + 1) * 128]
            sum_a = jnp.sum(jnp.where(low_half, product, 0.0), -1, keepdims=True)
            sum_b = jnp.sum(jnp.where(low_half, 0.0, product), -1, keepdims=True)
            inner = jnp.where(lane == p, ga * sum_a, inner)
            inner = jnp.where(lane == 64 + p, gb * sum_b, inner)
            grad_gates = jnp.where(hc[:, 2 * p : 2 * p + 1] == lane_f, sum_a, grad_gates)
            grad_gates = jnp.where(hc[:, 2 * p + 1 : 2 * p + 2] == lane_f, sum_b, grad_gates)
        dd_ref[...] = inner
        gate = gate_ref[...]
        total = jnp.sum(gate * grad_gates, -1, keepdims=True)
        gl_ref[...] = (gate * (grad_gates - total)).astype(bf16)

    @pl.when(step >= STEPS)
    def _():
        q = step - STEPS
        col = pl.multiple_of(idx[REDUCE + VDP + q] * CA, 128)
        part[...] = dot(grad_t[...], spread_ref[:, pl.ds(col, CA)])
        hand_out(targets, part, idx, 0, TA)


def attn_backward_kernel(
    idx, mid_ref, x_ref, hc_ref, segc_ref, segr_ref, qs_ref, gh_ref, kv_ref, lse_ref, dd_ref, gl_ref, gains_ref, gfg_ref, *rest
):
    w_refs, rest = rest[:2], rest[2:]
    out_ref = rest[0]
    targets, rest = rest[1:-18], rest[-18:]
    (wq, misc, kt_lo, kt_hi, vt_lo, vt_hi, k_lo, k_hi, dkv_t, qst, gst, dq_s, gq_s, act_t) = rest[:14]
    (dkv_s, gain_s, part, pmisc) = rest[14:]
    step = pl.program_id(0)

    @pl.when(step == 0)
    def _():
        place(w_refs, wq, idx, 0, TA)
        place_misc(w_refs, misc, idx, TA * RW)
        low = lanes(LEN) < 64
        kv = kv_ref[...].astype(f32)
        one = jnp.where(low, kv, 0.0)
        two = pltpu.roll(one, 64, 1)
        k_lo[...] = one.astype(bf16)
        k_hi[...] = two.astype(bf16)
        kt_lo[...] = one.T.astype(bf16)
        kt_hi[...] = two.T.astype(bf16)
        one = jnp.where(low, 0.0, kv)
        vt_hi[...] = one.T.astype(bf16)
        vt_lo[...] = pltpu.roll(one, 64, 1).T.astype(bf16)
        dkv_t[...] = jnp.zeros_like(dkv_t)
        gain_s[...] = jnp.zeros_like(gain_s)

    @pl.when(step < STEPS)
    def _():
        row = pl.multiple_of(step * ROWS, ROWS)
        for p in range(PAIRS):
            for s in range(ROWS // SUB):
                qst[s, p * SUB : (p + 1) * SUB, :] = qs_ref[s * SUB : (s + 1) * SUB, p * 128 : (p + 1) * 128]
                gst[s, p * SUB : (p + 1) * SUB, :] = gh_ref[s * SUB : (s + 1) * SUB, p * 128 : (p + 1) * 128]
        for s in range(ROWS // SUB):
            block = step * (ROWS // SUB) + s
            count = idx[BLOCKS + block]
            rows = slice(s * SUB, (s + 1) * SUB)

            def attend(n, s=s, block=block, rows=rows):
                width = n * SUB
                start = pl.multiple_of((block + 1 - n) * SUB, SUB)
                win = pl.ds(start, width)
                bias = bias_of(segc_ref[rows, :], segr_ref, block * SUB, start, width)
                q4 = qst[s]
                g4 = gst[s]
                q4t = q4.astype(f32).T.astype(bf16)
                g4t = g4.astype(f32).T.astype(bf16)
                lse = lse_ref[rows, :]
                dd = dd_ref[rows, :]
                dq = None
                dk = None
                dv = None
                for half, (kt, vt, kk) in enumerate(((kt_lo, vt_lo, k_lo), (kt_hi, vt_hi, k_hi))):
                    off = 64 * half
                    log_sum = jnp.stack([lse[:, off + p : off + p + 1] for p in range(PAIRS)])
                    inner = jnp.stack([dd[:, off + p : off + p + 1] for p in range(PAIRS)])
                    scores = dot(q4, kt[:, win]).reshape(PAIRS, SUB, width)
                    prob = jnp.exp(scores + bias[None] - log_sum)
                    dprob = dot(g4, vt[:, win]).reshape(PAIRS, SUB, width)
                    dscore = (prob * (dprob - inner)).astype(bf16).reshape(PAIRS * SUB, width)
                    low_prob = prob.astype(bf16).reshape(PAIRS * SUB, width)
                    a = dot(dscore, kk[win, :])
                    b = dot(q4t[off : off + 64], dscore)
                    c = dot(g4t[off : off + 64], low_prob)
                    dq = a if dq is None else dq + a
                    dk = b if dk is None else dk + b
                    dv = c if dv is None else dv + c
                dkv_t[0:64, win] += dk
                dkv_t[64:128, win] += dv
                dq = dq * (H ** (-0.5))
                for p in range(PAIRS):
                    dq_s[rows, p * 128 : (p + 1) * 128] = dq[p * SUB : (p + 1) * SUB]

            for n in range(1, 6):
                pl.when(count == n)(functools.partial(attend, n))

        slots = slot_columns(hc_ref[...])

        def store(c, value):
            gq_s[pl.ds(row, ROWS), c * 128 : (c + 1) * 128] = value

        spread_heads([dq_s[:, p * 128 : (p + 1) * 128] for p in range(PAIRS)], slots, store)

    @pl.when(step == STEPS)
    def _():
        dkv_s[...] = dkv_t[...].T.astype(bf16)

    @pl.when((step >= STEPS) & (step < 2 * STEPS))
    def _():
        row = pl.multiple_of((step - STEPS) * ROWS, ROWS)
        here = pl.ds(row, ROWS)
        gain = gains_ref[0:1, :]
        normed, factor = normalize(x_ref[...].astype(f32))
        act_t[:, here] = (normed * gain).T.astype(bf16)
        grad_act = dot_nt(gq_s[here, :], wq[...])
        grad_act += dot_nt(dkv_s[here, :], misc[:, 0:128])
        router = jnp.where(lanes(D) < E, misc[:, 128:256].astype(f32), 0.0).astype(bf16)
        grad_act += dot_nt(gl_ref[here, :], router)
        scaled = grad_act * gain
        inner = jnp.mean(scaled * normed, -1, keepdims=True)
        out_ref[...] = mid_ref[...] + factor * (scaled - normed * inner)
        gain_s[0:1, :] += jnp.sum(grad_act * normed, 0, keepdims=True)

    @pl.when(step == 2 * STEPS)
    def _():
        pmisc[:, 0:128] = dot(act_t[...], dkv_s[...])
        router = dot(act_t[...], gl_ref[...])
        gain_s[1:2, :] = gfg_ref[0:1, :]
        turned = gain_s[...].T
        lane = lanes(D)
        router = jnp.where(lane < E, router, 0.0)
        router = jnp.where(lane == E, turned[:, 0:1], router)
        router = jnp.where(lane == E + 1, turned[:, 1:2], router)
        pmisc[:, 128:256] = router

    @pl.when(step >= 2 * STEPS)
    def _():
        q = step - 2 * STEPS
        col = pl.multiple_of(idx[REDUCE + VDP + q] * CA, 128)
        part[...] = dot(act_t[...], gq_s[:, pl.ds(col, CA)])
        hand_out(targets, part, idx, 0, TA)
        for j in range(VDP):
            row = pl.multiple_of((idx[REDUCE + j] * VTP + idx[REDUCE + VDP + q]) * RM, RM)
            target, place_at = target_of(targets, j)
            for t in range(2):
                start = TA * RW + t * RM
                target[place_at, 0, start : start + RM, :] = pmisc[
                    pl.ds(row, RM), t * 128 : (t + 1) * 128
                ].astype(bf16)


def pack_attn(out, base, query, output, keyval, router, columns, layer):
    for t in range(TA):
        cut = slice(t * 128, (t + 1) * 128)
        out[base + t * RW : base + (t + 1) * RW, :] = query[layer, :, cut].astype(bf16)
        start = base + RQ + t * RW
        out[start : start + RW, :] = output[layer, :, cut].astype(bf16)
    start = base + TA * RW
    out[start : start + RM, :] = keyval[layer].astype(bf16)
    misc = slice(start + RM, start + 2 * RM)
    lane = lanes(RM)
    block = jnp.zeros((RM, 128), f32)
    gains = columns[layer]
    for which in range(2):
        part = gains[:, which : which + 1]
        for i in range(3):
            high = part.astype(bf16).astype(f32)
            block = jnp.where(lane == E + 3 * which + i, high, block)
            part = part - high
    out[misc, :] = block.astype(bf16)
    out[misc, 0:E] = router[layer].astype(bf16)


def pack_ffn(out, base, up, down, layer):
    for t in range(TF):
        cut = slice(t * 128, (t + 1) * 128)
        out[base + t * RW : base + (t + 1) * RW, :] = up[layer, :, cut].astype(bf16)
        start = base + (TF + t) * RW
        out[start : start + RW, :] = down[layer, :, cut].astype(bf16)


def pack_first_kernel(query, output, keyval, router, columns, out):
    pack_attn(out, 0, query, output, keyval, router, columns, 0)


def pack_other_kernel(query, output, keyval, router, columns, up, down, rest, last):
    pack_ffn(rest, 0, up, down, 0)
    pack_attn(rest, RF, query, output, keyval, router, columns, 1)
    rest[RF + RA :, :] = jnp.zeros((REST - RF - RA, 128), bf16)
    pack_ffn(last, 0, up, down, 1)


def sum_kernel(scale, parts, total, square):
    value = parts[0].astype(f32)
    for k in range(1, VTP):
        value = value + parts[k].astype(f32)
    value = value * scale
    total[...] = value
    rows = value.shape[0]
    square[...] = jnp.sum((value * value).reshape(rows // 8, 8, 128), 0)


def update_kernel(square, query0, rest, last, *refs):
    state, norm_ref, outs = refs[:28], refs[28], refs[29:]
    norm = jnp.sqrt(jnp.sum(jnp.sum(square[...], 0, keepdims=True), 1, keepdims=True))
    norm_ref[...] = norm
    factor = jnp.minimum(1.0, clip_bound / norm)

    def step(i, at, grad):
        result = adamw(
            state[i][at], state[7 + i][at], state[14 + i][at], state[21 + i][at], grad, factor, learn_rates[i]
        )
        for k in range(4):
            outs[4 * i + k][at] = result[k]

    def tile(i, layer, t, ref, start):
        step(i, (layer, slice(None), slice(t * 128, (t + 1) * 128)), ref[start : start + RW, :])

    for t in range(TA):
        tile(0, 0, t, query0, t * RW)
        tile(0, 1, t, rest, t * RW)
        tile(1, 0, t, rest, RA + RF + t * RW)
        tile(1, 1, t, rest, RQ + t * RW)
    for t in range(TF):
        tile(2, 0, t, rest, RA + t * RW)
        tile(3, 0, t, rest, RA + (TF + t) * RW)
        tile(2, 1, t, last, t * RW)
        tile(3, 1, t, last, (TF + t) * RW)
    for layer, ref in ((0, query0), (1, rest)):
        start = TA * RW
        step(4, (layer,), ref[start : start + RM, :])
        block = ref[start + RM : start + 2 * RM, :]
        step(5, (layer,), block[:, 0:E])
        step(6, (layer,), block.T[E : E + 2, :])


def whole_call(kernel, out_shapes, name, *args):
    return pl.pallas_call(
        kernel,
        in_specs=[pl.BlockSpec(memory_space=pltpu.VMEM)] * len(args),
        out_specs=[pl.BlockSpec(memory_space=pltpu.VMEM)] * len(out_shapes),
        out_shape=[jax.ShapeDtypeStruct(shape, kind) for shape, kind in out_shapes],
        compiler_params=pltpu.CompilerParams(vmem_limit_bytes=VMEM),
        name=name,
    )(*args)


def sum_parts(parts, scale):
    rows = parts.shape[1]
    return whole_call(
        functools.partial(sum_kernel, scale), [((rows, 128), f32), ((8, 128), f32)], "sum_parts", parts
    )


def rows_spec(width, phase=0, single=False):
    def index(i, idx):
        return (jnp.clip(i - phase * STEPS, 0, STEPS - 1), 0)

    return pl.BlockSpec((ROWS, width), index)


def full_spec(shape):
    zeros = (0,) * len(shape)
    return pl.BlockSpec(shape, lambda i, idx: zeros, pipeline_mode=pl.Buffered(1))


def kept_spec(shape):
    zeros = (0,) * len(shape)
    return pl.BlockSpec(shape, lambda i, idx: zeros)


def parts_specs(rows, phase, split):
    def index(i, idx):
        return (0, jnp.maximum(i - phase * STEPS, 0), 0, 0)

    count = VDP // 2 if split else VDP
    return [pl.BlockSpec((count, 1, rows, 128), index)] * (VDP // count)


def parts_shapes(rows, split):
    count = VDP // 2 if split else VDP
    return [((count, VTP, rows, 128), bf16)] * (VDP // count)


def call(kernel, steps, in_specs, out_specs, out_shapes, scratch, name, flops, moved):
    return pl.pallas_call(
        kernel,
        grid_spec=pltpu.PrefetchScalarGridSpec(
            num_scalar_prefetch=1,
            grid=(steps,),
            in_specs=in_specs,
            out_specs=out_specs,
            scratch_shapes=scratch,
        ),
        out_shape=[jax.ShapeDtypeStruct(s, d) for s, d in out_shapes],
        compiler_params=pltpu.CompilerParams(
            dimension_semantics=("arbitrary",), vmem_limit_bytes=VMEM
        ),
        cost_estimate=pl.CostEstimate(flops=flops, bytes_accessed=moved, transcendentals=0),
        name=name,
    )


def vm(*shape, dtype=bf16):
    return pltpu.VMEM(shape, dtype)


def attn_forward(idx, x, hc, segc, segr, weights):
    return call(
        attn_forward_kernel,
        STEPS,
        [rows_spec(D), rows_spec(TOPK), rows_spec(128), full_spec((8, LEN))]
        + [full_spec((16 * RA, 128))] * 2,
        [
            rows_spec(D), rows_spec(KH), rows_spec(128), rows_spec(KH), rows_spec(128),
            rows_spec(EH), rows_spec(128), rows_spec(128), kept_spec((8, D)),
        ],
        [
            ((LEN, D), f32), ((LEN, KH), bf16), ((LEN, 128), bf16), ((LEN, KH), f32), ((LEN, 128), f32),
            ((LEN, EH), bf16), ((LEN, 128), f32), ((LEN, 128), f32), ((8, D), f32),
        ],
        [
            vm(D, EH), vm(D, EH), vm(D, 256), vm(8, D, dtype=f32), vm(128, LEN), vm(128, LEN),
            vm(LEN, 256), vm(LEN, 256), vm(ROWS // SUB, PAIRS * SUB, 128),
        ],
        "attn_forward", 8 * 10**9, 14 * 10**6,
    )(idx, x, hc, segc, segr, *weights)


def ffn_forward(idx, x, gains, weights, last, plane_first):
    return call(
        functools.partial(ffn_forward_kernel, plane_first),
        STEPS,
        [rows_spec(D), full_spec((8, D))] + [full_spec((16 * RF, 128))] * 2,
        [rows_spec(D)],
        [((LEN, D), bf16 if last else f32)],
        [vm(D, FF), vm(D, FF)],
        "ffn_forward", 5 * 10**9, 8 * 10**6,
    )(idx, x, gains, *weights)[0]


def ffn_backward(idx, upstream, x, gains, weights, plane_first, split):
    return call(
        functools.partial(ffn_backward_kernel, plane_first),
        2 * STEPS,
        [rows_spec(D), rows_spec(D), full_spec((8, D))] + [full_spec((16 * RF, 128))] * 2,
        [rows_spec(D), kept_spec((8, D))] + parts_specs(RF, 1, split),
        [
            ((LEN, D), f32), ((8, D), f32),
        ]
        + parts_shapes(RF, split),
        [
            vm(D, FF), vm(D, FF), vm(LEN, FF), vm(LEN, FF), vm(D, LEN), vm(D, LEN), vm(D, CF, dtype=f32),
        ],
        "ffn_backward", 13 * 10**9, 14 * 10**6,
    )(idx, upstream, x, gains, *weights)


def output_backward(idx, mid, hc, heads, gate, gsl, spread, weights, split):
    return call(
        output_backward_kernel,
        2 * STEPS,
        [rows_spec(D), rows_spec(TOPK), rows_spec(KH), rows_spec(128), rows_spec(128), full_spec((LEN, EH))]
        + [full_spec((16 * RA, 128))] * 2,
        [rows_spec(KH), rows_spec(128), rows_spec(128)] + parts_specs(TA * RW, 1, split),
        [
            ((LEN, KH), bf16), ((LEN, 128), f32), ((LEN, 128), bf16),
        ]
        + parts_shapes(TA * RW, split),
        [vm(D, EH), vm(D, LEN), vm(D, CA, dtype=f32)],
        "output_backward", 5 * 10**9, 16 * 10**6,
    )(idx, mid, hc, heads, gate, gsl, spread, *weights)


def attn_backward(idx, mid, x, hc, segc, segr, qs, gh, kv, lse, dd, gl, gains, gfg, weights, split):
    return call(
        attn_backward_kernel,
        3 * STEPS,
        [
            rows_spec(D, 1), rows_spec(D, 1), rows_spec(TOPK), rows_spec(128), full_spec((8, LEN)),
            rows_spec(KH), rows_spec(KH), full_spec((LEN, 128)), rows_spec(128), rows_spec(128),
            full_spec((LEN, 128)), full_spec((8, D)), full_spec((8, D)),
        ]
        + [full_spec((16 * RA, 128))] * 2,
        [rows_spec(D, 1)] + parts_specs(RQ, 2, split),
        [((LEN, D), f32)] + parts_shapes(RQ, split),
        [
            vm(D, EH), vm(D, 256), vm(128, LEN), vm(128, LEN), vm(128, LEN), vm(128, LEN),
            vm(LEN, 128), vm(LEN, 128), vm(128, LEN, dtype=f32), vm(ROWS // SUB, PAIRS * SUB, 128),
            vm(ROWS // SUB, PAIRS * SUB, 128), vm(ROWS, KH, dtype=f32), vm(LEN, EH), vm(D, LEN),
            vm(LEN, 128), vm(8, D, dtype=f32), vm(D, CA, dtype=f32), vm(D, 256, dtype=f32),
        ],
        "attn_backward", 10 * 10**9, 16 * 10**6,
    )(idx, mid, x, hc, segc, segr, qs, gh, kv, lse, dd, gl, gains, gfg, *weights)


def swap(k):
    return [(i, i ^ k) for i in range(VDP)]


def plane_moves(block):
    return [block] + [lax.ppermute(block, "dp", swap(2 * k)) for k in range(1, 4)]


def core_move(block):
    return [block, lax.ppermute(block, "dp", swap(1))]


def stacked(blocks):
    return jnp.concatenate(blocks, 0)


def tiled(block):
    return jnp.concatenate([block[:, t : t + 128] for t in range(0, block.shape[1], 128)], 0)


def after(value, *others):
    flat, tree = jax.tree.flatten((value, others))
    return jax.tree.unflatten(tree, lax.optimization_barrier(flat))[0]


def reduce_core(keep, send):
    return keep, lax.ppermute(send, "dp", swap(1))


def reduce_plane(keep, got):
    pair = [(keep[k].astype(f32) + got[k].astype(f32)).astype(bf16) for k in range(4)]
    return pair[:1] + [lax.ppermute(pair[k], "dp", swap(2 * k)) for k in range(1, 4)]


def plane_sum(parts):
    total = parts[0].astype(f32)
    for part in parts[1:]:
        total = total + part.astype(f32)
    return total.astype(bf16)


def line_swap(parts):
    return lax.all_to_all(parts, "tp", 0, 0)


def block_piece(block, plane_first):
    order = sorted(spots(plane_first), key=lambda entry: entry[2])
    made = [block(j, q) for j, q, _ in order]
    return [jnp.concatenate(made[:16], 0), jnp.concatenate(made[16:], 0)]


def unblock_matrix(both, rows):
    tiles = both.shape[2] // rows
    return both.reshape(VDP, VTP, tiles, rows, 128).transpose(0, 3, 1, 2, 4).reshape(D, VTP * tiles * 128)


def split_gain(gain):
    high = lax.reduce_precision(gain, 8, 7)
    rest = gain - high
    middle = lax.reduce_precision(rest, 8, 7)
    return [high, middle, rest - middle]


def global_sum(value):
    for k in (1, 2, 4):
        value = value + lax.ppermute(value, "dp", swap(k))
    for k in (1, 2):
        value = value + lax.ppermute(value, "tp", [(i, i ^ k) for i in range(VTP)])
    return value


def adamw(weight, moment_one, moment_two, average, grad_full, factor, learn_rate):
    clipped = grad_full * factor
    first_new = beta_one * moment_one + (1.0 - beta_one) * clipped
    second_new = beta_two * moment_two + (1.0 - beta_two) * clipped * clipped
    step_ratio = (
        first_new
        / (1.0 - beta_one**STEP)
        / (jnp.sqrt(second_new / (1.0 - beta_two**STEP)) + adam_floor)
    )
    weight_new = weight - learn_rate * (step_ratio + weight_decay * weight)
    return (weight_new, first_new, second_new, ema_decay * average + (1.0 - ema_decay) * weight_new)


def local(tokens, cotangent, head_choice, segment_ids, *state):
    weights, firsts, seconds, averages = state[0:7], state[7:14], state[14:21], state[21:28]
    query_w, output_w, up_w, down_w, keyval_w, router_w, gains_w = weights
    size_dp = lax.axis_size("dp")
    size_tp = lax.axis_size("tp")
    token_total = tokens.shape[0] * size_dp * size_tp
    native = (size_dp, size_tp) == (VDP, VTP)
    scale = 1.0 / token_total

    steady = jnp.arange(VDP + VTP, dtype=jnp.int32)
    steady = jnp.where(steady < VDP, steady, steady - VDP)
    if native:
        own = jnp.arange(VDP, dtype=jnp.int32) ^ lax.axis_index("dp").astype(jnp.int32)
        gathers = jnp.concatenate([own, steady[VDP:]])
        reduces = [gathers, steady]
    else:
        gathers = steady
        reduces = [steady, steady]
    segment = segment_ids.reshape(LEN)
    heads_at = segment[:: SUB]
    first_at = jnp.sum((segment[None, :] < heads_at[:, None]).astype(jnp.int32), 1)
    blocks = jnp.arange(LEN // SUB, dtype=jnp.int32) - first_at // SUB + 1
    tables = [jnp.concatenate([gathers, r, blocks]) for r in reduces]
    segc = jnp.broadcast_to(segment.astype(f32)[:, None], (LEN, 128))
    segr = jnp.broadcast_to(segment.astype(f32)[None, :], (8, LEN))
    hc = head_choice.astype(f32)

    def split(l):
        return native and l == 0

    def run_attn_forward(l, x, a):
        saved[l] = (x,) + tuple(attn_forward(tables[l], x, hc, segc, segr, a))

    def run_ffn_forward(l, f):
        return ffn_forward(tables[l], saved[l][1], saved[l][9], f, l == LAYERS - 1, l == LAYERS - 1)

    def run_ffn_backward(l, upstream, f):
        return ffn_backward(
            tables[l], upstream, saved[l][1], saved[l][9], f, l == LAYERS - 1, split(l)
        )

    def run_output_backward(l, mid_grad, a):
        _, _, _, _, heads, _, spread, gate, gsl, _ = saved[l]
        return output_backward(tables[l], mid_grad, hc, heads, gate, gsl, spread, a, split(l))

    def run_attn_backward(l, mid_grad, gh, dd, gl, gain_ffn_grad, a):
        x, _, qs, kv, _, lse, _, _, _, gains = saved[l]
        return attn_backward(
            tables[l], mid_grad, x, hc, segc, segr, qs, gh, kv, lse, dd, gl, gains, gain_ffn_grad, a, split(l)
        )

    saved = [None] * LAYERS
    if native:
        columns = gains_w.transpose(0, 2, 1)
        small = (query_w, output_w, keyval_w, router_w, columns)
        (first,) = whole_call(pack_first_kernel, [((RA, 128), bf16)], "pack_first", *small)
        a0 = lax.all_gather(first, "tp", tiled=True)
        rest, f1 = whole_call(
            pack_other_kernel, [((REST, 128), bf16), ((RF, 128), bf16)], "pack_other",
            *small, up_w, after(down_w, first),
        )
        rest, f1 = after((rest, f1), a0)
        a0 = plane_moves(a0)
        rest = lax.all_gather(rest, "tp")
        a0, f1 = after((a0, f1), a0)
        a0 = core_move(stacked(a0))
        f1 = plane_moves(f1)
        rest, f1 = after((rest, f1), rest, f1)
        f0 = plane_moves(rest[:, :RF].reshape(VTP * RF, 128))
        f1 = lax.all_gather(stacked(f1), "tp", tiled=True)
        run_attn_forward(0, after(tokens, rest), a0)
        saved[0], f0, rest = after((saved[0], f0, rest), saved[0][1], f0)
        f0 = core_move(stacked(f0))
        a1 = plane_moves(rest[:, RF : RF + RA].reshape(VTP * RA, 128))
        residual = run_ffn_forward(0, f0)
        residual, a1, f1 = after((residual, a1, f1), residual, a1, f1)
        a1 = core_move(stacked(a1))
        f1 = core_move(f1)
        run_attn_forward(1, residual, a1)
        mid_grad, gain_grad, rf1 = run_ffn_backward(1, cotangent, after(f1, saved[1][1]))
        rf1 = lax.psum_scatter(rf1, "dp")
        gh, dd, gl, ro1 = run_output_backward(1, mid_grad, a1)
        upstream, rq1 = run_attn_backward(1, mid_grad, gh, dd, gl, gain_grad, a1)
        ra1 = lax.psum_scatter(jnp.concatenate([rq1, ro1], 2), "dp")
        mid_grad, gain_grad, keep, send = run_ffn_backward(0, upstream, f0)
        rf0 = reduce_core(keep, send)
        mid_grad, rf1 = after((mid_grad, rf1), mid_grad, rf1)
        gh, dd, gl, keep, send = run_output_backward(0, mid_grad, a0)
        ro0 = reduce_core(keep, send)
        gh, rf0, ro0, rf1 = after((gh, rf0, ro0, rf1), gh, rf0, ro0, rf1)
        rf1 = line_swap(rf1)
        rfo = reduce_plane(*[jnp.concatenate([x, y], 2) for x, y in zip(rf0, ro0)])
        upstream, keep, send = run_attn_backward(0, mid_grad, gh, dd, gl, gain_grad, a0)
        upstream, keep, send, rfo, ra1, rf1 = after(
            (upstream, keep, send, rfo, ra1, rf1), upstream, rfo, ra1, rf1
        )
        rq0 = reduce_core(keep, send)
        rest = jnp.concatenate([ra1, plane_sum(rfo)], 1)
        saved[1], rq0, rest = after((saved[1], rq0, rest), upstream, rq0, rest)
        rq0 = reduce_plane(*rq0)
        rest = line_swap(rest)
        layer_out = run_ffn_forward(1, f1)
        layer_out, rq0, rest = after((layer_out, rq0, rest), layer_out, rq0)
        rf1, square_a = sum_parts(rf1, scale)
        rest, square_b = sum_parts(rest, scale)
        rq0, square_c = sum_parts(line_swap(plane_sum(rq0)), scale)
        square = global_sum(square_a + square_b + square_c)
        shapes = [((1, 1), f32)] + [(w.shape, f32) for w in weights for _ in range(4)]
        updates = whole_call(update_kernel, shapes, "update", square, rq0, rest, rf1, *state)
        return (layer_out, upstream, updates[0][0, 0]) + tuple(updates[1:])
    else:
        gain_parts = split_gain(gains_w)
        low_parts = [w.astype(bf16) for w in weights[:6]]

        def small_block(kv, router, gains):
            block = jnp.concatenate([kv, router] + [g[:, None] for g in gains], 1)
            return jnp.pad(block, ((0, 0), (0, 256 - block.shape[1])))

        def piece_a(query, output, misc):
            return jnp.concatenate([tiled(query), tiled(misc), tiled(output)], 0)

        def piece_f(up, down):
            return jnp.concatenate([tiled(up), tiled(down)], 0)

        big = [
            lax.all_gather(lax.all_gather(w, "dp", axis=1, tiled=True), "tp", axis=2, tiled=True)
            for w in low_parts[:4]
        ]
        small = [lax.all_gather(w, ("dp", "tp"), axis=1, tiled=True) for w in low_parts[4:6]]
        wide = [lax.all_gather(g.astype(bf16), ("dp", "tp"), axis=2, tiled=True) for g in gain_parts]

        def cut(matrix, j, q):
            width = matrix.shape[1] // VTP
            return matrix[j * RW : (j + 1) * RW, q * width : (q + 1) * width]

        pieces = []
        for l in range(LAYERS):
            misc = small_block(small[0][l], small[1][l], [g[l, w] for w in range(2) for g in wide])

            def block_a(j, q, l=l, misc=misc):
                row = (j * VTP + q) * RM
                return piece_a(cut(big[0][l], j, q), cut(big[1][l], j, q), misc[row : row + RM])

            def block_f(j, q, l=l):
                return piece_f(cut(big[2][l], j, q), cut(big[3][l], j, q))

            pieces.append((block_piece(block_a, False), block_piece(block_f, l == LAYERS - 1)))
        residual = tokens
        for l in range(LAYERS):
            run_attn_forward(l, residual, pieces[l][0])
            residual = run_ffn_forward(l, pieces[l][1])
        layer_out = residual
        upstream = cotangent
        whole = [None] * LAYERS
        for l in reversed(range(LAYERS)):
            a, f = pieces[l]
            mid_grad, gain_grad, both_f = run_ffn_backward(l, upstream, f)
            gh, dd, gl, both_o = run_output_backward(l, mid_grad, a)
            upstream, both_q = run_attn_backward(l, mid_grad, gh, dd, gl, gain_grad, a)
            misc = both_q[:, :, TA * RW :].reshape(VDP, VTP, 2, RM, 128).transpose(0, 1, 3, 2, 4).reshape(D, 256)
            whole[l] = (
                unblock_matrix(both_q[:, :, : TA * RW], RW),
                unblock_matrix(both_o, RW),
                unblock_matrix(both_f[:, :, : TF * RW], RW),
                unblock_matrix(both_f[:, :, TF * RW :], RW),
                misc,
            )

    sums = []
    for i in range(4):
        grad = jnp.stack([w[i] for w in whole]).astype(f32)
        grad = lax.psum_scatter(grad, "tp", scatter_dimension=2, tiled=True)
        sums.append(lax.psum_scatter(grad, "dp", scatter_dimension=1, tiled=True))
    misc = jnp.stack([w[4] for w in whole]).astype(f32)
    misc = lax.psum_scatter(misc, ("dp", "tp"), scatter_dimension=1, tiled=True)
    sums += [misc[:, :, :128], misc[:, :, 128 : 128 + E], misc[:, :, 128 + E : 130 + E].transpose(0, 2, 1)]
    sums = [s * scale for s in sums]
    squares = jnp.sum(jnp.stack([jnp.sum(s * s) for s in sums]))
    grad_norm = jnp.sqrt(lax.psum(squares, ("dp", "tp")))
    factor = jnp.minimum(1.0, clip_bound / grad_norm)
    outs = [layer_out, upstream, grad_norm]
    for i in range(7):
        outs += adamw(weights[i], firsts[i], seconds[i], averages[i], sums[i], factor, learn_rates[i])
    return tuple(outs)


def solution(mesh):
    token = P(("dp", "tp"), None)
    big = P(None, "dp", "tp")
    small = P(None, ("dp", "tp"), None)
    gain = P(None, None, ("dp", "tp"))
    group = (big, big, big, big, small, small, gain)
    in_specs = (token,) * 4 + group * 4
    out_specs = (token, token, P()) + tuple(spec for spec in group for _ in range(4))
    return jax.shard_map(local, mesh=mesh, in_specs=in_specs, out_specs=out_specs, check_vma=False)
```

```python
import functools

import jax
import jax.numpy as jnp
from jax import lax
from jax.experimental import pallas as pl
from jax.experimental.pallas import tpu as pltpu
from jax.sharding import PartitionSpec as P

E = 24
H = 64
TOPK = 8
LEN = 1024
LAYERS = 2
STEP = 10
D = 512
FF = 2048
EH = E * H
KH = TOPK * H
PAIRS = TOPK // 2
COLS = EH // 128
ROWS = 512
AROWS = 256
STEPS = LEN // ROWS
SUB = 128
VDP = 8
VTP = 4
RW = D // VDP
CA = EH // VTP
CF = FF // VTP
RM = D // (VDP * VTP)
TA = CA // 128
TF = CF // 128
RQ = TA * RW + 2 * RM
RA = RQ + TA * RW
RF = 2 * TF * RW
AT_Q = TA * RW
AT_MISC = 2 * TA * RW
REST = 1024
REDUCE = VDP + VTP
BLOCKS = 2 * (VDP + VTP)
VMEM = 60 * 1024 * 1024

epsilon = 1e-06
clip_bound = 0.05
learn_rates = (0.1, 1.0, 0.1, 0.1, 0.1, 0.1, 0.6)
beta_one = 0.9
beta_two = 0.95
adam_floor = 1e-08
weight_decay = 0.1
ema_decay = 0.7
masked_value = -1e30
f32 = jnp.float32
bf16 = jnp.bfloat16


def dot(a, b):
    return lax.dot_general(a, b, (((1,), (0,)), ((), ())), preferred_element_type=f32)


def dot_nt(a, b):
    return lax.dot_general(a, b, (((1,), (1,)), ((), ())), preferred_element_type=f32)


def lanes(rows, dtype=jnp.int32):
    return lax.broadcasted_iota(jnp.int32, (rows, 128), 1).astype(dtype)


def normalize(x):
    factor = lax.rsqrt(jnp.mean(x * x, -1, keepdims=True) + epsilon)
    return x * factor, factor


def both_halves(x, low_half):
    turned = pltpu.roll(x, 64, 1)
    return jnp.where(low_half, x, turned), jnp.where(low_half, turned, x)


def slot_columns(hc):
    rows = hc.shape[0]
    return [jnp.broadcast_to(hc[:, k : k + 1], (rows, 128)).astype(bf16) for k in range(TOPK)]


def pick_heads(full, slots):
    rows = full.shape[0]
    low_half = lanes(rows) < 64
    low_half16 = lanes(rows).astype(bf16) < jnp.asarray(64, bf16)
    pairs = [jnp.where(low_half16, slots[2 * p], slots[2 * p + 1]) for p in range(PAIRS)]
    out = [jnp.zeros((rows, 128), bf16) for _ in range(PAIRS)]
    for c in range(COLS):
        even, odd = both_halves(full[:, c * 128 : (c + 1) * 128], low_half)
        even = even.astype(bf16)
        odd = odd.astype(bf16)
        for p in range(PAIRS):
            out[p] = jnp.where(pairs[p] == jnp.asarray(2 * c, bf16), even, out[p])
            out[p] = jnp.where(pairs[p] == jnp.asarray(2 * c + 1, bf16), odd, out[p])
    return out


def spread_heads(pair_values, slots, store):
    rows = pair_values[0].shape[0]
    low_half = lanes(rows) < 64
    copies = []
    for p in range(PAIRS):
        even, odd = both_halves(pair_values[p], low_half)
        copies += [even.astype(bf16), odd.astype(bf16)]
    half = jnp.where(lanes(rows).astype(bf16) < jnp.asarray(64, bf16), jnp.asarray(0, bf16), jnp.asarray(1, bf16))
    for c in range(COLS):
        expert = half + jnp.asarray(2 * c, bf16)
        total = jnp.zeros((rows, 128), bf16)
        for k in range(TOPK):
            total = jnp.where(slots[k] == expert, copies[k], total)
        store(c, total)


def block_of(refs, core, position):
    if len(refs) == 2:
        return refs[core].at[position]
    return refs[2 * (position // 4) + core].at[position % 4]


def spots(plane_first):
    out = []
    for j in range(VDP):
        for q in range(VTP):
            position = q * 4 + j // 2 if plane_first else (j // 2) * 4 + q
            out.append((j, q, (j % 2, position)))
    return out


def place(refs, scratch, idx, first, tiles, plane_first=False):
    for j, q, (core, position) in spots(plane_first):
        row = pl.multiple_of(idx[j] * RW, RW)
        for t in range(tiles):
            col = pl.multiple_of(idx[VDP + q] * (tiles * 128) + t * 128, 128)
            start = first + t * RW
            scratch[pl.ds(row, RW), pl.ds(col, 128)] = block_of(refs, core, position)[start : start + RW, :]


def place_misc(refs, scratch, idx, first):
    for j, q, (core, position) in spots(False):
        row = pl.multiple_of((idx[j] * VTP + idx[VDP + q]) * RM, RM)
        for t in range(2):
            start = first + t * RM
            scratch[pl.ds(row, RM), t * 128 : (t + 1) * 128] = block_of(refs, core, position)[start : start + RM, :]


def target_of(targets, j):
    return (targets[0], j) if len(targets) == 1 else (targets[j % 2], j // 2)


def hand_out(targets, grad, idx, first, tiles, at=0):
    for j in range(VDP):
        row = pl.multiple_of(idx[REDUCE + j] * RW, RW)
        target, place_at = target_of(targets, j)
        for t in range(tiles):
            start = first + t * RW
            target[place_at, at, start : start + RW, :] = grad[pl.ds(row, RW), t * 128 : (t + 1) * 128].astype(bf16)


def bias_of(segc, segr_ref, row0, start, width):
    rows = row0 + lax.broadcasted_iota(jnp.int32, (SUB, width), 0)
    cols = start + lax.broadcasted_iota(jnp.int32, (SUB, width), 1)
    same = segc[:, 0:1] == segr_ref[0:1, pl.ds(start, width)]
    return jnp.where((cols <= rows) & same, 0.0, masked_value).astype(f32)


def attn_forward_kernel(idx, x_ref, hc_ref, segc_ref, segr_ref, *rest):
    w_refs, rest = rest[:8], rest[8:]
    (mid_ref, qs_ref, kv_ref, ho_ref, lse_ref, spread_ref, gate_ref, gains_ref) = rest[:8]
    (wq, wo, misc, gain_s, kt_lo, kt_hi, v_lo, v_hi, qst, heads_s) = rest[8:]
    step = pl.program_id(0)

    @pl.when(step == 0)
    def _():
        place(w_refs, wq, idx, AT_Q, TA)
        place(w_refs, wo, idx, 0, TA)
        place_misc(w_refs, misc, idx, AT_MISC)
        turned = misc[:, 128:256].astype(f32).T
        gain_s[...] = jnp.zeros_like(gain_s)
        gain_s[0:1, :] = turned[24:25] + turned[25:26] + turned[26:27]
        gain_s[1:2, :] = turned[27:28] + turned[28:29] + turned[29:30]
        gains_ref[...] = gain_s[...]

    x = x_ref[...].astype(f32)
    normed, _ = normalize(x)
    act = (normed * gain_s[0:1, :]).astype(bf16)
    hc = hc_ref[...]
    slots = slot_columns(hc)
    low_half = lanes(AROWS) < 64
    lane = lanes(AROWS)
    small = dot(act, misc[:, 0:256])
    kv = small[:, 0:128].astype(bf16)
    logits = jnp.where(lane < E, small[:, 128:256], masked_value)
    top = jnp.max(logits, -1, keepdims=True)
    lane_f = lane.astype(f32)
    hit = [hc[:, k : k + 1] == lane_f for k in range(TOPK)]
    chosen = hit[0]
    for k in range(1, TOPK):
        chosen = chosen | hit[k]
    powers = jnp.where(chosen, jnp.exp(logits - top), 0.0)
    gate = powers / jnp.sum(powers, -1, keepdims=True)
    gate_ref[...] = gate
    gate_low = gate.astype(bf16).astype(f32)
    gates = [jnp.sum(jnp.where(hit[k], gate_low, 0.0), -1, keepdims=True) for k in range(TOPK)]
    kv_ref[...] = kv
    row = pl.multiple_of(step * AROWS, AROWS)
    kv_f = kv.astype(f32)
    k_lo = jnp.where(low_half, kv_f, 0.0)
    k_hi = pltpu.roll(k_lo, 64, 1)
    val_hi = jnp.where(low_half, 0.0, kv_f)
    val_lo = pltpu.roll(val_hi, 64, 1)
    kt_lo[:, pl.ds(row, AROWS)] = k_lo.T.astype(bf16)
    kt_hi[:, pl.ds(row, AROWS)] = k_hi.T.astype(bf16)
    ones = jnp.where(low_half, 1.0, 0.0)
    v_lo[pl.ds(row, AROWS), 0:128] = val_lo.astype(bf16)
    v_lo[pl.ds(row, AROWS), 128:256] = ones.astype(bf16)
    v_hi[pl.ds(row, AROWS), 0:128] = val_hi.astype(bf16)
    v_hi[pl.ds(row, AROWS), 128:256] = (1.0 - ones).astype(bf16)
    queries = dot(act, wq[...])
    picked = pick_heads(queries, slots)
    for p in range(PAIRS):
        scaled = picked[p] * jnp.asarray(H ** (-0.5), bf16)
        qs_ref[:, p * 128 : (p + 1) * 128] = scaled
        for s in range(AROWS // SUB):
            qst[s, p * SUB : (p + 1) * SUB, :] = scaled[s * SUB : (s + 1) * SUB]

    def sub_block(s, carry):
        block = step * (AROWS // SUB) + s
        count = idx[BLOCKS + block]
        rows = pl.ds(pl.multiple_of(s * SUB, SUB), SUB)

        def attend(n):
            width = n * SUB
            start = pl.multiple_of((block + 1 - n) * SUB, SUB)
            bias = bias_of(segc_ref[rows, :], segr_ref, block * SUB, start, width)
            q4 = qst[s]
            parts = []
            tops = []
            for kt in (kt_lo, kt_hi):
                scores = dot(q4, kt[:, pl.ds(start, width)]).reshape(PAIRS, SUB, width) + bias[None]
                peak = jnp.max(scores, -1, keepdims=True)
                parts.append(jnp.exp(scores - peak).astype(bf16).reshape(PAIRS * SUB, width))
                tops.append(peak.reshape(PAIRS * SUB, 1))
            result = dot(parts[0], v_lo[pl.ds(start, width), :]) + dot(parts[1], v_hi[pl.ds(start, width), :])
            total = result[:, 128:256]
            heads = result[:, 0:128] / total
            log_sum = jnp.where(lanes(PAIRS * SUB) < 64, tops[0], tops[1]) + jnp.log(total)
            keep = jnp.zeros((SUB, 128), f32)
            for p in range(PAIRS):
                one = slice(p * SUB, (p + 1) * SUB)
                heads_s[rows, p * 128 : (p + 1) * 128] = heads[one]
                keep = jnp.where((lanes(SUB) & 63) == p, log_sum[one], keep)
            lse_ref[rows, :] = keep

        for n in range(1, 6):
            pl.when(count == n)(functools.partial(attend, n))
        return carry

    lax.fori_loop(0, AROWS // SUB, sub_block, 0)
    mixed = []
    for p in range(PAIRS):
        gate_pair = jnp.where(low_half, gates[2 * p], gates[2 * p + 1])
        mixed.append(gate_pair * heads_s[:, p * 128 : (p + 1) * 128])
    ho_ref[...] = heads_s[...].astype(bf16)

    def store(c, value):
        spread_ref[:, c * 128 : (c + 1) * 128] = value

    spread_heads(mixed, slots, store)
    mid_ref[...] = x + dot_nt(spread_ref[...], wo[...])


def ffn_forward_kernel(plane_first, idx, x_ref, gains_ref, *rest):
    count = 2 if plane_first else 8
    w_refs, rest = rest[:count], rest[count:]
    out_ref = rest[0]
    wu, wd = rest[1:]

    @pl.when(pl.program_id(0) == 0)
    def _():
        place(w_refs, wu, idx, 0, TF, plane_first)
        place(w_refs, wd, idx, TF * RW, TF, plane_first)

    x = x_ref[...]
    normed, _ = normalize(x)
    act = (normed * gains_ref[1:2, :]).astype(bf16)
    pre = dot(act, wu[...])
    hidden = jax.nn.gelu(pre, approximate=True).astype(bf16)
    out_ref[...] = (x + dot_nt(hidden, wd[...])).astype(out_ref.dtype)


def ffn_backward_kernel(plane_first, idx, up_ref, x_ref, gains_ref, *rest):
    count = 2 if plane_first else 8
    w_refs, rest = rest[:count], rest[count:]
    mid_ref, gain_ref = rest[:2]
    targets = rest[2:-7]
    wu, wd, hid_s, gp_s, grad_t, act_t, part = rest[-7:]
    step = pl.program_id(0)

    @pl.when(step == 0)
    def _():
        place(w_refs, wu, idx, 0, TF, plane_first)
        place(w_refs, wd, idx, TF * RW, TF, plane_first)
        gain_ref[...] = jnp.zeros_like(gain_ref)

    @pl.when(step < STEPS)
    def _():
        row = pl.multiple_of(step * ROWS, ROWS)
        up = up_ref[...].astype(f32)
        gain = gains_ref[1:2, :]
        normed, factor = normalize(x_ref[...])
        act_f = normed * gain
        act = act_f.astype(bf16)
        act_t[:, pl.ds(row, ROWS)] = act_f.T.astype(bf16)
        grad_t[:, pl.ds(row, ROWS)] = up.T.astype(bf16)
        pre = dot(act, wu[...])
        square = pre * pre
        bend = jnp.tanh(0.7978845608028654 * pre * (1.0 + 0.044715 * square))
        half = 0.5 * (1.0 + bend)
        hid_s[pl.ds(row, ROWS), :] = (pre * half).astype(bf16)
        slope = half + (0.5 * 0.7978845608028654) * pre * (1.0 - bend * bend) * (1.0 + 3.0 * 0.044715 * square)
        grad_pre = (dot(up.astype(bf16), wd[...]) * slope).astype(bf16)
        gp_s[pl.ds(row, ROWS), :] = grad_pre
        grad_act = dot_nt(grad_pre, wu[...])
        scaled = grad_act * gain
        inner = jnp.mean(scaled * normed, -1, keepdims=True)
        mid_ref[...] = up + factor * (scaled - normed * inner)
        gain_ref[0:1, :] += jnp.sum(grad_act * normed, 0, keepdims=True)

    @pl.when(step >= STEPS)
    def _():
        q = step - STEPS
        col = pl.multiple_of(idx[REDUCE + VDP + q] * CF, CF)
        part[...] = dot(act_t[...], gp_s[:, pl.ds(col, CF)])
        hand_out(targets, part, idx, 0, TF)
        part[...] = dot(grad_t[...], hid_s[:, pl.ds(col, CF)])
        hand_out(targets, part, idx, TF * RW, TF)


def output_backward_kernel(idx, mid_ref, hc_ref, ho_ref, gate_ref, spread_ref, *rest):
    w_refs, rest = rest[:8], rest[8:]
    gh_ref, dd_ref, gl_ref = rest[:3]
    targets = rest[3:-7]
    wo, grad_t, part, by_expert, by_expert_t, by_slot, spread_s = rest[-7:]
    step = pl.program_id(0)

    @pl.when(step == 0)
    def _():
        place(w_refs, wo, idx, 0, TA)
        made = lax.broadcasted_iota(jnp.int32, (EH, 128), 0) // H
        wide = (made == lax.broadcasted_iota(jnp.int32, (EH, 128), 1)).astype(f32)
        by_expert[...] = wide.astype(bf16)
        by_expert_t[...] = wide.T.astype(bf16)
        row = lax.broadcasted_iota(jnp.int32, (KH, 128), 0)
        slot = row // 128 + (row & 64)
        by_slot[...] = (slot == lax.broadcasted_iota(jnp.int32, (KH, 128), 1)).astype(bf16)

    @pl.when(step < STEPS)
    def _():
        row = pl.multiple_of(step * ROWS, ROWS)
        mid = mid_ref[...]
        grad_t[:, pl.ds(row, ROWS)] = mid.T.astype(bf16)
        full = dot(mid.astype(bf16), wo[...])
        gate = gate_ref[...]
        grads = pick_heads(dot(gate.astype(bf16), by_expert_t[...]) * full, slot_columns(hc_ref[...]))
        inner = jnp.zeros((ROWS, 128), f32)
        for p in range(PAIRS):
            cut = slice(p * 128, (p + 1) * 128)
            gh_ref[:, cut] = grads[p]
            product = grads[p].astype(f32) * ho_ref[:, cut].astype(f32)
            high = product.astype(bf16)
            low = (product - high.astype(f32)).astype(bf16)
            inner += dot(high, by_slot[cut, :]) + dot(low, by_slot[cut, :])
        dd_ref[...] = inner
        spread = spread_ref[...]
        spread_s[pl.ds(row, ROWS), :] = spread
        weighted = dot((full * spread.astype(f32)).astype(bf16), by_expert[...])
        total = jnp.sum(weighted, -1, keepdims=True)
        gl_ref[...] = (weighted - gate * total).astype(bf16)

    @pl.when(step >= STEPS)
    def _():
        for q in range(VTP):
            col = pl.multiple_of(idx[REDUCE + VDP + q] * CA, 128)
            part[q] = dot(grad_t[...], spread_s[:, pl.ds(col, CA)])
            hand_out(targets, part.at[q], idx, 0, TA, q)


def attn_backward_kernel(
    idx, mid_ref, x_ref, hc_ref, segc_ref, segr_ref, qs_ref, gh_ref, kv_ref, lse_ref, dd_ref, gl_ref, gains_ref, gfg_ref, *rest
):
    w_refs, misc_refs, rest = rest[:8], rest[8:16], rest[16:]
    out_ref = rest[0]
    targets, rest = rest[1:-18], rest[-18:]
    (wq, misc, kt_lo, kt_hi, vt_lo, vt_hi, k_lo, k_hi, dkv_t, qst, gst, dq_s, gq_s, act_t) = rest[:14]
    (dkv_s, gain_s, part, pmisc) = rest[14:]
    step = pl.program_id(0)

    @pl.when(step == 0)
    def _():
        place(w_refs, wq, idx, 0, TA)
        place_misc(misc_refs, misc, idx, 0)
        low = lanes(LEN) < 64
        kv = kv_ref[...].astype(f32)
        one = jnp.where(low, kv, 0.0)
        two = pltpu.roll(one, 64, 1)
        k_lo[...] = one.astype(bf16)
        k_hi[...] = two.astype(bf16)
        kt_lo[...] = one.T.astype(bf16)
        kt_hi[...] = two.T.astype(bf16)
        one = jnp.where(low, 0.0, kv)
        vt_hi[...] = one.T.astype(bf16)
        vt_lo[...] = pltpu.roll(one, 64, 1).T.astype(bf16)
        dkv_t[...] = jnp.zeros_like(dkv_t)
        gain_s[...] = jnp.zeros_like(gain_s)

    @pl.when(step < STEPS)
    def _():
        row = pl.multiple_of(step * ROWS, ROWS)
        for p in range(PAIRS):
            for s in range(ROWS // SUB):
                qst[s, p * SUB : (p + 1) * SUB, :] = qs_ref[s * SUB : (s + 1) * SUB, p * 128 : (p + 1) * 128]
                gst[s, p * SUB : (p + 1) * SUB, :] = gh_ref[s * SUB : (s + 1) * SUB, p * 128 : (p + 1) * 128]

        def sub_block(s, carry):
            block = step * (ROWS // SUB) + s
            count = idx[BLOCKS + block]
            rows = pl.ds(pl.multiple_of(s * SUB, SUB), SUB)

            def attend(n):
                width = n * SUB
                start = pl.multiple_of((block + 1 - n) * SUB, SUB)
                win = pl.ds(start, width)
                bias = bias_of(segc_ref[rows, :], segr_ref, block * SUB, start, width)
                q4 = qst[s]
                g4 = gst[s]
                q4t = q4.astype(f32).T.astype(bf16)
                g4t = g4.astype(f32).T.astype(bf16)
                lse = lse_ref[rows, :]
                dd = dd_ref[rows, :]
                dq = None
                dk = None
                dv = None
                for half, (kt, vt, kk) in enumerate(((kt_lo, vt_lo, k_lo), (kt_hi, vt_hi, k_hi))):
                    off = 64 * half
                    log_sum = jnp.stack([lse[:, off + p : off + p + 1] for p in range(PAIRS)])
                    inner = jnp.stack([dd[:, off + p : off + p + 1] for p in range(PAIRS)])
                    scores = dot(q4, kt[:, win]).reshape(PAIRS, SUB, width)
                    prob = jnp.exp(scores + bias[None] - log_sum)
                    dprob = dot(g4, vt[:, win]).reshape(PAIRS, SUB, width)
                    dscore = (prob * (dprob - inner)).astype(bf16).reshape(PAIRS * SUB, width)
                    low_prob = prob.astype(bf16).reshape(PAIRS * SUB, width)
                    a = dot(dscore, kk[win, :])
                    b = dot(q4t[off : off + 64], dscore)
                    c = dot(g4t[off : off + 64], low_prob)
                    dq = a if dq is None else dq + a
                    dk = b if dk is None else dk + b
                    dv = c if dv is None else dv + c
                dkv_t[0:64, win] += dk
                dkv_t[64:128, win] += dv
                dq = dq * (H ** (-0.5))
                for p in range(PAIRS):
                    dq_s[rows, p * 128 : (p + 1) * 128] = dq[p * SUB : (p + 1) * SUB]

            for n in range(1, 6):
                pl.when(count == n)(functools.partial(attend, n))
            return carry

        lax.fori_loop(0, ROWS // SUB, sub_block, 0)
        slots = slot_columns(hc_ref[...])

        def store(c, value):
            gq_s[pl.ds(row, ROWS), c * 128 : (c + 1) * 128] = value

        spread_heads([dq_s[:, p * 128 : (p + 1) * 128] for p in range(PAIRS)], slots, store)

    @pl.when(step == STEPS)
    def _():
        dkv_s[...] = dkv_t[...].T.astype(bf16)

    @pl.when((step >= STEPS) & (step < 2 * STEPS))
    def _():
        row = pl.multiple_of((step - STEPS) * ROWS, ROWS)
        here = pl.ds(row, ROWS)
        gain = gains_ref[0:1, :]
        normed, factor = normalize(x_ref[...].astype(f32))
        act_t[:, here] = (normed * gain).T.astype(bf16)
        grad_act = dot_nt(gq_s[here, :], wq[...])
        grad_act += dot_nt(dkv_s[here, :], misc[:, 0:128])
        router = jnp.where(lanes(D) < E, misc[:, 128:256].astype(f32), 0.0).astype(bf16)
        grad_act += dot_nt(gl_ref[here, :], router)
        scaled = grad_act * gain
        inner = jnp.mean(scaled * normed, -1, keepdims=True)
        out_ref[...] = mid_ref[...] + factor * (scaled - normed * inner)
        gain_s[0:1, :] += jnp.sum(grad_act * normed, 0, keepdims=True)

    @pl.when(step == 2 * STEPS)
    def _():
        pmisc[:, 0:128] = dot(act_t[...], dkv_s[...])
        router = dot(act_t[...], gl_ref[...])
        gain_s[1:2, :] = gfg_ref[0:1, :]
        turned = gain_s[...].T
        lane = lanes(D)
        router = jnp.where(lane < E, router, 0.0)
        router = jnp.where(lane == E, turned[:, 0:1], router)
        router = jnp.where(lane == E + 1, turned[:, 1:2], router)
        pmisc[:, 128:256] = router

    @pl.when(step >= 2 * STEPS)
    def _():
        for q in range(VTP):
            col = pl.multiple_of(idx[REDUCE + VDP + q] * CA, 128)
            part[q] = dot(act_t[...], gq_s[:, pl.ds(col, CA)])
            hand_out(targets, part.at[q], idx, 0, TA, q)
            for j in range(VDP):
                row = pl.multiple_of((idx[REDUCE + j] * VTP + idx[REDUCE + VDP + q]) * RM, RM)
                target, place_at = target_of(targets, j)
                for t in range(2):
                    start = TA * RW + t * RM
                    target[place_at, q, start : start + RM, :] = pmisc[
                        pl.ds(row, RM), t * 128 : (t + 1) * 128
                    ].astype(bf16)


def pack_attn(out, base, query, output, keyval, router, columns, layer):
    for t in range(TA):
        cut = slice(t * 128, (t + 1) * 128)
        out[base + t * RW : base + (t + 1) * RW, :] = output[layer, :, cut].astype(bf16)
        start = base + AT_Q + t * RW
        out[start : start + RW, :] = query[layer, :, cut].astype(bf16)
    start = base + AT_MISC
    out[start : start + RM, :] = keyval[layer].astype(bf16)
    misc = slice(start + RM, start + 2 * RM)
    lane = lanes(RM)
    block = jnp.zeros((RM, 128), f32)
    gains = columns[layer]
    for which in range(2):
        part = gains[:, which : which + 1]
        for i in range(3):
            high = part.astype(bf16).astype(f32)
            block = jnp.where(lane == E + 3 * which + i, high, block)
            part = part - high
    out[misc, :] = block.astype(bf16)
    out[misc, 0:E] = router[layer].astype(bf16)


def pack_ffn(out, base, up, down, layer):
    for t in range(TF):
        cut = slice(t * 128, (t + 1) * 128)
        out[base + t * RW : base + (t + 1) * RW, :] = up[layer, :, cut].astype(bf16)
        start = base + (TF + t) * RW
        out[start : start + RW, :] = down[layer, :, cut].astype(bf16)


def pack_first_kernel(query, output, keyval, router, columns, out):
    pack_attn(out, 0, query, output, keyval, router, columns, 0)


def pack_other_kernel(query, output, keyval, router, columns, up, down, rest, last):
    pack_ffn(rest, 0, up, down, 0)
    pack_attn(rest, RF, query, output, keyval, router, columns, 1)
    rest[RF + RA :, :] = jnp.zeros((REST - RF - RA, 128), bf16)
    pack_ffn(last, 0, up, down, 1)


def sum_kernel(scale, parts, total, square):
    value = parts[0].astype(f32)
    for k in range(1, parts.shape[0]):
        value = value + parts[k].astype(f32)
    value = value * scale
    total[...] = value
    rows = value.shape[0]
    square[...] = jnp.sum((value * value).reshape(rows // 8, 8, 128), 0)


def update_kernel(square, query0, rest, last, *refs):
    state, norm_ref, outs = refs[:28], refs[28], refs[29:]
    norm = jnp.sqrt(jnp.sum(jnp.sum(square[...], 0, keepdims=True), 1, keepdims=True))
    norm_ref[...] = norm
    factor = jnp.minimum(1.0, clip_bound / norm)

    def step(i, at, grad):
        result = adamw(
            state[i][at], state[7 + i][at], state[14 + i][at], state[21 + i][at], grad, factor, learn_rates[i]
        )
        for k in range(4):
            outs[4 * i + k][at] = result[k]

    def tile(i, layer, t, ref, start):
        step(i, (layer, slice(None), slice(t * 128, (t + 1) * 128)), ref[start : start + RW, :])

    for t in range(TA):
        tile(0, 0, t, query0, t * RW)
        tile(0, 1, t, last, t * RW)
        tile(1, 0, t, rest, RF + t * RW)
        tile(1, 1, t, last, RQ + t * RW)
    for t in range(TF):
        tile(2, 0, t, rest, t * RW)
        tile(3, 0, t, rest, (TF + t) * RW)
        tile(2, 1, t, last, RA + t * RW)
        tile(3, 1, t, last, RA + (TF + t) * RW)
    for layer, ref in ((0, query0), (1, last)):
        start = TA * RW
        step(4, (layer,), ref[start : start + RM, :])
        block = ref[start + RM : start + 2 * RM, :]
        step(5, (layer,), block[:, 0:E])
        step(6, (layer,), block.T[E : E + 2, :])


def add_kernel(pieces, *refs):
    step = pl.program_id(0)
    outs = refs[2 * pieces :]
    first = 0
    for piece in range(pieces):
        one, two = refs[2 * piece], refs[2 * piece + 1]
        rows = one.shape[2]
        for k in range(4):
            outs[k][0, first : first + rows, :] = (one[k, 0].astype(f32) + two[k, 0].astype(f32)).astype(bf16)
        first += rows


def add_pairs(pairs):
    rows = sum(keep.shape[2] for keep, _ in pairs)
    flat = [x for pair in pairs for x in pair]
    return pl.pallas_call(
        functools.partial(add_kernel, len(pairs)),
        grid=(VTP,),
        in_specs=[pl.BlockSpec((4, 1) + x.shape[2:], lambda i: (0, i, 0, 0)) for x in flat],
        out_specs=[pl.BlockSpec((1, rows, 128), lambda i: (i, 0, 0))] * 4,
        out_shape=[jax.ShapeDtypeStruct((VTP, rows, 128), bf16)] * 4,
        compiler_params=pltpu.CompilerParams(dimension_semantics=("arbitrary",), vmem_limit_bytes=24 * 1024 * 1024),
        name="add_pairs",
    )(*[in_hbm(x) for x in flat])


def whole_call(kernel, out_shapes, name, *args):
    return pl.pallas_call(
        kernel,
        in_specs=[pl.BlockSpec(memory_space=pltpu.VMEM)] * len(args),
        out_specs=[pl.BlockSpec(memory_space=pltpu.VMEM)] * len(out_shapes),
        out_shape=[jax.ShapeDtypeStruct(shape, kind) for shape, kind in out_shapes],
        compiler_params=pltpu.CompilerParams(vmem_limit_bytes=VMEM),
        name=name,
    )(*args)


def sum_parts(parts, scale):
    rows = parts.shape[1]
    return whole_call(
        functools.partial(sum_kernel, scale), [((rows, 128), f32), ((8, 128), f32)], "sum_parts", parts
    )


def rows_spec(width, phase=0, rows=ROWS):
    steps = LEN // rows

    def index(i, idx):
        return (jnp.clip(i - phase * steps, 0, steps - 1), 0)

    return pl.BlockSpec((rows, width), index)


def full_spec(shape):
    zeros = (0,) * len(shape)
    return pl.BlockSpec(shape, lambda i, idx: zeros, pipeline_mode=pl.Buffered(1))


def kept_spec(shape):
    zeros = (0,) * len(shape)
    return pl.BlockSpec(shape, lambda i, idx: zeros)


def part_specs(rows, at, count):
    return [
        pl.BlockSpec((32 // count, rows, 128), lambda i, idx: (0, at, 0), pipeline_mode=pl.Buffered(1))
    ] * count


def stacks(arrays, rows):
    return [in_hbm(x.reshape(-1, rows, 128)) for x in arrays]


def parts_specs(rows, phase, split):
    def index(i, idx):
        return (0, jnp.maximum(i - phase * STEPS, 0), 0, 0)

    count = VDP // 2 if split else VDP
    if phase is None:
        return [kept_spec((count, VTP, rows, 128))] * (VDP // count)
    return [pl.BlockSpec((count, 1, rows, 128), index)] * (VDP // count)


def parts_shapes(rows, split):
    count = VDP // 2 if split else VDP
    return [((count, VTP, rows, 128), bf16, 1)] * (VDP // count)


def call(kernel, steps, in_specs, out_specs, out_shapes, scratch, name, flops, moved, vmem):
    return pl.pallas_call(
        kernel,
        grid_spec=pltpu.PrefetchScalarGridSpec(
            num_scalar_prefetch=1,
            grid=(steps,),
            in_specs=in_specs,
            out_specs=out_specs,
            scratch_shapes=scratch,
        ),
        out_shape=[jax.ShapeDtypeStruct(s[0], s[1]) if len(s) == 2 else pltpu.HBM(s[0], s[1]) for s in out_shapes],
        compiler_params=pltpu.CompilerParams(
            dimension_semantics=("arbitrary",), vmem_limit_bytes=vmem * 1024 * 1024
        ),
        cost_estimate=pl.CostEstimate(flops=flops, bytes_accessed=moved, transcendentals=0),
        name=name,
    )


def in_hbm(x):
    return pltpu.with_memory_space_constraint(x, pltpu.HBM)


def vm(*shape, dtype=bf16):
    return pltpu.VMEM(shape, dtype)


def attn_forward(idx, x, hc, segc, segr, weights, far):
    pin = (1,) if far else ()
    return call(
        attn_forward_kernel,
        LEN // AROWS,
        [rows_spec(D, 0, AROWS), rows_spec(TOPK, 0, AROWS), rows_spec(128, 0, AROWS), full_spec((8, LEN))]
        + part_specs(RA, 0, 8),
        [
            rows_spec(D, 0, AROWS), rows_spec(KH, 0, AROWS), rows_spec(128, 0, AROWS), rows_spec(KH, 0, AROWS), rows_spec(128, 0, AROWS),
            rows_spec(EH, 0, AROWS), rows_spec(128, 0, AROWS), kept_spec((8, D)),
        ],
        [
            ((LEN, D), f32, 1), ((LEN, KH), bf16) + pin, ((LEN, 128), bf16) + pin, ((LEN, KH), bf16) + pin,
            ((LEN, 128), f32) + pin, ((LEN, EH), bf16) + pin, ((LEN, 128), f32) + pin, ((8, D), f32),
        ],
        [
            vm(D, EH), vm(D, EH), vm(D, 256), vm(8, D, dtype=f32), vm(128, LEN), vm(128, LEN),
            vm(LEN, 256), vm(LEN, 256), vm(AROWS // SUB, PAIRS * SUB, 128), vm(AROWS, KH, dtype=f32),
        ],
        "attn_forward", 8 * 10**9, 14 * 10**6, 26,
    )(idx, in_hbm(x), hc, segc, segr, *stacks(weights, RA))


def ffn_forward(idx, x, gains, weights, last, plane_first):
    return call(
        functools.partial(ffn_forward_kernel, plane_first),
        STEPS,
        [rows_spec(D), full_spec((8, D))] + part_specs(RF, 0, 2 if plane_first else 8),
        [rows_spec(D)],
        [((LEN, D), bf16 if last else f32, 1)],
        [vm(D, FF), vm(D, FF)],
        "ffn_forward", 5 * 10**9, 8 * 10**6, 28,
    )(idx, in_hbm(x), gains, *stacks(weights, RF))[0]


def ffn_backward(idx, upstream, x, gains, weights, plane_first, split):
    return call(
        functools.partial(ffn_backward_kernel, plane_first),
        STEPS + VTP,
        [rows_spec(D), rows_spec(D), full_spec((8, D))] + part_specs(RF, 0, 2 if plane_first else 8),
        [rows_spec(D), kept_spec((8, D))] + parts_specs(RF, 1, split),
        [
            ((LEN, D), f32, 1), ((8, D), f32),
        ]
        + parts_shapes(RF, split),
        [
            vm(D, FF), vm(D, FF), vm(LEN, FF), vm(LEN, FF), vm(D, LEN), vm(D, LEN), vm(D, CF, dtype=f32),
        ],
        "ffn_backward", 13 * 10**9, 14 * 10**6, 56,
    )(idx, in_hbm(upstream), in_hbm(x), gains, *stacks(weights, RF))


def output_backward(idx, mid, hc, heads, gate, spread, weights, split):
    return call(
        output_backward_kernel,
        STEPS + 1,
        [rows_spec(D), rows_spec(TOPK), rows_spec(KH), rows_spec(128), rows_spec(EH)]
        + part_specs(TA * RW, 0, 8),
        [rows_spec(KH), rows_spec(128), rows_spec(128)] + parts_specs(TA * RW, None, split),
        [
            ((LEN, KH), bf16), ((LEN, 128), f32), ((LEN, 128), bf16),
        ]
        + parts_shapes(TA * RW, split),
        [
            vm(D, EH), vm(D, LEN), vm(VTP, D, CA, dtype=f32), vm(EH, 128), vm(128, EH), vm(KH, 128), vm(LEN, EH),
        ],
        "output_backward", 5 * 10**9, 16 * 10**6, 30,
    )(idx, in_hbm(mid), hc, in_hbm(heads), in_hbm(gate), in_hbm(spread), *stacks(weights, RA))


def attn_backward(idx, mid, x, hc, segc, segr, qs, gh, kv, lse, dd, gl, gains, gfg, weights, split):
    return call(
        attn_backward_kernel,
        2 * STEPS + 1,
        [
            rows_spec(D, 1), rows_spec(D, 1), rows_spec(TOPK), rows_spec(128), full_spec((8, LEN)),
            rows_spec(KH), rows_spec(KH), full_spec((LEN, 128)), rows_spec(128), rows_spec(128),
            full_spec((LEN, 128)), full_spec((8, D)), full_spec((8, D)),
        ]
        + part_specs(TA * RW, 1, 8)
        + part_specs(2 * RM, AT_MISC // (2 * RM), 8),
        [rows_spec(D, 1)] + parts_specs(RQ, None, split),
        [((LEN, D), f32, 1)] + parts_shapes(RQ, split),
        [
            vm(D, EH), vm(D, 256), vm(128, LEN), vm(128, LEN), vm(128, LEN), vm(128, LEN),
            vm(LEN, 128), vm(LEN, 128), vm(128, LEN, dtype=f32), vm(ROWS // SUB, PAIRS * SUB, 128),
            vm(ROWS // SUB, PAIRS * SUB, 128), vm(ROWS, KH, dtype=f32), vm(LEN, EH), vm(D, LEN),
            vm(LEN, 128), vm(8, D, dtype=f32), vm(VTP, D, CA, dtype=f32), vm(D, 256, dtype=f32),
        ],
        "attn_backward", 10 * 10**9, 16 * 10**6, 38,
    )(idx, in_hbm(mid), in_hbm(x), hc, segc, segr, in_hbm(qs), gh, kv, in_hbm(lse), dd, gl, gains, gfg, *stacks(weights, RA), *stacks(weights, RA))


def swap(k):
    return [(i, i ^ k) for i in range(VDP)]


def plane_moves(block):
    return [block] + [lax.ppermute(block, "dp", swap(2 * k)) for k in range(1, 4)]


def core_moves(blocks):
    return [x for block in blocks for x in (block, lax.ppermute(block, "dp", swap(1)))]


def stacked(blocks):
    return jnp.concatenate(blocks, 0)


def tiled(block):
    return jnp.concatenate([block[:, t : t + 128] for t in range(0, block.shape[1], 128)], 0)


def after(value, *others):
    flat, tree = jax.tree.flatten((value, others))
    return jax.tree.unflatten(tree, lax.optimization_barrier(flat))[0]


def reduce_core(keep, send):
    return keep, lax.ppermute(send, "dp", swap(1))


def reduce_plane(pair):
    return list(pair[:1]) + [lax.ppermute(pair[k], "dp", swap(2 * k)) for k in range(1, 4)]


def plane_sum(parts):
    total = parts[0].astype(f32)
    for part in parts[1:]:
        total = total + part.astype(f32)
    return total.astype(bf16)


def line_swap(parts):
    return lax.all_to_all(parts, "tp", 0, 0)


def block_piece(block, plane_first):
    order = sorted(spots(plane_first), key=lambda entry: entry[2])
    made = [block(j, q) for j, q, _ in order]
    if plane_first:
        return [jnp.concatenate(made[:16], 0), jnp.concatenate(made[16:], 0)]
    return [jnp.concatenate(made[16 * c + 4 * k : 16 * c + 4 * k + 4], 0) for k in range(4) for c in range(2)]


def unblock_matrix(both, rows):
    tiles = both.shape[2] // rows
    return both.reshape(VDP, VTP, tiles, rows, 128).transpose(0, 3, 1, 2, 4).reshape(D, VTP * tiles * 128)


def split_gain(gain):
    high = lax.reduce_precision(gain, 8, 7)
    rest = gain - high
    middle = lax.reduce_precision(rest, 8, 7)
    return [high, middle, rest - middle]


def global_sum(value):
    for k in (1, 2, 4):
        value = value + lax.ppermute(value, "dp", swap(k))
    for k in (1, 2):
        value = value + lax.ppermute(value, "tp", [(i, i ^ k) for i in range(VTP)])
    return value


def adamw(weight, moment_one, moment_two, average, grad_full, factor, learn_rate):
    clipped = grad_full * factor
    first_new = beta_one * moment_one + (1.0 - beta_one) * clipped
    second_new = beta_two * moment_two + (1.0 - beta_two) * clipped * clipped
    step_ratio = (
        first_new
        / (1.0 - beta_one**STEP)
        / (jnp.sqrt(second_new / (1.0 - beta_two**STEP)) + adam_floor)
    )
    weight_new = weight - learn_rate * (step_ratio + weight_decay * weight)
    return (weight_new, first_new, second_new, ema_decay * average + (1.0 - ema_decay) * weight_new)


def local(tokens, cotangent, head_choice, segment_ids, *state):
    weights, firsts, seconds, averages = state[0:7], state[7:14], state[14:21], state[21:28]
    query_w, output_w, up_w, down_w, keyval_w, router_w, gains_w = weights
    size_dp = lax.axis_size("dp")
    size_tp = lax.axis_size("tp")
    token_total = tokens.shape[0] * size_dp * size_tp
    native = (size_dp, size_tp) == (VDP, VTP)
    scale = 1.0 / token_total

    steady = jnp.arange(VDP + VTP, dtype=jnp.int32)
    steady = jnp.where(steady < VDP, steady, steady - VDP)
    if native:
        own = jnp.arange(VDP, dtype=jnp.int32) ^ lax.axis_index("dp").astype(jnp.int32)
        gathers = jnp.concatenate([own, steady[VDP:]])
        reduces = [gathers, steady]
    else:
        gathers = steady
        reduces = [steady, steady]
    segment = segment_ids.reshape(LEN)
    heads_at = segment[:: SUB]
    first_at = jnp.sum((segment[None, :] < heads_at[:, None]).astype(jnp.int32), 1)
    blocks = jnp.arange(LEN // SUB, dtype=jnp.int32) - first_at // SUB + 1
    tables = [jnp.concatenate([gathers, r, blocks]) for r in reduces]
    segc = jnp.broadcast_to(segment.astype(f32)[:, None], (LEN, 128))
    segr = jnp.broadcast_to(segment.astype(f32)[None, :], (8, LEN))
    hc = head_choice.astype(f32)

    def split(l):
        return native and l == 0

    def run_attn_forward(l, x, a):
        saved[l] = (x,) + tuple(attn_forward(tables[l], x, hc, segc, segr, a, True))

    def run_ffn_forward(l, f):
        return ffn_forward(tables[l], saved[l][1], saved[l][8], f, l == LAYERS - 1, l == LAYERS - 1)

    def run_ffn_backward(l, upstream, f):
        return ffn_backward(
            tables[l], upstream, saved[l][1], saved[l][8], f, l == LAYERS - 1, split(l)
        )

    def run_output_backward(l, mid_grad, a):
        _, _, _, _, heads, _, spread, gate, _ = saved[l]
        return output_backward(tables[l], mid_grad, hc, heads, gate, spread, a, split(l))

    def run_attn_backward(l, mid_grad, gh, dd, gl, gain_ffn_grad, a):
        x, _, qs, kv, _, lse, _, _, gains = saved[l]
        return attn_backward(
            tables[l], mid_grad, x, hc, segc, segr, qs, gh, kv, lse, dd, gl, gains, gain_ffn_grad, a, split(l)
        )

    saved = [None] * LAYERS
    if native:
        columns = gains_w.transpose(0, 2, 1)
        small = (query_w, output_w, keyval_w, router_w, columns)
        (first,) = whole_call(pack_first_kernel, [((RA, 128), bf16)], "pack_first", *small)
        a0 = lax.all_gather(first, "tp", tiled=True)
        rest, f1 = whole_call(
            pack_other_kernel, [((REST, 128), bf16), ((RF, 128), bf16)], "pack_other",
            *small, up_w, after(down_w, first),
        )
        rest, f1 = after((rest, f1), a0)
        a0 = plane_moves(a0)
        rest = lax.all_gather(rest, "tp")
        a0, f1 = after((a0, f1), a0)
        a0 = core_moves(a0)
        f1 = plane_moves(f1)
        rest, f1 = after((rest, f1), rest, f1)
        f0 = plane_moves(rest[:, :RF].reshape(VTP * RF, 128))
        f1 = lax.all_gather(stacked(f1), "tp", tiled=True)
        run_attn_forward(0, after(tokens, rest), a0)
        saved[0], f0, rest = after((saved[0], f0, rest), saved[0][1], f0)
        f0 = core_moves(f0)
        a1 = plane_moves(rest[:, RF : RF + RA].reshape(VTP * RA, 128))
        residual = run_ffn_forward(0, f0)
        residual, a1, f1 = after((residual, a1, f1), residual, a1, f1)
        a1 = core_moves(a1)
        f1 = core_moves([f1])
        run_attn_forward(1, residual, a1)
        mid_grad, gain_grad, rf1 = run_ffn_backward(1, cotangent, after(f1, saved[1][1]))
        rf1 = lax.psum_scatter(rf1, "dp")
        gh, dd, gl, ro1 = run_output_backward(1, mid_grad, a1)
        upstream, rq1 = run_attn_backward(1, mid_grad, gh, dd, gl, gain_grad, a1)
        ra1 = lax.psum_scatter(jnp.concatenate([rq1, ro1], 2), "dp")
        mid_grad, gain_grad, keep, send = run_ffn_backward(0, upstream, f0)
        rf0 = reduce_core(keep, send)
        mid_grad, rf1 = after((mid_grad, rf1), mid_grad, rf1)
        gh, dd, gl, keep, send = run_output_backward(0, mid_grad, a0)
        ro0 = reduce_core(keep, send)
        gh, rf0, ro0, rf1 = after((gh, rf0, ro0, rf1), gh, rf0, ro0, rf1)
        rfo = add_pairs([rf0, ro0])
        gh, rfo = after((gh, rfo), gh, rfo)
        rfo = reduce_plane(rfo)
        upstream, keep, send = run_attn_backward(0, mid_grad, gh, dd, gl, gain_grad, a0)
        rq0 = reduce_core(keep, send)
        ra1, rf1 = after((ra1, rf1), upstream, ra1, rf1)
        r1 = lax.psum_scatter(jnp.concatenate([ra1, rf1], 1), "tp")
        saved[1], rfo = after((saved[1], rfo), upstream, rfo)
        rest = plane_sum(rfo)
        rq0 = reduce_plane(add_pairs([rq0]))
        rest = line_swap(rest)
        layer_out = run_ffn_forward(1, f1)
        layer_out, rq0, rest = after((layer_out, rq0, rest), layer_out, rq0)
        r1, square_a = sum_parts(r1[None], scale)
        rest, square_b = sum_parts(rest, scale)
        rq0, square_c = sum_parts(line_swap(plane_sum(rq0)), scale)
        square = global_sum(square_a + square_b + square_c)
        shapes = [((1, 1), f32)] + [(w.shape, f32) for w in weights for _ in range(4)]
        updates = whole_call(update_kernel, shapes, "update", square, rq0, rest, r1, *state)
        return (layer_out, upstream, updates[0][0, 0]) + tuple(updates[1:])
    else:
        gain_parts = split_gain(gains_w)
        low_parts = [w.astype(bf16) for w in weights[:6]]

        def small_block(kv, router, gains):
            block = jnp.concatenate([kv, router] + [g[:, None] for g in gains], 1)
            return jnp.pad(block, ((0, 0), (0, 256 - block.shape[1])))

        def piece_a(query, output, misc):
            return jnp.concatenate([tiled(output), tiled(query), tiled(misc)], 0)

        def piece_f(up, down):
            return jnp.concatenate([tiled(up), tiled(down)], 0)

        big = [
            lax.all_gather(lax.all_gather(w, "dp", axis=1, tiled=True), "tp", axis=2, tiled=True)
            for w in low_parts[:4]
        ]
        small = [lax.all_gather(w, ("dp", "tp"), axis=1, tiled=True) for w in low_parts[4:6]]
        wide = [lax.all_gather(g.astype(bf16), ("dp", "tp"), axis=2, tiled=True) for g in gain_parts]

        def cut(matrix, j, q):
            width = matrix.shape[1] // VTP
            return matrix[j * RW : (j + 1) * RW, q * width : (q + 1) * width]

        pieces = []
        for l in range(LAYERS):
            misc = small_block(small[0][l], small[1][l], [g[l, w] for w in range(2) for g in wide])

            def block_a(j, q, l=l, misc=misc):
                row = (j * VTP + q) * RM
                return piece_a(cut(big[0][l], j, q), cut(big[1][l], j, q), misc[row : row + RM])

            def block_f(j, q, l=l):
                return piece_f(cut(big[2][l], j, q), cut(big[3][l], j, q))

            pieces.append((block_piece(block_a, False), block_piece(block_f, l == LAYERS - 1)))
        residual = tokens
        for l in range(LAYERS):
            run_attn_forward(l, residual, pieces[l][0])
            residual = run_ffn_forward(l, pieces[l][1])
        layer_out = residual
        upstream = cotangent
        whole = [None] * LAYERS
        for l in reversed(range(LAYERS)):
            a, f = pieces[l]
            mid_grad, gain_grad, both_f = run_ffn_backward(l, upstream, f)
            gh, dd, gl, both_o = run_output_backward(l, mid_grad, a)
            upstream, both_q = run_attn_backward(l, mid_grad, gh, dd, gl, gain_grad, a)
            misc = both_q[:, :, TA * RW :].reshape(VDP, VTP, 2, RM, 128).transpose(0, 1, 3, 2, 4).reshape(D, 256)
            whole[l] = (
                unblock_matrix(both_q[:, :, : TA * RW], RW),
                unblock_matrix(both_o, RW),
                unblock_matrix(both_f[:, :, : TF * RW], RW),
                unblock_matrix(both_f[:, :, TF * RW :], RW),
                misc,
            )

    sums = []
    for i in range(4):
        grad = jnp.stack([w[i] for w in whole]).astype(f32)
        grad = lax.psum_scatter(grad, "tp", scatter_dimension=2, tiled=True)
        sums.append(lax.psum_scatter(grad, "dp", scatter_dimension=1, tiled=True))
    misc = jnp.stack([w[4] for w in whole]).astype(f32)
    misc = lax.psum_scatter(misc, ("dp", "tp"), scatter_dimension=1, tiled=True)
    sums += [misc[:, :, :128], misc[:, :, 128 : 128 + E], misc[:, :, 128 + E : 130 + E].transpose(0, 2, 1)]
    sums = [s * scale for s in sums]
    squares = jnp.sum(jnp.stack([jnp.sum(s * s) for s in sums]))
    grad_norm = jnp.sqrt(lax.psum(squares, ("dp", "tp")))
    factor = jnp.minimum(1.0, clip_bound / grad_norm)
    outs = [layer_out, upstream, grad_norm]
    for i in range(7):
        outs += adamw(weights[i], firsts[i], seconds[i], averages[i], sums[i], factor, learn_rates[i])
    return tuple(outs)


def solution(mesh):
    token = P(("dp", "tp"), None)
    big = P(None, "dp", "tp")
    small = P(None, ("dp", "tp"), None)
    gain = P(None, None, ("dp", "tp"))
    group = (big, big, big, big, small, small, gain)
    in_specs = (token,) * 4 + group * 4
    out_specs = (token, token, P()) + tuple(spec for spec in group for _ in range(4))
    return jax.shard_map(local, mesh=mesh, in_specs=in_specs, out_specs=out_specs, check_vma=False)
```

```python
import functools

import jax
import jax.numpy as jnp
from jax import lax
from jax.experimental import pallas as pl
from jax.experimental.pallas import tpu as pltpu
from jax.sharding import PartitionSpec as P

E = 24
H = 64
TOPK = 8
LEN = 1024
LAYERS = 2
STEP = 10
D = 512
FF = 2048
EH = E * H
KH = TOPK * H
PAIRS = TOPK // 2
COLS = EH // 128
ROWS = 512
AROWS = 256
STEPS = LEN // ROWS
SUB = 128
VDP = 8
VTP = 4
RW = D // VDP
CA = EH // VTP
CF = FF // VTP
RM = D // (VDP * VTP)
TA = CA // 128
TF = CF // 128
RQ = TA * RW + 2 * RM
RA = RQ + TA * RW
RF = 2 * TF * RW
AT_Q = TA * RW
AT_MISC = 2 * TA * RW
REST = 1024
REDUCE = VDP + VTP
BLOCKS = 2 * (VDP + VTP)
VMEM = 60 * 1024 * 1024

epsilon = 1e-06
clip_bound = 0.05
learn_rates = (0.1, 1.0, 0.1, 0.1, 0.1, 0.1, 0.6)
beta_one = 0.9
beta_two = 0.95
adam_floor = 1e-08
weight_decay = 0.1
ema_decay = 0.7
masked_value = -1e30
f32 = jnp.float32
bf16 = jnp.bfloat16


def dot(a, b):
    return lax.dot_general(a, b, (((1,), (0,)), ((), ())), preferred_element_type=f32)


def dot_nt(a, b):
    return lax.dot_general(a, b, (((1,), (1,)), ((), ())), preferred_element_type=f32)


def lanes(rows, dtype=jnp.int32):
    return lax.broadcasted_iota(jnp.int32, (rows, 128), 1).astype(dtype)


def normalize(x):
    factor = lax.rsqrt(jnp.mean(x * x, -1, keepdims=True) + epsilon)
    return x * factor, factor


def both_halves(x, low_half):
    turned = pltpu.roll(x, 64, 1)
    return jnp.where(low_half, x, turned), jnp.where(low_half, turned, x)


def slot_columns(hc):
    rows = hc.shape[0]
    return [jnp.broadcast_to(hc[:, k : k + 1], (rows, 128)).astype(bf16) for k in range(TOPK)]


def pick_heads(full, slots):
    rows = full.shape[0]
    low_half = lanes(rows) < 64
    low_half16 = lanes(rows).astype(bf16) < jnp.asarray(64, bf16)
    pairs = [jnp.where(low_half16, slots[2 * p], slots[2 * p + 1]) for p in range(PAIRS)]
    out = [jnp.zeros((rows, 128), bf16) for _ in range(PAIRS)]
    for c in range(COLS):
        even, odd = both_halves(full[:, c * 128 : (c + 1) * 128], low_half)
        even = even.astype(bf16)
        odd = odd.astype(bf16)
        for p in range(PAIRS):
            out[p] = jnp.where(pairs[p] == jnp.asarray(2 * c, bf16), even, out[p])
            out[p] = jnp.where(pairs[p] == jnp.asarray(2 * c + 1, bf16), odd, out[p])
    return out


def spread_heads(pair_values, slots, store):
    rows = pair_values[0].shape[0]
    low_half = lanes(rows) < 64
    copies = []
    for p in range(PAIRS):
        even, odd = both_halves(pair_values[p], low_half)
        copies += [even.astype(bf16), odd.astype(bf16)]
    half = jnp.where(lanes(rows).astype(bf16) < jnp.asarray(64, bf16), jnp.asarray(0, bf16), jnp.asarray(1, bf16))
    for c in range(COLS):
        expert = half + jnp.asarray(2 * c, bf16)
        total = jnp.zeros((rows, 128), bf16)
        for k in range(TOPK):
            total = jnp.where(slots[k] == expert, copies[k], total)
        store(c, total)


def block_of(refs, core, position):
    if len(refs) == 2:
        return refs[core].at[position]
    return refs[2 * (position // 4) + core].at[position % 4]


def spots(plane_first):
    out = []
    for j in range(VDP):
        for q in range(VTP):
            position = q * 4 + j // 2 if plane_first else (j // 2) * 4 + q
            out.append((j, q, (j % 2, position)))
    return out


def place(refs, scratch, idx, first, tiles, plane_first=False):
    for j, q, (core, position) in spots(plane_first):
        row = pl.multiple_of(idx[j] * RW, RW)
        for t in range(tiles):
            col = pl.multiple_of(idx[VDP + q] * (tiles * 128) + t * 128, 128)
            start = first + t * RW
            scratch[pl.ds(row, RW), pl.ds(col, 128)] = block_of(refs, core, position)[start : start + RW, :]


def place_misc(refs, scratch, idx, first):
    for j, q, (core, position) in spots(False):
        row = pl.multiple_of((idx[j] * VTP + idx[VDP + q]) * RM, RM)
        for t in range(2):
            start = first + t * RM
            scratch[pl.ds(row, RM), t * 128 : (t + 1) * 128] = block_of(refs, core, position)[start : start + RM, :]


def target_of(targets, j):
    return (targets[0], j) if len(targets) == 1 else (targets[j % 2], j // 2)


def hand_out(targets, grad, idx, first, tiles, at=0):
    for j in range(VDP):
        row = pl.multiple_of(idx[REDUCE + j] * RW, RW)
        target, place_at = target_of(targets, j)
        for t in range(tiles):
            start = first + t * RW
            target[place_at, at, start : start + RW, :] = grad[pl.ds(row, RW), t * 128 : (t + 1) * 128].astype(bf16)


def bias_of(segc, segr_ref, row0, start, width):
    rows = row0 + lax.broadcasted_iota(jnp.int32, (SUB, width), 0)
    cols = start + lax.broadcasted_iota(jnp.int32, (SUB, width), 1)
    same = segc[:, 0:1] == segr_ref[0:1, pl.ds(start, width)]
    return jnp.where((cols <= rows) & same, 0.0, masked_value).astype(f32)


def attn_forward_kernel(idx, x_ref, hc_ref, segc_ref, segr_ref, *rest):
    w_refs, rest = rest[:8], rest[8:]
    (mid_ref, qs_ref, kv_ref, ho_ref, lse_ref, spread_ref, gate_ref, gains_ref) = rest[:8]
    (wq, wo, misc, gain_s, kt_lo, kt_hi, v_lo, v_hi, qst, heads_s) = rest[8:]
    step = pl.program_id(0)

    @pl.when(step == 0)
    def _():
        place(w_refs, wq, idx, AT_Q, TA)
        place(w_refs, wo, idx, 0, TA)
        place_misc(w_refs, misc, idx, AT_MISC)
        turned = misc[:, 128:256].astype(f32).T
        gain_s[...] = jnp.zeros_like(gain_s)
        gain_s[0:1, :] = turned[24:25] + turned[25:26] + turned[26:27]
        gain_s[1:2, :] = turned[27:28] + turned[28:29] + turned[29:30]
        gains_ref[...] = gain_s[...]

    x = x_ref[...].astype(f32)
    normed, _ = normalize(x)
    act = (normed * gain_s[0:1, :]).astype(bf16)
    hc = hc_ref[...]
    slots = slot_columns(hc)
    low_half = lanes(AROWS) < 64
    lane = lanes(AROWS)
    small = dot(act, misc[:, 0:256])
    kv = small[:, 0:128].astype(bf16)
    logits = jnp.where(lane < E, small[:, 128:256], masked_value)
    top = jnp.max(logits, -1, keepdims=True)
    lane_f = lane.astype(f32)
    hit = [hc[:, k : k + 1] == lane_f for k in range(TOPK)]
    chosen = hit[0]
    for k in range(1, TOPK):
        chosen = chosen | hit[k]
    powers = jnp.where(chosen, jnp.exp(logits - top), 0.0)
    gate = powers / jnp.sum(powers, -1, keepdims=True)
    gate_ref[...] = gate
    gate_low = gate.astype(bf16).astype(f32)
    gates = [jnp.sum(jnp.where(hit[k], gate_low, 0.0), -1, keepdims=True) for k in range(TOPK)]
    kv_ref[...] = kv
    row = pl.multiple_of(step * AROWS, AROWS)
    kv_f = kv.astype(f32)
    k_lo = jnp.where(low_half, kv_f, 0.0)
    k_hi = pltpu.roll(k_lo, 64, 1)
    val_hi = jnp.where(low_half, 0.0, kv_f)
    val_lo = pltpu.roll(val_hi, 64, 1)
    kt_lo[:, pl.ds(row, AROWS)] = k_lo.T.astype(bf16)
    kt_hi[:, pl.ds(row, AROWS)] = k_hi.T.astype(bf16)
    ones = jnp.where(low_half, 1.0, 0.0)
    v_lo[pl.ds(row, AROWS), 0:128] = val_lo.astype(bf16)
    v_lo[pl.ds(row, AROWS), 128:256] = ones.astype(bf16)
    v_hi[pl.ds(row, AROWS), 0:128] = val_hi.astype(bf16)
    v_hi[pl.ds(row, AROWS), 128:256] = (1.0 - ones).astype(bf16)
    queries = dot(act, wq[...])
    picked = pick_heads(queries, slots)
    for p in range(PAIRS):
        scaled = picked[p] * jnp.asarray(H ** (-0.5), bf16)
        qs_ref[:, p * 128 : (p + 1) * 128] = scaled
        for s in range(AROWS // SUB):
            qst[s, p * SUB : (p + 1) * SUB, :] = scaled[s * SUB : (s + 1) * SUB]

    def sub_block(s, carry):
        block = step * (AROWS // SUB) + s
        count = idx[BLOCKS + block]
        rows = pl.ds(pl.multiple_of(s * SUB, SUB), SUB)

        def attend(n):
            width = n * SUB
            start = pl.multiple_of((block + 1 - n) * SUB, SUB)
            bias = bias_of(segc_ref[rows, :], segr_ref, block * SUB, start, width)
            q4 = qst[s]
            parts = []
            tops = []
            for kt in (kt_lo, kt_hi):
                scores = dot(q4, kt[:, pl.ds(start, width)]).reshape(PAIRS, SUB, width) + bias[None]
                peak = jnp.max(scores, -1, keepdims=True)
                parts.append(jnp.exp(scores - peak).astype(bf16).reshape(PAIRS * SUB, width))
                tops.append(peak.reshape(PAIRS * SUB, 1))
            result = dot(parts[0], v_lo[pl.ds(start, width), :]) + dot(parts[1], v_hi[pl.ds(start, width), :])
            total = result[:, 128:256]
            heads = result[:, 0:128] / total
            log_sum = jnp.where(lanes(PAIRS * SUB) < 64, tops[0], tops[1]) + jnp.log(total)
            keep = jnp.zeros((SUB, 128), f32)
            for p in range(PAIRS):
                one = slice(p * SUB, (p + 1) * SUB)
                heads_s[rows, p * 128 : (p + 1) * 128] = heads[one]
                keep = jnp.where((lanes(SUB) & 63) == p, log_sum[one], keep)
            lse_ref[rows, :] = keep

        for n in range(1, 6):
            pl.when(count == n)(functools.partial(attend, n))
        return carry

    lax.fori_loop(0, AROWS // SUB, sub_block, 0)
    mixed = []
    for p in range(PAIRS):
        gate_pair = jnp.where(low_half, gates[2 * p], gates[2 * p + 1])
        mixed.append(gate_pair * heads_s[:, p * 128 : (p + 1) * 128])
    ho_ref[...] = heads_s[...].astype(bf16)

    def store(c, value):
        spread_ref[:, c * 128 : (c + 1) * 128] = value

    spread_heads(mixed, slots, store)
    mid_ref[...] = x + dot_nt(spread_ref[...], wo[...])


def ffn_forward_kernel(plane_first, idx, x_ref, gains_ref, *rest):
    count = 2 if plane_first else 8
    w_refs, rest = rest[:count], rest[count:]
    out_ref = rest[0]
    wu, wd = rest[1:]

    @pl.when(pl.program_id(0) == 0)
    def _():
        place(w_refs, wu, idx, 0, TF, plane_first)
        place(w_refs, wd, idx, TF * RW, TF, plane_first)

    x = x_ref[...]
    normed, _ = normalize(x)
    act = (normed * gains_ref[1:2, :]).astype(bf16)
    pre = dot(act, wu[...])
    hidden = jax.nn.gelu(pre, approximate=True).astype(bf16)
    out_ref[...] = (x + dot_nt(hidden, wd[...])).astype(out_ref.dtype)


def ffn_backward_kernel(plane_first, idx, up_ref, x_ref, gains_ref, *rest):
    count = 2 if plane_first else 8
    w_refs, rest = rest[:count], rest[count:]
    mid_ref, gain_ref = rest[:2]
    targets = rest[2:-7]
    wu, wd, hid_s, gp_s, grad_t, act_t, part = rest[-7:]
    step = pl.program_id(0)

    @pl.when(step == 0)
    def _():
        place(w_refs, wu, idx, 0, TF, plane_first)
        place(w_refs, wd, idx, TF * RW, TF, plane_first)
        gain_ref[...] = jnp.zeros_like(gain_ref)

    @pl.when(step < STEPS)
    def _():
        row = pl.multiple_of(step * ROWS, ROWS)
        up = up_ref[...].astype(f32)
        gain = gains_ref[1:2, :]
        normed, factor = normalize(x_ref[...])
        act_f = normed * gain
        act = act_f.astype(bf16)
        act_t[:, pl.ds(row, ROWS)] = act_f.T.astype(bf16)
        grad_t[:, pl.ds(row, ROWS)] = up.T.astype(bf16)
        pre = dot(act, wu[...])
        square = pre * pre
        bend = jnp.tanh(0.7978845608028654 * pre * (1.0 + 0.044715 * square))
        half = 0.5 * (1.0 + bend)
        hid_s[pl.ds(row, ROWS), :] = (pre * half).astype(bf16)
        slope = half + (0.5 * 0.7978845608028654) * pre * (1.0 - bend * bend) * (1.0 + 3.0 * 0.044715 * square)
        grad_pre = (dot(up.astype(bf16), wd[...]) * slope).astype(bf16)
        gp_s[pl.ds(row, ROWS), :] = grad_pre
        grad_act = dot_nt(grad_pre, wu[...])
        scaled = grad_act * gain
        inner = jnp.mean(scaled * normed, -1, keepdims=True)
        mid_ref[...] = up + factor * (scaled - normed * inner)
        gain_ref[0:1, :] += jnp.sum(grad_act * normed, 0, keepdims=True)

    @pl.when(step >= STEPS)
    def _():
        q = step - STEPS
        col = pl.multiple_of(idx[REDUCE + VDP + q] * CF, CF)
        part[...] = dot(act_t[...], gp_s[:, pl.ds(col, CF)])
        hand_out(targets, part, idx, 0, TF)
        part[...] = dot(grad_t[...], hid_s[:, pl.ds(col, CF)])
        hand_out(targets, part, idx, TF * RW, TF)


def output_backward_kernel(idx, mid_ref, hc_ref, ho_ref, gate_ref, spread_ref, *rest):
    w_refs, rest = rest[:8], rest[8:]
    gh_ref, dd_ref, gl_ref = rest[:3]
    targets = rest[3:-7]
    wo, grad_t, part, by_expert, by_expert_t, by_slot, spread_s = rest[-7:]
    step = pl.program_id(0)

    @pl.when(step == 0)
    def _():
        place(w_refs, wo, idx, 0, TA)
        made = lax.broadcasted_iota(jnp.int32, (EH, 128), 0) // H
        wide = (made == lax.broadcasted_iota(jnp.int32, (EH, 128), 1)).astype(f32)
        by_expert[...] = wide.astype(bf16)
        by_expert_t[...] = wide.T.astype(bf16)
        row = lax.broadcasted_iota(jnp.int32, (KH, 128), 0)
        slot = row // 128 + (row & 64)
        by_slot[...] = (slot == lax.broadcasted_iota(jnp.int32, (KH, 128), 1)).astype(bf16)

    @pl.when(step < STEPS)
    def _():
        row = pl.multiple_of(step * ROWS, ROWS)
        mid = mid_ref[...]
        grad_t[:, pl.ds(row, ROWS)] = mid.T.astype(bf16)
        full = dot(mid.astype(bf16), wo[...])
        gate = gate_ref[...]
        grads = pick_heads(dot(gate.astype(bf16), by_expert_t[...]) * full, slot_columns(hc_ref[...]))
        inner = jnp.zeros((ROWS, 128), f32)
        for p in range(PAIRS):
            cut = slice(p * 128, (p + 1) * 128)
            gh_ref[:, cut] = grads[p]
            product = grads[p].astype(f32) * ho_ref[:, cut].astype(f32)
            high = product.astype(bf16)
            low = (product - high.astype(f32)).astype(bf16)
            inner += dot(high, by_slot[cut, :]) + dot(low, by_slot[cut, :])
        dd_ref[...] = inner
        spread = spread_ref[...]
        spread_s[pl.ds(row, ROWS), :] = spread
        weighted = dot((full * spread.astype(f32)).astype(bf16), by_expert[...])
        total = jnp.sum(weighted, -1, keepdims=True)
        gl_ref[...] = (weighted - gate * total).astype(bf16)

    @pl.when(step >= STEPS)
    def _():
        for q in range(VTP):
            col = pl.multiple_of(idx[REDUCE + VDP + q] * CA, 128)
            part[q] = dot(grad_t[...], spread_s[:, pl.ds(col, CA)])
            hand_out(targets, part.at[q], idx, 0, TA, q)


def attn_backward_kernel(
    idx, mid_ref, x_ref, hc_ref, segc_ref, segr_ref, qs_ref, gh_ref, kv_ref, lse_ref, dd_ref, gl_ref, gains_ref, gfg_ref, *rest
):
    w_refs, misc_refs, rest = rest[:8], rest[8:16], rest[16:]
    out_ref = rest[0]
    targets, rest = rest[1:-18], rest[-18:]
    (wq, misc, kt_lo, kt_hi, vt_lo, vt_hi, k_lo, k_hi, dkv_t, qst, gst, dq_s, gq_s, act_t) = rest[:14]
    (dkv_s, gain_s, part, pmisc) = rest[14:]
    step = pl.program_id(0)

    @pl.when(step == 0)
    def _():
        place(w_refs, wq, idx, 0, TA)
        place_misc(misc_refs, misc, idx, 0)
        low = lanes(LEN) < 64
        kv = kv_ref[...].astype(f32)
        one = jnp.where(low, kv, 0.0)
        two = pltpu.roll(one, 64, 1)
        k_lo[...] = one.astype(bf16)
        k_hi[...] = two.astype(bf16)
        kt_lo[...] = one.T.astype(bf16)
        kt_hi[...] = two.T.astype(bf16)
        one = jnp.where(low, 0.0, kv)
        vt_hi[...] = one.T.astype(bf16)
        vt_lo[...] = pltpu.roll(one, 64, 1).T.astype(bf16)
        dkv_t[...] = jnp.zeros_like(dkv_t)
        gain_s[...] = jnp.zeros_like(gain_s)

    @pl.when(step < STEPS)
    def _():
        row = pl.multiple_of(step * ROWS, ROWS)
        for p in range(PAIRS):
            for s in range(ROWS // SUB):
                qst[s, p * SUB : (p + 1) * SUB, :] = qs_ref[s * SUB : (s + 1) * SUB, p * 128 : (p + 1) * 128]
                gst[s, p * SUB : (p + 1) * SUB, :] = gh_ref[s * SUB : (s + 1) * SUB, p * 128 : (p + 1) * 128]

        def sub_block(s, carry):
            block = step * (ROWS // SUB) + s
            count = idx[BLOCKS + block]
            rows = pl.ds(pl.multiple_of(s * SUB, SUB), SUB)

            def attend(n):
                width = n * SUB
                start = pl.multiple_of((block + 1 - n) * SUB, SUB)
                win = pl.ds(start, width)
                bias = bias_of(segc_ref[rows, :], segr_ref, block * SUB, start, width)
                q4 = qst[s]
                g4 = gst[s]
                q4t = q4.astype(f32).T.astype(bf16)
                g4t = g4.astype(f32).T.astype(bf16)
                lse = lse_ref[rows, :]
                dd = dd_ref[rows, :]
                dq = None
                dk = None
                dv = None
                for half, (kt, vt, kk) in enumerate(((kt_lo, vt_lo, k_lo), (kt_hi, vt_hi, k_hi))):
                    off = 64 * half
                    log_sum = jnp.stack([lse[:, off + p : off + p + 1] for p in range(PAIRS)])
                    inner = jnp.stack([dd[:, off + p : off + p + 1] for p in range(PAIRS)])
                    scores = dot(q4, kt[:, win]).reshape(PAIRS, SUB, width)
                    prob = jnp.exp(scores + bias[None] - log_sum)
                    dprob = dot(g4, vt[:, win]).reshape(PAIRS, SUB, width)
                    dscore = (prob * (dprob - inner)).astype(bf16).reshape(PAIRS * SUB, width)
                    low_prob = prob.astype(bf16).reshape(PAIRS * SUB, width)
                    a = dot(dscore, kk[win, :])
                    b = dot(q4t[off : off + 64], dscore)
                    c = dot(g4t[off : off + 64], low_prob)
                    dq = a if dq is None else dq + a
                    dk = b if dk is None else dk + b
                    dv = c if dv is None else dv + c
                dkv_t[0:64, win] += dk
                dkv_t[64:128, win] += dv
                dq = dq * (H ** (-0.5))
                for p in range(PAIRS):
                    dq_s[rows, p * 128 : (p + 1) * 128] = dq[p * SUB : (p + 1) * SUB]

            for n in range(1, 6):
                pl.when(count == n)(functools.partial(attend, n))
            return carry

        lax.fori_loop(0, ROWS // SUB, sub_block, 0)
        slots = slot_columns(hc_ref[...])

        def store(c, value):
            gq_s[pl.ds(row, ROWS), c * 128 : (c + 1) * 128] = value

        spread_heads([dq_s[:, p * 128 : (p + 1) * 128] for p in range(PAIRS)], slots, store)

    @pl.when(step == STEPS)
    def _():
        dkv_s[...] = dkv_t[...].T.astype(bf16)

    @pl.when((step >= STEPS) & (step < 2 * STEPS))
    def _():
        row = pl.multiple_of((step - STEPS) * ROWS, ROWS)
        here = pl.ds(row, ROWS)
        gain = gains_ref[0:1, :]
        normed, factor = normalize(x_ref[...].astype(f32))
        act_t[:, here] = (normed * gain).T.astype(bf16)
        grad_act = dot_nt(gq_s[here, :], wq[...])
        grad_act += dot_nt(dkv_s[here, :], misc[:, 0:128])
        router = jnp.where(lanes(D) < E, misc[:, 128:256].astype(f32), 0.0).astype(bf16)
        grad_act += dot_nt(gl_ref[here, :], router)
        scaled = grad_act * gain
        inner = jnp.mean(scaled * normed, -1, keepdims=True)
        out_ref[...] = mid_ref[...] + factor * (scaled - normed * inner)
        gain_s[0:1, :] += jnp.sum(grad_act * normed, 0, keepdims=True)

    @pl.when(step == 2 * STEPS)
    def _():
        pmisc[:, 0:128] = dot(act_t[...], dkv_s[...])
        router = dot(act_t[...], gl_ref[...])
        gain_s[1:2, :] = gfg_ref[0:1, :]
        turned = gain_s[...].T
        lane = lanes(D)
        router = jnp.where(lane < E, router, 0.0)
        router = jnp.where(lane == E, turned[:, 0:1], router)
        router = jnp.where(lane == E + 1, turned[:, 1:2], router)
        pmisc[:, 128:256] = router

    @pl.when(step >= 2 * STEPS)
    def _():
        for q in range(VTP):
            col = pl.multiple_of(idx[REDUCE + VDP + q] * CA, 128)
            part[q] = dot(act_t[...], gq_s[:, pl.ds(col, CA)])
            hand_out(targets, part.at[q], idx, 0, TA, q)
            for j in range(VDP):
                row = pl.multiple_of((idx[REDUCE + j] * VTP + idx[REDUCE + VDP + q]) * RM, RM)
                target, place_at = target_of(targets, j)
                for t in range(2):
                    start = TA * RW + t * RM
                    target[place_at, q, start : start + RM, :] = pmisc[
                        pl.ds(row, RM), t * 128 : (t + 1) * 128
                    ].astype(bf16)


def pack_attn(out, base, query, output, keyval, router, columns, layer):
    for t in range(TA):
        cut = slice(t * 128, (t + 1) * 128)
        out[base + t * RW : base + (t + 1) * RW, :] = output[layer, :, cut].astype(bf16)
        start = base + AT_Q + t * RW
        out[start : start + RW, :] = query[layer, :, cut].astype(bf16)
    start = base + AT_MISC
    out[start : start + RM, :] = keyval[layer].astype(bf16)
    misc = slice(start + RM, start + 2 * RM)
    lane = lanes(RM)
    block = jnp.zeros((RM, 128), f32)
    gains = columns[layer]
    for which in range(2):
        part = gains[:, which : which + 1]
        for i in range(3):
            high = part.astype(bf16).astype(f32)
            block = jnp.where(lane == E + 3 * which + i, high, block)
            part = part - high
    out[misc, :] = block.astype(bf16)
    out[misc, 0:E] = router[layer].astype(bf16)


def pack_ffn(out, base, up, down, layer):
    for t in range(TF):
        cut = slice(t * 128, (t + 1) * 128)
        out[base + t * RW : base + (t + 1) * RW, :] = up[layer, :, cut].astype(bf16)
        start = base + (TF + t) * RW
        out[start : start + RW, :] = down[layer, :, cut].astype(bf16)


def pack_first_kernel(query, output, keyval, router, columns, out):
    pack_attn(out, 0, query, output, keyval, router, columns, 0)


def pack_other_kernel(query, output, keyval, router, columns, up, down, rest, last):
    pack_ffn(rest, 0, up, down, 0)
    pack_attn(rest, RF, query, output, keyval, router, columns, 1)
    rest[RF + RA :, :] = jnp.zeros((REST - RF - RA, 128), bf16)
    pack_ffn(last, 0, up, down, 1)


def sum_kernel(scale, parts, total, square):
    value = parts[0].astype(f32)
    for k in range(1, parts.shape[0]):
        value = value + parts[k].astype(f32)
    value = value * scale
    total[...] = value
    rows = value.shape[0]
    square[...] = jnp.sum((value * value).reshape(rows // 8, 8, 128), 0)


def update_kernel(square, query0, rest, last, *refs):
    state, norm_ref, outs = refs[:28], refs[28], refs[29:]
    norm = jnp.sqrt(jnp.sum(jnp.sum(square[...], 0, keepdims=True), 1, keepdims=True))
    norm_ref[...] = norm
    factor = jnp.minimum(1.0, clip_bound / norm)

    def step(i, at, grad):
        result = adamw(
            state[i][at], state[7 + i][at], state[14 + i][at], state[21 + i][at], grad, factor, learn_rates[i]
        )
        for k in range(4):
            outs[4 * i + k][at] = result[k]

    def tile(i, layer, t, ref, start):
        step(i, (layer, slice(None), slice(t * 128, (t + 1) * 128)), ref[start : start + RW, :])

    for t in range(TA):
        tile(0, 0, t, query0, t * RW)
        tile(0, 1, t, last, t * RW)
        tile(1, 0, t, query0, RQ + t * RW)
        tile(1, 1, t, last, RQ + t * RW)
    for t in range(TF):
        tile(2, 0, t, rest, t * RW)
        tile(3, 0, t, rest, (TF + t) * RW)
        tile(2, 1, t, last, RA + t * RW)
        tile(3, 1, t, last, RA + (TF + t) * RW)
    for layer, ref in ((0, query0), (1, last)):
        start = TA * RW
        step(4, (layer,), ref[start : start + RM, :])
        block = ref[start + RM : start + 2 * RM, :]
        step(5, (layer,), block[:, 0:E])
        step(6, (layer,), block.T[E : E + 2, :])


def add_kernel(pieces, *refs):
    step = pl.program_id(0)
    outs = refs[2 * pieces :]
    first = 0
    for piece in range(pieces):
        one, two = refs[2 * piece], refs[2 * piece + 1]
        rows = one.shape[2]
        for k in range(4):
            outs[k][0, first : first + rows, :] = (one[k, 0].astype(f32) + two[k, 0].astype(f32)).astype(bf16)
        first += rows


def add_pairs(pairs):
    rows = sum(keep.shape[2] for keep, _ in pairs)
    flat = [x for pair in pairs for x in pair]
    return pl.pallas_call(
        functools.partial(add_kernel, len(pairs)),
        grid=(VTP,),
        in_specs=[pl.BlockSpec((4, 1) + x.shape[2:], lambda i: (0, i, 0, 0)) for x in flat],
        out_specs=[pl.BlockSpec((1, rows, 128), lambda i: (i, 0, 0))] * 4,
        out_shape=[jax.ShapeDtypeStruct((VTP, rows, 128), bf16)] * 4,
        compiler_params=pltpu.CompilerParams(dimension_semantics=("arbitrary",), vmem_limit_bytes=24 * 1024 * 1024),
        name="add_pairs",
    )(*[in_hbm(x) for x in flat])


def whole_call(kernel, out_shapes, name, *args):
    return pl.pallas_call(
        kernel,
        in_specs=[pl.BlockSpec(memory_space=pltpu.VMEM)] * len(args),
        out_specs=[pl.BlockSpec(memory_space=pltpu.VMEM)] * len(out_shapes),
        out_shape=[jax.ShapeDtypeStruct(shape, kind) for shape, kind in out_shapes],
        compiler_params=pltpu.CompilerParams(vmem_limit_bytes=VMEM),
        name=name,
    )(*args)


def sum_parts(parts, scale):
    rows = parts.shape[1]
    return whole_call(
        functools.partial(sum_kernel, scale), [((rows, 128), f32), ((8, 128), f32)], "sum_parts", parts
    )


def rows_spec(width, phase=0, rows=ROWS):
    steps = LEN // rows

    def index(i, idx):
        return (jnp.clip(i - phase * steps, 0, steps - 1), 0)

    return pl.BlockSpec((rows, width), index)


def full_spec(shape):
    zeros = (0,) * len(shape)
    return pl.BlockSpec(shape, lambda i, idx: zeros, pipeline_mode=pl.Buffered(1))


def kept_spec(shape):
    zeros = (0,) * len(shape)
    return pl.BlockSpec(shape, lambda i, idx: zeros)


def part_specs(rows, at, count):
    return [
        pl.BlockSpec((32 // count, rows, 128), lambda i, idx: (0, at, 0), pipeline_mode=pl.Buffered(1))
    ] * count


def stacks(arrays, rows):
    return [in_hbm(x.reshape(-1, rows, 128)) for x in arrays]


def parts_specs(rows, phase, split):
    def index(i, idx):
        return (0, jnp.maximum(i - phase * STEPS, 0), 0, 0)

    count = VDP // 2 if split else VDP
    if phase is None:
        return [kept_spec((count, VTP, rows, 128))] * (VDP // count)
    return [pl.BlockSpec((count, 1, rows, 128), index)] * (VDP // count)


def parts_shapes(rows, split):
    count = VDP // 2 if split else VDP
    return [((count, VTP, rows, 128), bf16, 1)] * (VDP // count)


def call(kernel, steps, in_specs, out_specs, out_shapes, scratch, name, flops, moved, vmem):
    return pl.pallas_call(
        kernel,
        grid_spec=pltpu.PrefetchScalarGridSpec(
            num_scalar_prefetch=1,
            grid=(steps,),
            in_specs=in_specs,
            out_specs=out_specs,
            scratch_shapes=scratch,
        ),
        out_shape=[jax.ShapeDtypeStruct(s[0], s[1]) if len(s) == 2 else pltpu.HBM(s[0], s[1]) for s in out_shapes],
        compiler_params=pltpu.CompilerParams(
            dimension_semantics=("arbitrary",), vmem_limit_bytes=vmem * 1024 * 1024
        ),
        cost_estimate=pl.CostEstimate(flops=flops, bytes_accessed=moved, transcendentals=0),
        name=name,
    )


def in_hbm(x):
    return pltpu.with_memory_space_constraint(x, pltpu.HBM)


def vm(*shape, dtype=bf16):
    return pltpu.VMEM(shape, dtype)


def attn_forward(idx, x, hc, segc, segr, weights, far):
    pin = (1,) if far else ()
    return call(
        attn_forward_kernel,
        LEN // AROWS,
        [rows_spec(D, 0, AROWS), rows_spec(TOPK, 0, AROWS), rows_spec(128, 0, AROWS), full_spec((8, LEN))]
        + part_specs(RA, 0, 8),
        [
            rows_spec(D, 0, AROWS), rows_spec(KH, 0, AROWS), rows_spec(128, 0, AROWS), rows_spec(KH, 0, AROWS), rows_spec(128, 0, AROWS),
            rows_spec(EH, 0, AROWS), rows_spec(128, 0, AROWS), kept_spec((8, D)),
        ],
        [
            ((LEN, D), f32, 1), ((LEN, KH), bf16) + pin, ((LEN, 128), bf16) + pin, ((LEN, KH), bf16) + pin,
            ((LEN, 128), f32) + pin, ((LEN, EH), bf16) + pin, ((LEN, 128), f32) + pin, ((8, D), f32),
        ],
        [
            vm(D, EH), vm(D, EH), vm(D, 256), vm(8, D, dtype=f32), vm(128, LEN), vm(128, LEN),
            vm(LEN, 256), vm(LEN, 256), vm(AROWS // SUB, PAIRS * SUB, 128), vm(AROWS, KH, dtype=f32),
        ],
        "attn_forward", 8 * 10**9, 14 * 10**6, 26,
    )(idx, in_hbm(x), hc, segc, segr, *stacks(weights, RA))


def ffn_forward(idx, x, gains, weights, last, plane_first):
    return call(
        functools.partial(ffn_forward_kernel, plane_first),
        STEPS,
        [rows_spec(D), full_spec((8, D))] + part_specs(RF, 0, 2 if plane_first else 8),
        [rows_spec(D)],
        [((LEN, D), bf16 if last else f32, 1)],
        [vm(D, FF), vm(D, FF)],
        "ffn_forward", 5 * 10**9, 8 * 10**6, 28,
    )(idx, in_hbm(x), gains, *stacks(weights, RF))[0]


def ffn_backward(idx, upstream, x, gains, weights, plane_first, split):
    return call(
        functools.partial(ffn_backward_kernel, plane_first),
        STEPS + VTP,
        [rows_spec(D), rows_spec(D), full_spec((8, D))] + part_specs(RF, 0, 2 if plane_first else 8),
        [rows_spec(D), kept_spec((8, D))] + parts_specs(RF, 1, split),
        [
            ((LEN, D), f32, 1), ((8, D), f32),
        ]
        + parts_shapes(RF, split),
        [
            vm(D, FF), vm(D, FF), vm(LEN, FF), vm(LEN, FF), vm(D, LEN), vm(D, LEN), vm(D, CF, dtype=f32),
        ],
        "ffn_backward", 13 * 10**9, 14 * 10**6, 56,
    )(idx, in_hbm(upstream), in_hbm(x), gains, *stacks(weights, RF))


def output_backward(idx, mid, hc, heads, gate, spread, weights, split):
    return call(
        output_backward_kernel,
        STEPS + 1,
        [rows_spec(D), rows_spec(TOPK), rows_spec(KH), rows_spec(128), rows_spec(EH)]
        + part_specs(TA * RW, 0, 8),
        [rows_spec(KH), rows_spec(128), rows_spec(128)] + parts_specs(TA * RW, None, split),
        [
            ((LEN, KH), bf16), ((LEN, 128), f32), ((LEN, 128), bf16),
        ]
        + parts_shapes(TA * RW, split),
        [
            vm(D, EH), vm(D, LEN), vm(VTP, D, CA, dtype=f32), vm(EH, 128), vm(128, EH), vm(KH, 128), vm(LEN, EH),
        ],
        "output_backward", 5 * 10**9, 16 * 10**6, 30,
    )(idx, in_hbm(mid), hc, in_hbm(heads), in_hbm(gate), in_hbm(spread), *stacks(weights, RA))


def attn_backward(idx, mid, x, hc, segc, segr, qs, gh, kv, lse, dd, gl, gains, gfg, weights, split):
    return call(
        attn_backward_kernel,
        2 * STEPS + 1,
        [
            rows_spec(D, 1), rows_spec(D, 1), rows_spec(TOPK), rows_spec(128), full_spec((8, LEN)),
            rows_spec(KH), rows_spec(KH), full_spec((LEN, 128)), rows_spec(128), rows_spec(128),
            full_spec((LEN, 128)), full_spec((8, D)), full_spec((8, D)),
        ]
        + part_specs(TA * RW, 1, 8)
        + part_specs(2 * RM, AT_MISC // (2 * RM), 8),
        [rows_spec(D, 1)] + parts_specs(RQ, None, split),
        [((LEN, D), f32, 1)] + parts_shapes(RQ, split),
        [
            vm(D, EH), vm(D, 256), vm(128, LEN), vm(128, LEN), vm(128, LEN), vm(128, LEN),
            vm(LEN, 128), vm(LEN, 128), vm(128, LEN, dtype=f32), vm(ROWS // SUB, PAIRS * SUB, 128),
            vm(ROWS // SUB, PAIRS * SUB, 128), vm(ROWS, KH, dtype=f32), vm(LEN, EH), vm(D, LEN),
            vm(LEN, 128), vm(8, D, dtype=f32), vm(VTP, D, CA, dtype=f32), vm(D, 256, dtype=f32),
        ],
        "attn_backward", 10 * 10**9, 16 * 10**6, 38,
    )(idx, in_hbm(mid), in_hbm(x), hc, segc, segr, in_hbm(qs), gh, kv, in_hbm(lse), dd, gl, gains, gfg, *stacks(weights, RA), *stacks(weights, RA))


def swap(k):
    return [(i, i ^ k) for i in range(VDP)]


def plane_moves(block):
    return [block] + [lax.ppermute(block, "dp", swap(2 * k)) for k in range(1, 4)]


def core_moves(blocks):
    return [x for block in blocks for x in (block, lax.ppermute(block, "dp", swap(1)))]


def stacked(blocks):
    return jnp.concatenate(blocks, 0)


def tiled(block):
    return jnp.concatenate([block[:, t : t + 128] for t in range(0, block.shape[1], 128)], 0)


def after(value, *others):
    flat, tree = jax.tree.flatten((value, others))
    return jax.tree.unflatten(tree, lax.optimization_barrier(flat))[0]


def reduce_core(keep, send):
    return keep, lax.ppermute(send, "dp", swap(1))


def reduce_plane(pair):
    return list(pair[:1]) + [lax.ppermute(pair[k], "dp", swap(2 * k)) for k in range(1, 4)]


def plane_sum(parts):
    total = parts[0].astype(f32)
    for part in parts[1:]:
        total = total + part.astype(f32)
    return total.astype(bf16)


def line_swap(parts):
    return lax.all_to_all(parts, "tp", 0, 0)


def block_piece(block, plane_first):
    order = sorted(spots(plane_first), key=lambda entry: entry[2])
    made = [block(j, q) for j, q, _ in order]
    if plane_first:
        return [jnp.concatenate(made[:16], 0), jnp.concatenate(made[16:], 0)]
    return [jnp.concatenate(made[16 * c + 4 * k : 16 * c + 4 * k + 4], 0) for k in range(4) for c in range(2)]


def unblock_matrix(both, rows):
    tiles = both.shape[2] // rows
    return both.reshape(VDP, VTP, tiles, rows, 128).transpose(0, 3, 1, 2, 4).reshape(D, VTP * tiles * 128)


def split_gain(gain):
    high = lax.reduce_precision(gain, 8, 7)
    rest = gain - high
    middle = lax.reduce_precision(rest, 8, 7)
    return [high, middle, rest - middle]


def global_sum(value):
    for k in (1, 2, 4):
        value = value + lax.ppermute(value, "dp", swap(k))
    for k in (1, 2):
        value = value + lax.ppermute(value, "tp", [(i, i ^ k) for i in range(VTP)])
    return value


def adamw(weight, moment_one, moment_two, average, grad_full, factor, learn_rate):
    clipped = grad_full * factor
    first_new = beta_one * moment_one + (1.0 - beta_one) * clipped
    second_new = beta_two * moment_two + (1.0 - beta_two) * clipped * clipped
    step_ratio = (
        first_new
        / (1.0 - beta_one**STEP)
        / (jnp.sqrt(second_new / (1.0 - beta_two**STEP)) + adam_floor)
    )
    weight_new = weight - learn_rate * (step_ratio + weight_decay * weight)
    return (weight_new, first_new, second_new, ema_decay * average + (1.0 - ema_decay) * weight_new)


def local(tokens, cotangent, head_choice, segment_ids, *state):
    weights, firsts, seconds, averages = state[0:7], state[7:14], state[14:21], state[21:28]
    query_w, output_w, up_w, down_w, keyval_w, router_w, gains_w = weights
    size_dp = lax.axis_size("dp")
    size_tp = lax.axis_size("tp")
    token_total = tokens.shape[0] * size_dp * size_tp
    native = (size_dp, size_tp) == (VDP, VTP)
    scale = 1.0 / token_total

    steady = jnp.arange(VDP + VTP, dtype=jnp.int32)
    steady = jnp.where(steady < VDP, steady, steady - VDP)
    if native:
        own = jnp.arange(VDP, dtype=jnp.int32) ^ lax.axis_index("dp").astype(jnp.int32)
        gathers = jnp.concatenate([own, steady[VDP:]])
        reduces = [gathers, steady]
    else:
        gathers = steady
        reduces = [steady, steady]
    segment = segment_ids.reshape(LEN)
    heads_at = segment[:: SUB]
    first_at = jnp.sum((segment[None, :] < heads_at[:, None]).astype(jnp.int32), 1)
    blocks = jnp.arange(LEN // SUB, dtype=jnp.int32) - first_at // SUB + 1
    tables = [jnp.concatenate([gathers, r, blocks]) for r in reduces]
    segc = jnp.broadcast_to(segment.astype(f32)[:, None], (LEN, 128))
    segr = jnp.broadcast_to(segment.astype(f32)[None, :], (8, LEN))
    hc = head_choice.astype(f32)

    def split(l):
        return native and l == 0

    def run_attn_forward(l, x, a):
        saved[l] = (x,) + tuple(attn_forward(tables[l], x, hc, segc, segr, a, True))

    def run_ffn_forward(l, f):
        return ffn_forward(tables[l], saved[l][1], saved[l][8], f, l == LAYERS - 1, l == LAYERS - 1)

    def run_ffn_backward(l, upstream, f):
        return ffn_backward(
            tables[l], upstream, saved[l][1], saved[l][8], f, l == LAYERS - 1, split(l)
        )

    def run_output_backward(l, mid_grad, a):
        _, _, _, _, heads, _, spread, gate, _ = saved[l]
        return output_backward(tables[l], mid_grad, hc, heads, gate, spread, a, split(l))

    def run_attn_backward(l, mid_grad, gh, dd, gl, gain_ffn_grad, a):
        x, _, qs, kv, _, lse, _, _, gains = saved[l]
        return attn_backward(
            tables[l], mid_grad, x, hc, segc, segr, qs, gh, kv, lse, dd, gl, gains, gain_ffn_grad, a, split(l)
        )

    saved = [None] * LAYERS
    if native:
        columns = gains_w.transpose(0, 2, 1)
        small = (query_w, output_w, keyval_w, router_w, columns)
        (first,) = whole_call(pack_first_kernel, [((RA, 128), bf16)], "pack_first", *small)
        a0 = lax.all_gather(first, "tp", tiled=True)
        rest, f1 = whole_call(
            pack_other_kernel, [((REST, 128), bf16), ((RF, 128), bf16)], "pack_other",
            *small, up_w, after(down_w, first),
        )
        rest, f1 = after((rest, f1), a0)
        a0 = plane_moves(a0)
        rest = lax.all_gather(rest, "tp")
        a0, f1 = after((a0, f1), a0)
        a0 = core_moves(a0)
        f1 = plane_moves(f1)
        rest, f1 = after((rest, f1), rest, f1)
        f0 = plane_moves(rest[:, :RF].reshape(VTP * RF, 128))
        f1 = lax.all_gather(stacked(f1), "tp", tiled=True)
        run_attn_forward(0, after(tokens, rest), a0)
        saved[0], f0, rest = after((saved[0], f0, rest), saved[0][1], f0)
        f0 = core_moves(f0)
        a1 = plane_moves(rest[:, RF : RF + RA].reshape(VTP * RA, 128))
        residual = run_ffn_forward(0, f0)
        residual, a1, f1 = after((residual, a1, f1), residual, a1, f1)
        a1 = core_moves(a1)
        f1 = core_moves([f1])
        run_attn_forward(1, residual, a1)
        mid_grad, gain_grad, rf1 = run_ffn_backward(1, cotangent, after(f1, saved[1][1]))
        rf1 = lax.psum_scatter(rf1, "dp")
        gh, dd, gl, ro1 = run_output_backward(1, mid_grad, a1)
        upstream, rq1 = run_attn_backward(1, mid_grad, gh, dd, gl, gain_grad, a1)
        ra1 = lax.psum_scatter(jnp.concatenate([rq1, ro1], 2), "dp")
        mid_grad, gain_grad, keep, send = run_ffn_backward(0, upstream, f0)
        rf0 = reduce_core(keep, send)
        mid_grad, rf1 = after((mid_grad, rf1), mid_grad, rf1)
        gh, dd, gl, keep, send = run_output_backward(0, mid_grad, a0)
        ro0 = reduce_core(keep, send)
        gh, rf0, rf1 = after((gh, rf0, rf1), gh, rf0, rf1)
        rfo = add_pairs([rf0])
        gh, rfo = after((gh, rfo), gh, rfo)
        rfo = reduce_plane(rfo)
        upstream, keep, send = run_attn_backward(0, mid_grad, gh, dd, gl, gain_grad, a0)
        rq0 = reduce_core(keep, send)
        ra1, rf1 = after((ra1, rf1), upstream, ra1, rf1)
        r1 = lax.psum_scatter(jnp.concatenate([ra1, rf1], 1), "tp")
        saved[1], rfo, ro0 = after((saved[1], rfo, ro0), upstream, rfo, ro0)
        rest = plane_sum(rfo)
        rq0 = reduce_plane(add_pairs([rq0, ro0]))
        rest = line_swap(rest)
        layer_out = run_ffn_forward(1, f1)
        layer_out, rq0, rest = after((layer_out, rq0, rest), layer_out, rq0)
        r1, square_a = sum_parts(r1[None], scale)
        rest, square_b = sum_parts(rest, scale)
        rq0, square_c = sum_parts(line_swap(plane_sum(rq0)), scale)
        square = global_sum(square_a + square_b + square_c)
        shapes = [((1, 1), f32)] + [(w.shape, f32) for w in weights for _ in range(4)]
        updates = whole_call(update_kernel, shapes, "update", square, rq0, rest, r1, *state)
        return (layer_out, upstream, updates[0][0, 0]) + tuple(updates[1:])
    else:
        gain_parts = split_gain(gains_w)
        low_parts = [w.astype(bf16) for w in weights[:6]]

        def small_block(kv, router, gains):
            block = jnp.concatenate([kv, router] + [g[:, None] for g in gains], 1)
            return jnp.pad(block, ((0, 0), (0, 256 - block.shape[1])))

        def piece_a(query, output, misc):
            return jnp.concatenate([tiled(output), tiled(query), tiled(misc)], 0)

        def piece_f(up, down):
            return jnp.concatenate([tiled(up), tiled(down)], 0)

        big = [
            lax.all_gather(lax.all_gather(w, "dp", axis=1, tiled=True), "tp", axis=2, tiled=True)
            for w in low_parts[:4]
        ]
        small = [lax.all_gather(w, ("dp", "tp"), axis=1, tiled=True) for w in low_parts[4:6]]
        wide = [lax.all_gather(g.astype(bf16), ("dp", "tp"), axis=2, tiled=True) for g in gain_parts]

        def cut(matrix, j, q):
            width = matrix.shape[1] // VTP
            return matrix[j * RW : (j + 1) * RW, q * width : (q + 1) * width]

        pieces = []
        for l in range(LAYERS):
            misc = small_block(small[0][l], small[1][l], [g[l, w] for w in range(2) for g in wide])

            def block_a(j, q, l=l, misc=misc):
                row = (j * VTP + q) * RM
                return piece_a(cut(big[0][l], j, q), cut(big[1][l], j, q), misc[row : row + RM])

            def block_f(j, q, l=l):
                return piece_f(cut(big[2][l], j, q), cut(big[3][l], j, q))

            pieces.append((block_piece(block_a, False), block_piece(block_f, l == LAYERS - 1)))
        residual = tokens
        for l in range(LAYERS):
            run_attn_forward(l, residual, pieces[l][0])
            residual = run_ffn_forward(l, pieces[l][1])
        layer_out = residual
        upstream = cotangent
        whole = [None] * LAYERS
        for l in reversed(range(LAYERS)):
            a, f = pieces[l]
            mid_grad, gain_grad, both_f = run_ffn_backward(l, upstream, f)
            gh, dd, gl, both_o = run_output_backward(l, mid_grad, a)
            upstream, both_q = run_attn_backward(l, mid_grad, gh, dd, gl, gain_grad, a)
            misc = both_q[:, :, TA * RW :].reshape(VDP, VTP, 2, RM, 128).transpose(0, 1, 3, 2, 4).reshape(D, 256)
            whole[l] = (
                unblock_matrix(both_q[:, :, : TA * RW], RW),
                unblock_matrix(both_o, RW),
                unblock_matrix(both_f[:, :, : TF * RW], RW),
                unblock_matrix(both_f[:, :, TF * RW :], RW),
                misc,
            )

    sums = []
    for i in range(4):
        grad = jnp.stack([w[i] for w in whole]).astype(f32)
        grad = lax.psum_scatter(grad, "tp", scatter_dimension=2, tiled=True)
        sums.append(lax.psum_scatter(grad, "dp", scatter_dimension=1, tiled=True))
    misc = jnp.stack([w[4] for w in whole]).astype(f32)
    misc = lax.psum_scatter(misc, ("dp", "tp"), scatter_dimension=1, tiled=True)
    sums += [misc[:, :, :128], misc[:, :, 128 : 128 + E], misc[:, :, 128 + E : 130 + E].transpose(0, 2, 1)]
    sums = [s * scale for s in sums]
    squares = jnp.sum(jnp.stack([jnp.sum(s * s) for s in sums]))
    grad_norm = jnp.sqrt(lax.psum(squares, ("dp", "tp")))
    factor = jnp.minimum(1.0, clip_bound / grad_norm)
    outs = [layer_out, upstream, grad_norm]
    for i in range(7):
        outs += adamw(weights[i], firsts[i], seconds[i], averages[i], sums[i], factor, learn_rates[i])
    return tuple(outs)


def solution(mesh):
    token = P(("dp", "tp"), None)
    big = P(None, "dp", "tp")
    small = P(None, ("dp", "tp"), None)
    gain = P(None, None, ("dp", "tp"))
    group = (big, big, big, big, small, small, gain)
    in_specs = (token,) * 4 + group * 4
    out_specs = (token, token, P()) + tuple(spec for spec in group for _ in range(4))
    return jax.shard_map(local, mesh=mesh, in_specs=in_specs, out_specs=out_specs, check_vma=False)
```
